32 devices in a mesh: dp: 8 (over z, x), tensor: 4 (over y, core).
Axes of the slice: x: 2, y: 2, z: 4, core: 2. Of those that a mesh axis runs over, the one named last changes fastest.
Arguments:
- x_home: bfloat16 [16000, 1120], P('dp', 'tensor'), may hold values from -12 to 12
- cot_home: bfloat16 [16000, 1120], P('dp', 'tensor'), may hold values from -6 to 6
- cell_len: int32 [8, 4], replicated, may hold values from 128 to 500, as said below
- norm1_gain: float32 [1120], P('tensor'), may hold values from 0.1 to 1.9
- norm1_bias: float32 [1120], P('tensor'), may hold values from -3 to 3
- qkv_weight: bfloat16 [1120, 3, 1120], P(None, None, 'tensor'), may hold values from -0.1875 to 0.1875
- out_weight: bfloat16 [1120, 1120], P('tensor'), may hold values from -1 to 1
- norm2_gain: float32 [1120], P('tensor'), may hold values from 0.1 to 1.9
- norm2_bias: float32 [1120], P('tensor'), may hold values from -3 to 3
- up_weight: bfloat16 [1120, 4480], P(None, 'tensor'), may hold values from -0.1875 to 0.1875
- down_weight: bfloat16 [4480, 1120], P('tensor'), may hold values from -0.09375 to 0.09375
Outputs:
- out: bfloat16 [16000, 1120], P('dp', 'tensor')
- x_grad: bfloat16 [16000, 1120], P('dp', 'tensor')
- norm1_gain_grad: float32 [1120], P('tensor')
- norm1_bias_grad: float32 [1120], P('tensor')
- qkv_grad: float32 [1120, 3, 1120], P(None, None, 'tensor')
- out_grad: float32 [1120, 1120], P('tensor')
- norm2_gain_grad: float32 [1120], P('tensor')
- norm2_bias_grad: float32 [1120], P('tensor')
- up_grad: float32 [1120, 4480], P(None, 'tensor')
- down_grad: float32 [4480, 1120], P('tensor')
The draws below stay inside these ranges and needn't reach their ends.
Inputs may be any that keep to these rules, and one draw needn't show every extreme that they name: `cell_len`: every slot holds a cell of 128 or more genes, and some cell has exactly 500. With the masks M = (2, 1, 4, 5) of the four slots, the cells of slot k of homes g XOR M_k, over k, add up to at most 1536 rows for every group g, and to exactly 1536 for some group.
All inputs are finite; a program needn't handle non-finite values.
Results may differ from the reference program's by a relative error of at most 0.013.
The reference program's roundings to bfloat16 on the way count: a program that leaves them out, or rounds other values in their place, can miss the bound.
Values may be sent and summed in bfloat16 or wider, within the bound.
No kernel may reach another device: no remote copies, remote signals or barrier semaphores. Data moves between devices by JAX's collectives and lax.ppermute only.
A program may use at most 256 MiB of HBM per device.

```python
import jax
import jax.numpy as jnp
from jax import lax

D = 1120
H = 20
HD = 56
FF = 4480
MAXLEN = 500
MINLEN = 128
SLOTS = 4
WORK = 1536
HOME = 2000
N_DP = 8


def draw_cell_len(key, part):
    base = jax.random.fold_in(key, 7)
    streams = jax.random.split(base, 7)
    half_way = N_DP // 2
    short_bound = (WORK - MAXLEN) // 3
    slot_masks = jnp.array([2, 1, half_way, half_way + 1], jnp.int32)
    slot_class = jnp.arange(4).astype(jnp.int32)
    homes = jnp.arange(N_DP).astype(jnp.int32)
    home_class = homes % 2 + 2 * (homes // half_way)
    long_first = jax.random.randint(streams[3], (N_DP, 4), MINLEN, MAXLEN + 1)
    long_second = jax.random.randint(streams[4], (N_DP, 4), MINLEN, MAXLEN + 1)
    long_len = jnp.maximum(long_first, long_second)
    short_len = jax.random.randint(streams[5], (N_DP, 4), MINLEN, short_bound + 1)
    lengths = jnp.where((home_class == 0)[:, None], long_len, short_len).astype(jnp.int32)
    forced = jax.random.randint(streams[6], (), 0, N_DP).astype(jnp.int32)
    forced_class = forced % 2 + 2 * (forced // half_way)
    is_heavy = slot_class == forced_class
    rank = jnp.cumsum(jnp.where(is_heavy, 0, 1)) - 1
    fill_vals = jnp.array([short_bound, short_bound, WORK - MAXLEN - 2 * short_bound], jnp.int32)
    forced_vals = jnp.where(is_heavy, MAXLEN, fill_vals[jnp.clip(rank, 0, 2)]).astype(jnp.int32)
    slot_ids = jnp.arange(4).astype(jnp.int32)
    lengths = lengths.at[jnp.bitwise_xor(forced, slot_masks), slot_ids].set(forced_vals)
    return lengths.astype(jnp.int32)


def draw_x_home(key, part):
    row_count = N_DP * HOME
    first_key = jax.random.fold_in(jax.random.fold_in(key, 3), 0)
    column = jnp.arange(D, dtype=jnp.float32) / (D - 1) - 0.5
    base_vals = jnp.clip(jax.random.normal(first_key, (row_count, D), jnp.float32), -5.0, 5.0)
    values = base_vals * jnp.exp(jnp.log(4.0) * column)[None, :]
    return values.astype(jnp.bfloat16)


def level_of(own_key, shape, cuts, low, largest):
    def one(axis_at, blocks):
        draws = jax.random.uniform(jax.random.fold_in(jax.random.fold_in(own_key, 6), axis_at), (blocks,), jnp.float32, low / len(cuts), largest / len(cuts))
        return jnp.repeat(jnp.exp(draws), shape[axis_at] // blocks).reshape((-1,) + (1,) * (len(shape) - axis_at - 1))

    loudness = one(*cuts[0])
    for cut in cuts[1:]:
        loudness = loudness * one(*cut)
    return loudness


def normal_values(key, dims, width, most, shards=(), held_as=jnp.bfloat16):
    loudness = level_of(key, dims, shards, -0.22, 0.18) if shards else 1.0
    drawn = jax.random.normal(key, dims, jnp.float32) * width * loudness
    return jnp.minimum(jnp.maximum(drawn, -most), most).astype(held_as)


def setup_inputs(seed: int = 0) -> dict:
    streams_of = jax.random.split(jax.random.key(seed), 12)
    x_home = draw_x_home(jax.random.fold_in(streams_of[11], 71), 0)
    cot_home = normal_values(streams_of[1], (N_DP * HOME, D), 1.0, 6.0, ((0, 8), (1, 4)))
    cell_len = draw_cell_len(jax.random.fold_in(streams_of[11], 71), 0)
    norm1_gain = jnp.clip(1.0 + 0.18 * jax.random.normal(streams_of[3], (D,), jnp.float32), 0.1, 1.9)
    norm1_bias = normal_values(streams_of[4], (D,), 0.5, 3.0, ((0, 4),), jnp.float32)
    qkv_weight = normal_values(streams_of[5], (D, 3, D), D ** -0.5, 0.1875, ((2, 4),))
    out_weight = normal_values(streams_of[6], (D, D), (D // 32) ** -0.5, 1.0, ((0, 4),))
    norm2_gain = jnp.clip(1.0 + 0.18 * jax.random.normal(streams_of[7], (D,), jnp.float32), 0.1, 1.9)
    norm2_bias = normal_values(streams_of[8], (D,), 0.5, 3.0, ((0, 4),), jnp.float32)
    up_weight = normal_values(streams_of[9], (D, FF), D ** -0.5, 0.1875, ((1, 4),))
    down_weight = normal_values(streams_of[10], (FF, D), FF ** -0.5, 0.09375, ((0, 4),))
    return dict(x_home=x_home, cot_home=cot_home, cell_len=cell_len, norm1_gain=norm1_gain, norm1_bias=norm1_bias, qkv_weight=qkv_weight, out_weight=out_weight, norm2_gain=norm2_gain, norm2_bias=norm2_bias, up_weight=up_weight, down_weight=down_weight)


@jax.custom_vjp
def low(v):
    return lax.optimization_barrier(v.astype(jnp.bfloat16)).astype(jnp.float32)

@jax.custom_vjp
def low_back(v):
    return v

def low_keep(v):
    return (low(v), None)

def low_pass(kept, grad):
    return (grad,)

def back_keep(v):
    return (v, None)

def back_low(kept, grad):
    return (low(grad),)
low.defvjp(low_keep, low_pass)
low_back.defvjp(back_keep, back_low)
EPS = 1e-05
HIGH = lax.Precision.HIGHEST

def block_rows(row_count):
    block_size = row_count
    while block_size > 1024 and block_size % 2 == 0:
        block_size = block_size // 2
    return block_size

def layer_norm(values, gain, bias):
    mean_row = lax.optimization_barrier(jnp.mean(values, axis=-1, keepdims=True))
    var_row = lax.optimization_barrier(jnp.mean(jnp.square(values - mean_row), axis=-1, keepdims=True))
    return (values - mean_row) * lax.rsqrt(var_row + EPS) * gain + bias

def attention(queries, key_vals, values, cell_ids):
    row_count = queries.shape[0]
    block_size = block_rows(row_count)
    block_count = row_count // block_size
    positions = jnp.arange(row_count).astype(jnp.int32)
    score_scale = HD ** (-0.5)

    @jax.checkpoint
    def one_block(block_index):
        first_row = (block_index * block_size).astype(jnp.int32)
        query_block = lax.dynamic_slice_in_dim(queries, first_row, block_size)
        cell_block = lax.dynamic_slice_in_dim(cell_ids, first_row, block_size)
        row_block = first_row + jnp.arange(block_size).astype(jnp.int32)
        raw_scores = low_back(jnp.einsum('qhd,khd->hqk', query_block, key_vals, precision=HIGH))
        scores = raw_scores * score_scale
        allowed = (cell_block[:, None] == cell_ids[None, :]) & (positions[None, :] <= row_block[:, None])
        scores = jnp.where(allowed[None], scores, -1e+30)
        row_max = lax.optimization_barrier(jnp.max(scores, axis=2, keepdims=True))
        shifted = jnp.exp(scores - row_max)
        row_total = lax.optimization_barrier(jnp.sum(shifted, axis=2, keepdims=True))
        weights = low(shifted / row_total)
        return jnp.einsum('hqk,khd->qhd', weights, values, precision=HIGH)
    mixed_heads = lax.map(one_block, jnp.arange(block_count).astype(jnp.int32))
    return mixed_heads.reshape(row_count, H * HD)

def block_forward(rows_in, cell_ids, params):
    gain_one, bias_one, w_qkv, w_out, gain_two, bias_two, w_up, w_down = params
    row_count = rows_in.shape[0]
    normed1 = low(layer_norm(rows_in, gain_one, bias_one))
    joined = low_back(low(jnp.dot(normed1, w_qkv.reshape(D, 3 * D), precision=HIGH)))
    pieces = joined.reshape(row_count, 3, H, HD)
    mixed = low_back(low(attention(pieces[:, 0], pieces[:, 1], pieces[:, 2], cell_ids)))
    middle = rows_in + low_back(jnp.dot(mixed, w_out, precision=HIGH))
    normed2 = low(layer_norm(middle, gain_two, bias_two))
    hidden_pre = low_back(jnp.dot(normed2, w_up, precision=HIGH))
    hidden = low(jax.nn.gelu(hidden_pre, approximate=True))
    return middle + low_back(jnp.dot(hidden, w_down, precision=HIGH))

def reference(x_home, cot_home, cell_len, norm1_gain, norm1_bias, qkv_weight, out_weight, norm2_gain, norm2_bias, up_weight, down_weight):
    params = tuple((item.astype(jnp.float32) for item in (norm1_gain, norm1_bias, qkv_weight, out_weight, norm2_gain, norm2_bias, up_weight, down_weight)))
    rows_all = x_home.astype(jnp.float32).reshape(N_DP, HOME, D)
    grads_all = cot_home.astype(jnp.float32).reshape(N_DP, HOME, D)

    def one_group(grand_total, inputs):
        rows_in, grad_out, lengths = inputs
        starts = (jnp.cumsum(lengths) - lengths).astype(jnp.int32)
        home_pos = jnp.arange(HOME).astype(jnp.int32)[:, None]
        inside = (home_pos >= starts[None, :]) & (home_pos < (starts + lengths)[None, :])
        live_rows = jnp.any(inside, axis=1)
        slot_ids = jnp.arange(SLOTS).astype(jnp.int32)
        cell_ids = (lax.optimization_barrier(jnp.sum(jnp.where(inside, slot_ids[None, :] + 1, 0), axis=1)) - 1).astype(jnp.int32)

        def apply_layer(values, weights):
            return block_forward(values, cell_ids, weights)
        result, pull = jax.vjp(apply_layer, rows_in, params)
        grad_in, grad_params = pull(jnp.where(live_rows[:, None], grad_out, 0.0))
        grand_total = jax.tree.map(jnp.add, grand_total, grad_params)
        return (grand_total, (jnp.where(live_rows[:, None], result, 0.0), jnp.where(live_rows[:, None], grad_in, 0.0)))
    start_total = jax.tree.map(jnp.zeros_like, params)
    grand_total, outputs = lax.scan(one_group, start_total, (rows_all, grads_all, cell_len))
    weight = N_DP / jnp.sum(cell_len).astype(jnp.float32)
    scaled = tuple((item * weight for item in grand_total))
    out_rows = outputs[0].reshape(N_DP * HOME, D).astype(jnp.bfloat16)
    grad_rows = outputs[1].reshape(N_DP * HOME, D).astype(jnp.bfloat16)
    return (out_rows, grad_rows, scaled[0], scaled[1], scaled[2], scaled[3], scaled[4], scaled[5], scaled[6], scaled[7])
```

```python
import functools

import jax
import jax.numpy as jnp
from jax import lax
from jax.experimental import pallas as pl
from jax.experimental.pallas import tpu as pltpu
from jax.sharding import PartitionSpec as P

D = 1120
HD = 56
EPS = 1e-05
BF = jnp.bfloat16
F32 = jnp.float32
QB = 256
TAIL = 512
SCALE = HD ** (-0.5)


def swap(value, axis, mask):
    size = lax.axis_size(axis)
    return lax.ppermute(value, axis, [(i, i ^ mask) for i in range(size)])


def dot(left, right, dims=((1,), (0,))):
    return lax.dot_general(left, right, (dims, ((), ())), preferred_element_type=F32)


def gelu_tanh(values):
    return jax.nn.gelu(values, approximate=True)


def vmem_whole(shape):
    return pl.BlockSpec(shape, lambda i, *_: (0,) * len(shape))


def assemble_kernel(place, own, near, far, cross, out):
    parts = (own, near, far, cross)
    for mine in range(4):

        @pl.when(place[0] == mine)
        def _(mine=mine):
            out[...] = jnp.concatenate([parts[j ^ mine][...] for j in range(4)], axis=1)


def norm_kernel(place, own, near, far, cross, gain, bias, out, normed):
    assemble_kernel(place, own, near, far, cross, out)
    values = out[...].astype(F32)
    mean_row = jnp.sum(values, axis=1, keepdims=True) * (1.0 / D)
    centered = values - mean_row
    var_row = jnp.sum(centered * centered, axis=1, keepdims=True) * (1.0 / D)
    normed[...] = (centered * lax.rsqrt(var_row + EPS) * gain[...] + bias[...]).astype(BF)


def gather_columns(value):
    near = swap(value, "tensor", 1)
    far = swap(value, "tensor", 2)
    cross = swap(far, "tensor", 1)
    return (value, near, far, cross)


def assemble(parts, place, row_map=None, affine=None):
    rows = parts[0].shape[0]
    step = 256
    spec_in = pl.BlockSpec((step, 280), (lambda i, p: (i, 0)) if row_map is None else row_map)
    spec_out = pl.BlockSpec((step, D), lambda i, p: (i, 0))
    full = jax.ShapeDtypeStruct((rows, D), BF)
    if affine is None:
        body, extra, outs, specs = assemble_kernel, (), full, spec_out
        extra_specs = []
    else:
        body, extra, outs, specs = norm_kernel, affine, (full, full), (spec_out, spec_out)
        extra_specs = [vmem_whole((1, D))] * 2
    return pl.pallas_call(
        body,
        out_shape=outs,
        grid_spec=pltpu.PrefetchScalarGridSpec(
            num_scalar_prefetch=1,
            grid=(rows // step,),
            in_specs=[spec_in] * 4 + extra_specs,
            out_specs=specs,
        ),
        compiler_params=pltpu.CompilerParams(
            dimension_semantics=("arbitrary",), vmem_limit_bytes=16 << 20
        ),
        cost_estimate=pl.CostEstimate(
            flops=rows * D * 10, bytes_accessed=rows * D * 6, transcendentals=0
        ),
    )(place, *parts, *extra)


def first_of(rows, bounds):
    start = jnp.zeros_like(rows)
    for bound in bounds:
        start = jnp.where(rows >= bound, bound, start)
    return start


def block_setup(bounds, step):
    base = step * QB
    low = first_of(base, bounds)
    count = step - low // QB + 1
    return (base, count)


def allowed_keys(bounds, base, width):
    shape = (width, QB)
    keys = base + QB - width + lax.broadcasted_iota(jnp.int32, shape, 0)
    rows = base + lax.broadcasted_iota(jnp.int32, (1, QB), 1)
    return (keys >= first_of(rows, bounds)) & (keys <= rows)


def attend_kernel(heads, table, qkv, mixed, lse, kbuf, vtbuf):
    step = pl.program_id(0)
    cols = heads * HD
    bounds = [table[k] for k in range(4)]
    base, count = block_setup(bounds, step)

    @pl.when(step == 0)
    def _():
        for h in range(heads):
            kbuf[h] = qkv[:, cols + HD * h : cols + HD * (h + 1)]
            vtbuf[h] = qkv[:, 2 * cols + HD * h : 2 * cols + HD * (h + 1)].T

    @pl.when(base >= bounds[3])
    def _():
        mixed[...] = jnp.zeros_like(mixed)
        lse[...] = jnp.zeros_like(lse)

    for blocks in range(1, 4):

        @pl.when((count == blocks) & (base < bounds[3]))
        def _(blocks=blocks):
            width = blocks * QB
            offset = pl.multiple_of(base + QB - width, QB)
            allowed = allowed_keys(bounds, base, width)
            query = qkv[pl.ds(pl.multiple_of(base, QB), QB), :cols]
            pieces = []
            for h in range(heads):
                keys = kbuf[h, pl.ds(offset, width), :]
                scores = dot(keys, query[:, HD * h : HD * (h + 1)], ((1,), (1,))) * SCALE
                scores = jnp.where(allowed, scores, -1e30)
                top = jnp.max(scores, axis=0, keepdims=True)
                shifted = jnp.exp(scores - top)
                total = jnp.sum(shifted, axis=0, keepdims=True)
                weights = (shifted * (1.0 / total)).astype(BF)
                pieces.append(dot(vtbuf[h, :, pl.ds(offset, width)], weights))
                lse[h : h + 1, :] = top + jnp.log(total)
            mixed[...] = jnp.concatenate(pieces, axis=0).T.astype(BF)


def attend(table, qkv):
    rows, cols = qkv.shape[0], qkv.shape[1] // 3
    heads = cols // HD
    return pl.pallas_call(
        functools.partial(attend_kernel, heads),
        out_shape=(
            jax.ShapeDtypeStruct((rows, cols), BF),
            jax.ShapeDtypeStruct((8, rows), F32),
        ),
        grid_spec=pltpu.PrefetchScalarGridSpec(
            num_scalar_prefetch=1,
            grid=(rows // QB,),
            in_specs=[vmem_whole((rows, 3 * cols))],
            out_specs=(
                pl.BlockSpec((QB, cols), lambda i, *_: (i, 0)),
                pl.BlockSpec((8, QB), lambda i, *_: (0, i)),
            ),
            scratch_shapes=[
                pltpu.VMEM((heads, rows, HD), BF),
                pltpu.VMEM((heads, HD, rows), BF),
            ],
        ),
        compiler_params=pltpu.CompilerParams(
            dimension_semantics=("arbitrary",), vmem_limit_bytes=32 << 20
        ),
        cost_estimate=pl.CostEstimate(
            flops=4 * rows * 512 * 256 * heads,
            bytes_accessed=rows * cols * 8,
            transcendentals=rows * 512 * heads,
        ),
    )(table, qkv)


def attend_back_kernel(
    heads, table, qkv, lse, gmix, out, kbuf, vbuf, ktbuf, dkbuf, dvbuf, dqbuf
):
    step = pl.program_id(0)
    cols = heads * HD
    bounds = [table[k] for k in range(4)]
    base, count = block_setup(bounds, step)
    here = pl.ds(pl.multiple_of(base, QB), QB)

    @pl.when(step == 0)
    def _():
        for h in range(heads):
            keys = qkv[:, cols + HD * h : cols + HD * (h + 1)]
            kbuf[h] = keys
            ktbuf[h] = keys.T
            vbuf[h] = qkv[:, 2 * cols + HD * h : 2 * cols + HD * (h + 1)]
        dkbuf[...] = jnp.zeros_like(dkbuf)
        dvbuf[...] = jnp.zeros_like(dvbuf)

    @pl.when(base >= bounds[3])
    def _():
        dqbuf[here, :] = jnp.zeros((QB, cols), BF)

    for blocks in range(1, 4):

        @pl.when((count == blocks) & (base < bounds[3]))
        def _(blocks=blocks):
            width = blocks * QB
            window = pl.ds(pl.multiple_of(base + QB - width, QB), width)
            allowed = allowed_keys(bounds, base, width)
            query = qkv[here, :cols]
            grads = gmix[...]
            pieces = []
            for h in range(heads):
                one_query = query[:, HD * h : HD * (h + 1)]
                one_grad = grads[:, HD * h : HD * (h + 1)]
                scores = dot(kbuf[h, window, :], one_query, ((1,), (1,))) * SCALE
                probs = jnp.exp(jnp.where(allowed, scores, -1e30) - lse[h : h + 1, :])
                grad_probs = dot(vbuf[h, window, :], one_grad, ((1,), (1,)))
                dvbuf[h, window, :] += dot(probs.astype(BF), one_grad)
                delta = jnp.sum(probs * grad_probs, axis=0, keepdims=True)
                grad_scores = (probs * (grad_probs - delta) * SCALE).astype(BF)
                dkbuf[h, window, :] += dot(grad_scores, one_query)
                pieces.append(dot(ktbuf[h, :, window], grad_scores))
            dqbuf[here, :] = jnp.concatenate(pieces, axis=0).T.astype(BF)

    @pl.when(step == pl.num_programs(0) - 1)
    def _():
        out[:, :cols] = dqbuf[...]
        out[:, cols : 2 * cols] = jnp.concatenate(
            [dkbuf[h].astype(BF) for h in range(heads)], axis=1
        )
        out[:, 2 * cols :] = jnp.concatenate([dvbuf[h].astype(BF) for h in range(heads)], axis=1)


def attend_back(table, qkv, lse, gmix):
    rows, cols = qkv.shape[0], qkv.shape[1] // 3
    heads = cols // HD
    return pl.pallas_call(
        functools.partial(attend_back_kernel, heads),
        out_shape=jax.ShapeDtypeStruct((rows, 3 * cols), BF),
        grid_spec=pltpu.PrefetchScalarGridSpec(
            num_scalar_prefetch=1,
            grid=(rows // QB,),
            in_specs=[
                vmem_whole((rows, 3 * cols)),
                pl.BlockSpec((8, QB), lambda i, *_: (0, i)),
                pl.BlockSpec((QB, cols), lambda i, *_: (i, 0)),
            ],
            out_specs=vmem_whole((rows, 3 * cols)),
            scratch_shapes=[
                pltpu.VMEM((heads, rows, HD), BF),
                pltpu.VMEM((heads, rows, HD), BF),
                pltpu.VMEM((heads, HD, rows), BF),
                pltpu.VMEM((heads, rows, HD), F32),
                pltpu.VMEM((heads, rows, HD), F32),
                pltpu.VMEM((rows, cols), BF),
            ],
        ),
        compiler_params=pltpu.CompilerParams(
            dimension_semantics=("arbitrary",), vmem_limit_bytes=48 << 20
        ),
        cost_estimate=pl.CostEstimate(
            flops=10 * rows * 512 * 256 * heads,
            bytes_accessed=rows * cols * 16,
            transcendentals=rows * 512 * heads,
        ),
    )(table, qkv, lse, gmix)


def row_block(value, index, count):
    return lax.dynamic_slice_in_dim(value, index * count, count)


def col_block(value, index, count):
    return lax.dynamic_slice_in_dim(value, index * count, count, axis=1)


def fold_rows(keep, send):
    got = swap(send, "tensor", 1)
    both = keep + got.astype(F32)
    half = both.shape[0] // 2
    last = swap(both[half:].astype(BF), "tensor", 2)
    return both[:half] + last.astype(F32)


def fold_cols(keep, send, own_order=False):
    got = swap(send, "tensor", 1)
    if own_order:
        got = reorder(got, (2, 3, 0, 1))
    both = keep + got.astype(F32)
    half = both.shape[1] // 2
    last = swap(both[:, half:].astype(BF), "tensor", 2)
    if own_order:
        last = reorder(last, (1, 0, 3, 2))
    return both[:, :half] + last.astype(F32)


def reorder(value, blocks):
    count = value.shape[0] // len(blocks)
    return jnp.concatenate([value[b * count : (b + 1) * count] for b in blocks])


def spread_rows(value):
    near = swap(value, "tensor", 1)
    far = swap(value, "tensor", 2)
    cross = swap(far, "tensor", 1)
    return jnp.concatenate([value, far, near, cross], axis=0)


def total_over(value, axis):
    mask = 1
    while mask < lax.axis_size(axis):
        value = value + swap(value, axis, mask)
        mask *= 2
    return value


def shards(
    x_home,
    cot_home,
    cell_len,
    norm1_gain,
    norm1_bias,
    qkv_weight,
    out_weight,
    norm2_gain,
    norm2_bias,
    up_weight,
    down_weight,
):
    groups = cell_len.shape[0]
    home_rows, cols = x_home.shape
    rows = -(-home_rows // 512) * 512
    block = rows // 4
    me = lax.axis_index("tensor")
    group = lax.axis_index("dp")
    order = (me, me ^ 2, me ^ 1, me ^ 3)
    weight = groups / jnp.sum(cell_len).astype(F32)
    my_len = lax.dynamic_index_in_dim(cell_len, group, 0, keepdims=False)
    table = jnp.cumsum(my_len).astype(jnp.int32)
    live_count = table[3]
    place = me.reshape(1).astype(jnp.int32)

    pad = ((0, rows - home_rows), (0, 0))
    live = (jnp.arange(rows) < live_count)[:, None]
    x_own = jnp.pad(x_home, pad)
    cot_own = jnp.where(live, jnp.pad(cot_home, pad), jnp.zeros((), BF))

    affine = jnp.stack([norm1_gain, norm1_bias, norm2_gain, norm2_bias])
    affine_parts = gather_columns(affine)
    affine_all = jnp.stack(affine_parts)
    gain_one, bias_one, gain_two, bias_two = (
        jnp.concatenate(
            [lax.dynamic_index_in_dim(affine_all, me ^ j, 0, keepdims=False)[k] for j in range(4)]
        )[None, :]
        for k in range(4)
    )

    w_qkv = qkv_weight.reshape(D, 3 * cols)

    x_parts = gather_columns(x_own)
    x_full, full_one = assemble(x_parts, place, affine=(gain_one, bias_one))
    cot_parts = gather_columns(cot_own)
    qkv = dot(full_one, w_qkv).astype(BF)
    mixed, lse = attend(table, qkv)
    mixed_rel = jnp.concatenate([row_block(mixed, j, block) for j in order])
    half = rows // 2
    middle = row_block(x_full, me, block).astype(F32) + fold_rows(
        dot(mixed_rel[:half], out_weight), dot(mixed_rel[half:], out_weight).astype(BF)
    )
    mean_two = jnp.mean(middle, axis=1, keepdims=True)
    inv_two = lax.rsqrt(jnp.mean(jnp.square(middle - mean_two), axis=1, keepdims=True) + EPS)
    hat_two = (middle - mean_two) * inv_two
    full_two = spread_rows((hat_two * gain_two + bias_two).astype(BF))

    steps = block // 256

    def row_map(i, p):
        rel = i // steps
        mask = (rel % 2) * 2 + rel // 2
        return ((p[0] ^ mask) * steps + i % steps, 0)

    g_full = assemble(cot_parts, place, row_map=row_map)
    hidden_pre = dot(full_two, up_weight)
    hidden_f32, gelu_pull = jax.vjp(gelu_tanh, hidden_pre)
    hidden = hidden_f32.astype(BF)
    grad_pre = gelu_pull(dot(g_full, down_weight, ((1,), (1,))))[0].astype(BF)
    grad_norm_two = fold_rows(
        dot(grad_pre[:half], up_weight, ((1,), (1,))),
        dot(grad_pre[half:], up_weight, ((1,), (1,))).astype(BF),
    )
    grad_up = dot(full_two, grad_pre, ((0,), (0,))).astype(BF)
    grad_down = dot(hidden, g_full, ((0,), (0,))).astype(BF)
    grad_up, grad_down = lax.psum((grad_up, grad_down), "dp")

    down_rel = [col_block(down_weight, j, cols) for j in order]
    down_keep = jnp.concatenate(down_rel[:2], axis=1)
    down_send = jnp.concatenate(down_rel[2:], axis=1)
    middle_rel = [col_block(middle, j, cols) for j in order]
    skip = ((0, rows - block), (0, 0))
    out_rel = fold_cols(
        dot(hidden, down_keep) + jnp.pad(jnp.concatenate(middle_rel[:2], axis=1), skip),
        (dot(hidden, down_send) + jnp.pad(jnp.concatenate(middle_rel[2:], axis=1), skip)).astype(BF),
        own_order=True,
    ).astype(BF)

    def natural_rows(value):
        where = (0, 2, 1, 3)
        slot = [me ^ j for j in range(4)]
        spot = jnp.array(where, jnp.int32)
        return jnp.concatenate([row_block(value, spot[s], block) for s in slot])

    out_rows = jnp.where(live, natural_rows(out_rel), jnp.zeros((), BF))[:home_rows]

    a_two = grad_norm_two * gain_two
    grad_middle = row_block(g_full, 0, block).astype(F32) + inv_two * (
        a_two
        - jnp.mean(a_two, axis=1, keepdims=True)
        - hat_two * jnp.mean(a_two * hat_two, axis=1, keepdims=True)
    )
    gm_full = spread_rows(grad_middle.astype(BF))
    grad_out_w = dot(mixed_rel, gm_full, ((0,), (0,))).astype(BF)
    grad_mixed = natural_rows(dot(gm_full, out_weight, ((1,), (1,))).astype(BF))
    grad_joined = attend_back(table, qkv, lse, grad_mixed)
    grad_qkv = dot(full_one, grad_joined, ((0,), (0,))).astype(BF)
    grad_qkv, grad_out_w = lax.psum((grad_qkv, grad_out_w), "dp")

    w_rel = [row_block(w_qkv, j, cols) for j in order]
    grad_norm_one = fold_cols(
        dot(grad_joined, jnp.concatenate(w_rel[:2]), ((1,), (1,))),
        dot(grad_joined, jnp.concatenate(w_rel[2:]), ((1,), (1,))).astype(BF),
    )
    x_wide = x_full.astype(F32)
    mean_one = jnp.mean(x_wide, axis=1, keepdims=True)
    inv_one = lax.rsqrt(jnp.mean(jnp.square(x_wide - mean_one), axis=1, keepdims=True) + EPS)
    hat_one = (x_own.astype(F32) - mean_one) * inv_one
    a_one = grad_norm_one * norm1_gain
    sums = total_over(jnp.stack([jnp.sum(a_one, axis=1), jnp.sum(a_one * hat_one, axis=1)]), "tensor")
    gm_own = natural_rows(
        lax.switch(me, [lambda v, j=j: v[:, cols * j : cols * (j + 1)] for j in range(4)], gm_full)
    )
    x_grad = gm_own.astype(F32) + inv_one * (
        a_one - sums[0][:, None] / D - hat_one * (sums[1][:, None] / D)
    )
    x_grad = x_grad.astype(BF)[:home_rows]

    two = jnp.stack([jnp.sum(grad_norm_two * hat_two, axis=0), jnp.sum(grad_norm_two, axis=0)])
    two = total_over(two, "tensor")
    two = lax.dynamic_slice_in_dim(two, me * cols, cols, axis=1)
    one = jnp.stack([jnp.sum(grad_norm_one * hat_one, axis=0), jnp.sum(grad_norm_one, axis=0)])
    small = total_over(jnp.concatenate([one, two]), "dp") * weight

    def scaled(item):
        return item.astype(F32) * weight

    return (
        out_rows,
        x_grad,
        small[0],
        small[1],
        scaled(grad_qkv).reshape(D, 3, cols),
        scaled(grad_out_w),
        small[2],
        small[3],
        scaled(grad_up),
        scaled(grad_down),
    )


def solution(mesh):
    rows, vector = P("dp", "tensor"), P("tensor")
    qkv, wide, tall = P(None, None, "tensor"), P(None, "tensor"), P("tensor", None)
    return jax.shard_map(
        shards,
        mesh=mesh,
        in_specs=(rows, rows, P(), vector, vector, qkv, tall, vector, vector, wide, tall),
        out_specs=(rows, rows, vector, vector, qkv, tall, vector, vector, wide, tall),
        check_vma=False,
    )
```

```python
import functools

import jax
import jax.numpy as jnp
from jax import lax
from jax.experimental import pallas as pl
from jax.experimental.pallas import tpu as pltpu
from jax.sharding import PartitionSpec as P


D = 1120
HD = 56
EPS = 1e-05
BF = jnp.bfloat16
F32 = jnp.float32
QB = 256
SCALE = HD ** (-0.5)
MIB = 1 << 20


def swap(value, axis, mask):
    size = lax.axis_size(axis)
    return lax.ppermute(value, axis, [(i, i ^ mask) for i in range(size)])


def dot(left, right, dims=((1,), (0,))):
    return lax.dot_general(left, right, (dims, ((), ())), preferred_element_type=F32)


def gelu_tanh(values):
    return jax.nn.gelu(values, approximate=True)


def spot(rel):
    return (rel % 2) * 2 + rel // 2


def whole(shape):
    return pl.BlockSpec(shape, lambda i, *_: (0,) * len(shape), pipeline_mode=pl.Buffered(1))


def lanes(rows, width, where=None):
    return pl.BlockSpec((rows, width), (lambda i, s: (0, i)) if where is None else where)


def call(body, info, args, in_specs, outs, out_specs, steps, cost, scratch=(), vmem=40, alias=None):
    flops, moved = cost
    return pl.pallas_call(
        body,
        out_shape=outs,
        grid_spec=pltpu.PrefetchScalarGridSpec(
            num_scalar_prefetch=1,
            grid=(steps,),
            in_specs=in_specs,
            out_specs=out_specs,
            scratch_shapes=list(scratch),
        ),
        input_output_aliases=alias or {},
        compiler_params=pltpu.CompilerParams(
            dimension_semantics=("arbitrary",), vmem_limit_bytes=vmem * MIB
        ),
        cost_estimate=pl.CostEstimate(
            flops=int(flops), bytes_accessed=int(moved), transcendentals=0
        ),
    )(info, *args)


def array(*shape, dtype=BF):
    return jax.ShapeDtypeStruct(shape, dtype)


def place_features(info, parts, scratch, live=None):
    count = parts[0].shape[0]
    for rel in range(4):
        value = parts[rel][...].astype(F32)
        if live is not None:
            value = jnp.where(live, value, 0.0)
        start = pl.multiple_of((info[4] ^ rel) * count, 8)
        scratch[pl.ds(start, count), :] = value


def live_lanes(info, base, width):
    return base + lax.broadcasted_iota(jnp.int32, (1, width), 1) < info[3]


def first_of(rows, bounds):
    start = jnp.zeros_like(rows)
    for bound in bounds:
        start = jnp.where(rows >= bound, bound, start)
    return start


def window_blocks(bounds, step):
    return step - first_of(step * QB, bounds) // QB + 1


def allowed_keys(bounds, base, width):
    keys = base + QB - width + lax.broadcasted_iota(jnp.int32, (width, QB), 0)
    rows = base + lax.broadcasted_iota(jnp.int32, (1, QB), 1)
    return (keys >= first_of(rows, bounds)) & (keys <= rows)


def norm_rows(values):
    mean_row = jnp.sum(values, axis=0, keepdims=True) * (1.0 / D)
    centered = values - mean_row
    var_row = jnp.sum(centered * centered, axis=0, keepdims=True) * (1.0 / D)
    inv_row = lax.rsqrt(var_row + EPS)
    return (centered * inv_row, mean_row, inv_row)


def front_kernel(
    heads,
    info,
    own,
    near,
    far,
    cross,
    affine,
    wqkv,
    wout,
    normed,
    qkv,
    mixed,
    stats,
    keep,
    send,
    xmid,
    wide,
    kbuf,
    vtbuf,
    proj,
):
    step = pl.program_id(0)
    cols = heads * HD
    base = step * QB
    bounds = [info[k] for k in range(4)]
    count = window_blocks(bounds, step)
    here = pl.ds(pl.multiple_of(base, QB), QB)
    per = keep.shape[1] // 2 // QB
    rel = (step // per) ^ info[4]
    inner = step % per

    @pl.when(base >= bounds[3])
    def _():
        normed[...] = jnp.zeros_like(normed)
        qkv[...] = jnp.zeros_like(qkv)
        mixed[...] = jnp.zeros_like(mixed)
        stats[...] = jnp.zeros_like(stats)
        proj[...] = jnp.zeros_like(proj)
        wide[...] = jnp.zeros_like(wide)

    @pl.when(base < bounds[3])
    def _():
        place_features(info, (own, near, far, cross), wide, live_lanes(info, base, QB))
        hat, mean_row, inv_row = norm_rows(wide[...])
        stats[0:1, :] = mean_row
        stats[1:2, :] = inv_row
        normed[...] = (hat * affine[:, 0:1] + affine[:, 1:2]).astype(BF)
        joined = dot(wqkv[...], normed[...])
        qkv[...] = joined.astype(BF)
        for h in range(heads):
            keys = joined[cols + HD * h : cols + HD * (h + 1)]
            kbuf[h, here, :] = keys.T.astype(BF)
            vtbuf[h, :, here] = joined[2 * cols + HD * h : 2 * cols + HD * (h + 1)].astype(BF)
        for blocks in range(1, 4):

            @pl.when(count == blocks)
            def _(blocks=blocks):
                width = blocks * QB
                window = pl.ds(pl.multiple_of(base + QB - width, QB), width)
                allowed = allowed_keys(bounds, base, width)
                pieces = []
                for h in range(heads):
                    query = joined[HD * h : HD * (h + 1)].astype(BF)
                    scores = dot(kbuf[h, window, :], query) * SCALE
                    scores = jnp.where(allowed, scores, -1e30)
                    top = jnp.max(scores, axis=0, keepdims=True)
                    shifted = jnp.exp(scores - top)
                    total = jnp.sum(shifted, axis=0, keepdims=True)
                    weights = (shifted * (1.0 / total)).astype(BF)
                    pieces.append(dot(vtbuf[h, :, window], weights))
                    stats[2 + h : 3 + h, :] = top + jnp.log(total)
                mixed[...] = jnp.concatenate(pieces, axis=0).astype(BF)

        proj[...] = dot(wout[...], mixed[...]).astype(BF)

    target = pl.ds(pl.multiple_of((rel // 2) * (per * QB) + inner * QB, QB), QB)

    @pl.when(rel % 2 == 0)
    def _():
        keep[:, target] = proj[...]

    @pl.when(rel % 2 == 1)
    def _():
        send[:, target] = proj[...]

    @pl.when(rel == 0)
    def _():
        xmid[:, pl.ds(pl.multiple_of(inner * QB, QB), QB)] = wide[...].astype(BF)


def front(info, parts, affine, wqkv, wout, rows):
    joined, cols = wqkv.shape[0], wqkv.shape[0] // 3
    heads = cols // HD
    steps = rows // QB
    per = steps // 4

    def rel_lanes(i, s):
        return (0, spot((i // per) ^ s[4]) * per + i % per)

    return call(
        functools.partial(front_kernel, heads),
        info,
        (*parts, affine, wqkv, wout),
        [lanes(cols, QB)] * 4 + [whole((D, 4)), whole((joined, D)), whole((D, cols))],
        (
            array(D, rows),
            array(joined, rows),
            array(cols, rows),
            array(16, rows, dtype=F32),
            array(D, rows // 2),
            array(D, rows // 2),
            array(D, rows // 4),
        ),
        (
            lanes(D, QB),
            lanes(joined, QB),
            lanes(cols, QB, rel_lanes),
            lanes(16, QB),
            whole((D, rows // 2)),
            whole((D, rows // 2)),
            whole((D, rows // 4)),
        ),
        steps,
        (rows * D * 4 * cols * 4, rows * D * 20),
        [
            pltpu.VMEM((D, QB), F32),
            pltpu.VMEM((heads, rows, HD), BF),
            pltpu.VMEM((heads, HD, rows), BF),
            pltpu.VMEM((D, QB), BF),
        ],
    )


def add_kernel(info, left, right, out):
    out[...] = (left[...].astype(F32) + right[...].astype(F32)).astype(BF)


def fold_far(info, keep, got):
    rows = keep.shape[1] // 2
    step = 256
    shift = rows // step
    spec = lanes(D, step, lambda i, s: (0, i + shift))
    return call(
        add_kernel,
        info,
        (keep, got),
        [spec, spec],
        array(D, rows),
        lanes(D, step),
        rows // step,
        (rows * D, rows * D * 6),
    )


def middle_kernel(info, xmid, keep, got, last, affine, middle, normed, stats):
    values = xmid[...].astype(F32) + keep[...].astype(F32)
    values = values + got[...].astype(F32) + last[...].astype(F32)
    middle[...] = values
    hat, mean_row, inv_row = norm_rows(values)
    normed[...] = (hat * affine[:, 2:3] + affine[:, 3:4]).astype(BF)
    stats[...] = jnp.concatenate([mean_row, inv_row] * 4, axis=0)


def second_norm(info, xmid, keep, got, last, affine):
    rows = xmid.shape[1]
    step = 128
    return call(
        middle_kernel,
        info,
        (xmid, keep, got, last, affine),
        [lanes(D, step)] * 4 + [whole((D, 4))],
        (array(D, rows, dtype=F32), array(D, rows), array(8, rows, dtype=F32)),
        (lanes(D, step), lanes(D, step), lanes(8, step)),
        rows // step,
        (rows * D * 10, rows * D * 14),
    )


def cotangent_kernel(per, info, own, near, far, cross, out, wide):
    step = pl.program_id(0)
    place = step // per
    rel = (place % 2) * 2 + place // 2
    base = ((info[4] ^ rel) * per + step % per) * QB
    place_features(info, (own, near, far, cross), wide, live_lanes(info, base, QB))
    out[...] = wide[...].astype(BF)


def cotangent(info, parts, rows):
    steps = rows // QB
    per = steps // 4

    def natural(i, s):
        return (0, (s[4] ^ spot(i // per)) * per + i % per)

    return call(
        functools.partial(cotangent_kernel, per),
        info,
        parts,
        [lanes(parts[0].shape[0], QB, natural)] * 4,
        array(D, rows),
        lanes(D, QB),
        steps,
        (rows * D, rows * D * 6),
        [pltpu.VMEM((D, QB), F32)],
    )


def feed_kernel(
    first, per, info, n_one, n_two, g_rel, middle, wup_t, wup, wdown, wdown_t, *refs
):
    hidden, gpre, pn_one, pn_two, pd_keep, pd_send, now, act = refs[-8:]
    step = pl.program_id(0)
    rel = (0 if first else 2) + step // per
    base = ((info[4] ^ rel) * per + step % per) * QB
    cols = pd_keep.shape[0] // 2

    @pl.when(step < per)
    def _():
        now[...] = n_one[...]

    @pl.when(step >= per)
    def _():
        now[...] = n_two[...]

    @pl.when(base >= info[3])
    def _():
        for ref in (hidden, gpre, act, pd_keep, pd_send):
            ref[...] = jnp.zeros_like(ref)

    @pl.when(base < info[3])
    def _():
        pre = dot(wup_t[...], now[...])
        value, pull = jax.vjp(gelu_tanh, pre)
        hidden[...] = value.astype(BF)
        gpre[...] = pull(dot(wdown[...], g_rel[...]))[0].astype(BF)
        act[...] = dot(wup[...], gpre[...]).astype(BF)
        down = dot(wdown_t[...], hidden[...])
        if first:
            scale = jnp.where(step < per, 1.0, 0.0)
            for r, part in ((0, pd_keep), (2, pd_keep), (1, pd_send), (3, pd_send)):
                half = r // 2 * cols
                rows = pl.ds(pl.multiple_of((info[4] ^ r) * cols, 8), cols)
                start = half + (r % 2) * 2 * cols
                part[half : half + cols, :] = (
                    down[start : start + cols] + middle[rows, :] * scale
                ).astype(BF)
        else:
            pd_keep[...] = down[: 2 * cols].astype(BF)
            pd_send[...] = down[2 * cols :].astype(BF)

    @pl.when(step < per)
    def _():
        pn_one[...] = act[...]

    @pl.when(step >= per)
    def _():
        pn_two[...] = act[...]


def feed(info, first, n_one, n_two, g_rel, middle, weights, before=()):
    rows = g_rel.shape[1]
    steps = rows // QB // 2
    per = steps // 2
    cols = D // 4

    def place(i, s):
        return (0, ((i // per) * 2 + (0 if first else 1)) * per + i % per)

    low = lanes(D, QB, lambda i, s: (0, jnp.minimum(i, per - 1)))
    high = lanes(D, QB, lambda i, s: (0, jnp.maximum(i - per, 0)))
    spec = lanes(D, QB, place)
    half = lanes(2 * cols, QB, place)
    args = (n_one, n_two, g_rel, middle, *weights, *before)
    fixed = 4 + len(weights)
    return call(
        functools.partial(feed_kernel, first, per),
        info,
        args,
        [low, high, spec, low]
        + [whole((D, D))] * 4
        + [pl.BlockSpec(memory_space=pl.ANY)] * len(before),
        (
            array(D, rows),
            array(D, rows),
            array(D, rows // 4),
            array(D, rows // 4),
            array(2 * cols, rows),
            array(2 * cols, rows),
        ),
        (spec, spec, low, high, half, half),
        steps,
        (rows * D * D * 4, rows * D * 10 + D * D * 8),
        [pltpu.VMEM((D, QB), BF), pltpu.VMEM((D, QB), BF)],
        alias={fixed + 1 + k: out for k, out in enumerate((0, 1, 4, 5)[: len(before)])},
        vmem=48,
    )


def back_norm_kernel(info, keep, got, last, middle, stats, g_rel, affine, grad, sums):
    @pl.when(pl.program_id(0) == 0)
    def _():
        sums[...] = jnp.zeros_like(sums)

    total = keep[...].astype(F32) + got[...].astype(F32) + last[...].astype(F32)
    inv_row = stats[1:2, :]
    hat = (middle[...] - stats[0:1, :]) * inv_row
    scaled = total * affine[:, 2:3]
    product = scaled * hat
    mean_one = jnp.sum(scaled, axis=0, keepdims=True) * (1.0 / D)
    mean_two = jnp.sum(product, axis=0, keepdims=True) * (1.0 / D)
    grad[...] = (
        g_rel[...].astype(F32) + inv_row * (scaled - mean_one - hat * mean_two)
    ).astype(BF)
    sums[:, 0:1] += jnp.sum(total * hat, axis=1, keepdims=True)
    sums[:, 1:2] += jnp.sum(total, axis=1, keepdims=True)


def back_norm(info, keep, got, last, middle, stats, g_rel, affine):
    rows = middle.shape[1]
    step = 128
    return call(
        back_norm_kernel,
        info,
        (keep, got, last, middle, stats, g_rel, affine),
        [lanes(D, step)] * 4 + [lanes(8, step), lanes(D, step), whole((D, 4))],
        (array(D, rows), array(D, 2, dtype=F32)),
        (lanes(D, step), whole((D, 2))),
        rows // step,
        (rows * D * 20, rows * D * 14),
    )


def back_kernel(
    heads,
    info,
    own,
    near,
    far,
    cross,
    qkv,
    qkv_now,
    stats,
    wout,
    wqkv,
    joined,
    keep,
    send,
    gown,
    now,
    wide,
    kbuf,
    vbuf,
    ktbuf,
    dkbuf,
    dvbuf,
):
    steps = pl.num_programs(0)
    step = steps - 1 - pl.program_id(0)
    cols = heads * HD
    base = step * QB
    bounds = [info[k] for k in range(4)]
    count = window_blocks(bounds, step)
    here = pl.ds(pl.multiple_of(base, QB), QB)
    rel = (step // (steps // 4)) ^ info[4]

    @pl.when(pl.program_id(0) == 0)
    def _():
        dkbuf[...] = jnp.zeros_like(dkbuf)
        dvbuf[...] = jnp.zeros_like(dvbuf)
        for h in range(heads):
            keys = qkv[cols + HD * h : cols + HD * (h + 1), :]
            ktbuf[h] = keys
            kbuf[h] = keys.T
            vbuf[h] = qkv[2 * cols + HD * h : 2 * cols + HD * (h + 1), :].T

    for r, part in enumerate((own, near, far, cross)):

        @pl.when(rel == r)
        def _(part=part):
            now[...] = part[...]

    wide[...] = now[...].astype(F32)
    gown[...] = wide[pl.ds(pl.multiple_of(info[4] * cols, 8), cols), :].astype(BF)

    @pl.when(base >= bounds[3])
    def _():
        for ref in (joined, keep, send):
            ref[...] = jnp.zeros_like(ref)

    @pl.when(base < bounds[3])
    def _():
        gmix = dot(wout[...], now[...])
        for blocks in range(1, 4):

            @pl.when(count == blocks)
            def _(blocks=blocks):
                width = blocks * QB
                window = pl.ds(pl.multiple_of(base + QB - width, QB), width)
                allowed = allowed_keys(bounds, base, width)
                for h in range(heads):
                    query = qkv_now[HD * h : HD * (h + 1), :]
                    grads = gmix[HD * h : HD * (h + 1)].astype(BF)
                    scores = dot(kbuf[h, window, :], query) * SCALE
                    probs = jnp.exp(
                        jnp.where(allowed, scores, -1e30) - stats[2 + h : 3 + h, :]
                    )
                    grad_probs = dot(vbuf[h, window, :], grads)
                    dvbuf[h, :, window] += dot(grads, probs.astype(BF), ((1,), (1,)))
                    delta = jnp.sum(probs * grad_probs, axis=0, keepdims=True)
                    grad_scores = (probs * (grad_probs - delta) * SCALE).astype(BF)
                    dkbuf[h, :, window] += dot(query, grad_scores, ((1,), (1,)))
                    wide[HD * h : HD * (h + 1), :] = dot(ktbuf[h, :, window], grad_scores)

        for h in range(heads):
            wide[cols + HD * h : cols + HD * (h + 1), :] = dkbuf[h, :, here]
            wide[2 * cols + HD * h : 2 * cols + HD * (h + 1), :] = dvbuf[h, :, here]
        joined[...] = wide[: 3 * cols, :].astype(BF)
        partial = dot(wqkv[...], joined[...])
        keep[...] = partial[: 2 * cols].astype(BF)
        send[...] = partial[2 * cols :].astype(BF)


def back(info, parts, qkv, stats, wout, wqkv):
    rows = qkv.shape[1]
    joined, cols = qkv.shape[0], qkv.shape[0] // 3
    heads = cols // HD
    steps = rows // QB
    per = steps // 4

    def turn(i, s):
        return (0, steps - 1 - i)

    def part_spec(r):
        def where(i, s):
            step = steps - 1 - i
            return (0, jnp.where((step // per) ^ s[4] == r, step % per, 0))

        return lanes(D, QB, where)

    return call(
        functools.partial(back_kernel, heads),
        info,
        (*parts, qkv, qkv, stats, wout, wqkv),
        [part_spec(r) for r in range(4)]
        + [whole((joined, rows)), lanes(joined, QB, turn), lanes(16, QB, turn)]
        + [whole((cols, D)), whole((D, joined))],
        (array(joined, rows), array(2 * cols, rows), array(2 * cols, rows), array(cols, rows)),
        (
            lanes(joined, QB, turn),
            lanes(2 * cols, QB, turn),
            lanes(2 * cols, QB, turn),
            lanes(cols, QB, turn),
        ),
        steps,
        (rows * D * 4 * cols * 6, rows * D * 20),
        [
            pltpu.VMEM((D, QB), BF),
            pltpu.VMEM((D, QB), F32),
            pltpu.VMEM((heads, rows, HD), BF),
            pltpu.VMEM((heads, rows, HD), BF),
            pltpu.VMEM((heads, HD, rows), BF),
            pltpu.VMEM((heads, HD, rows), F32),
            pltpu.VMEM((heads, HD, rows), F32),
        ],
        vmem=48,
    )


def column_maps(per, relative, row):
    def mine(i, s):
        return (row, spot((i // per) ^ s[4]) * per + i % per if relative else i)

    def near(i, s):
        return (row, spot((i // per) ^ s[4] ^ 1) * per + i % per if relative else i)

    return (mine, near)


def fold_columns_far(info, keep, got, relative):
    cols, rows = keep.shape[0] // 2, keep.shape[1]
    steps = rows // QB
    mine, near = column_maps(steps // 4, relative, 1)
    return call(
        add_kernel,
        info,
        (keep, got),
        [lanes(cols, QB, mine), lanes(cols, QB, near)],
        array(cols, rows),
        lanes(cols, QB),
        steps,
        (rows * cols, rows * cols * 6),
    )


def out_kernel(info, keep, got, last, out):
    total = keep[...].astype(F32) + got[...].astype(F32) + last[...].astype(F32)
    live = live_lanes(info, pl.program_id(0) * QB, QB)
    out[...] = jnp.where(live, total, 0.0).astype(BF)


def out_rows(info, keep, got, last, home_rows):
    cols, rows = last.shape
    steps = rows // QB
    mine, near = column_maps(steps // 4, True, 0)
    return call(
        out_kernel,
        info,
        (keep, got, last),
        [lanes(cols, QB, mine), lanes(cols, QB, near), lanes(cols, QB)],
        array(cols, home_rows),
        lanes(cols, QB),
        steps,
        (rows * cols * 4, rows * cols * 8),
    )


def first_sums_kernel(info, keep, got, last, x, stats, gain, total, rowsums, sums):
    @pl.when(pl.program_id(0) == 0)
    def _():
        sums[...] = jnp.zeros_like(sums)

    live = live_lanes(info, pl.program_id(0) * QB, QB)
    grad = keep[...].astype(F32) + got[...].astype(F32) + last[...].astype(F32)
    grad = jnp.where(live, grad, 0.0)
    hat = (jnp.where(live, x[...].astype(F32), 0.0) - stats[0:1, :]) * stats[1:2, :]
    scaled = grad * gain[:, 0:1]
    total[...] = grad
    one = jnp.sum(scaled, axis=0, keepdims=True)
    two = jnp.sum(scaled * hat, axis=0, keepdims=True)
    rowsums[...] = jnp.concatenate([one, two] * 4, axis=0)
    sums[:, 0:1] += jnp.sum(grad * hat, axis=1, keepdims=True)
    sums[:, 1:2] += jnp.sum(grad, axis=1, keepdims=True)


def first_sums(info, keep, got, last, x, stats, gain):
    cols, rows = last.shape
    top = lanes(cols, QB)
    return call(
        first_sums_kernel,
        info,
        (keep, got, last, x, stats, gain),
        [top, top, top, top, lanes(16, QB), whole((cols, 2))],
        (array(cols, rows, dtype=F32), array(8, rows, dtype=F32), array(cols, 2, dtype=F32)),
        (top, lanes(8, QB), whole((cols, 2))),
        rows // QB,
        (rows * cols * 10, rows * cols * 14),
    )


def x_grad_kernel(info, total, rowsums, x, stats, gain, gown, out):
    live = live_lanes(info, pl.program_id(0) * QB, QB)
    inv_row = stats[1:2, :]
    hat = (jnp.where(live, x[...].astype(F32), 0.0) - stats[0:1, :]) * inv_row
    inner = total[...] * gain[:, 0:1] - rowsums[0:1, :] * (1.0 / D)
    inner = inner - hat * (rowsums[1:2, :] * (1.0 / D))
    grad = gown[...].astype(F32) + inv_row * inner
    out[...] = jnp.where(live, grad, 0.0).astype(BF)


def x_gradient(info, total, rowsums, x, stats, gain, gown, home_rows):
    cols, rows = total.shape
    top = lanes(cols, QB)
    return call(
        x_grad_kernel,
        info,
        (total, rowsums, x, stats, gain, gown),
        [top, lanes(8, QB), top, lanes(16, QB), whole((cols, 2)), top],
        array(cols, home_rows),
        top,
        rows // QB,
        (rows * cols * 10, rows * cols * 14),
    )


def gather_parts(value):
    near = swap(value, "tensor", 1)
    far = swap(value, "tensor", 2)
    return (value, near, far, swap(far, "tensor", 1))


def total_over(value, axis):
    mask = 1
    while mask < lax.axis_size(axis):
        value = value + swap(value, axis, mask)
        mask *= 2
    return value


def sum_groups(value, group):
    halved = []
    mask = 1
    while mask < lax.axis_size("dp"):
        if len(halved) < 2:
            half = value.shape[0] // 2
            bit = (group // mask) % 2
            got = swap(lax.dynamic_slice_in_dim(value, (1 - bit) * half, half), "dp", mask)
            mine = lax.dynamic_slice_in_dim(value, bit * half, half)
            halved.append((mask, bit))
        else:
            got, mine = swap(value, "dp", mask), value
        value = (mine.astype(F32) + got.astype(F32)).astype(BF)
        mask *= 2
    for mask, bit in reversed(halved):
        other = swap(value, "dp", mask)
        low = bit == 0
        value = jnp.concatenate([jnp.where(low, value, other), jnp.where(low, other, value)])
    return value


def shards(
    x_home,
    cot_home,
    cell_len,
    norm1_gain,
    norm1_bias,
    qkv_weight,
    out_weight,
    norm2_gain,
    norm2_bias,
    up_weight,
    down_weight,
):
    groups = cell_len.shape[0]
    home_rows, cols = x_home.shape
    rows = -(-home_rows // 1024) * 1024
    me = lax.axis_index("tensor").astype(jnp.int32)
    group = lax.axis_index("dp")
    weight = groups / jnp.sum(cell_len).astype(F32)
    my_len = lax.dynamic_index_in_dim(cell_len, group, 0, keepdims=False)
    bounds = jnp.cumsum(my_len).astype(jnp.int32)
    info = jnp.concatenate([bounds, jnp.broadcast_to(me, (4,))])
    order = (me, me ^ 2, me ^ 1, me ^ 3)

    x = x_home.T
    x_parts = gather_parts(x)
    cot_parts = gather_parts(cot_home.T)
    own_affine = jnp.stack([norm1_gain, norm1_bias, norm2_gain, norm2_bias], axis=1)
    stacked = jnp.stack(gather_parts(own_affine))
    affine = jnp.concatenate(
        [lax.dynamic_index_in_dim(stacked, me ^ j, 0, keepdims=False) for j in range(4)]
    )

    def rel_rows(value):
        return jnp.concatenate([lax.dynamic_slice_in_dim(value, j * cols, cols) for j in order])

    wqkv_t = qkv_weight.transpose(1, 2, 0).reshape(3 * cols, D)
    wqkv = rel_rows(qkv_weight.reshape(D, 3 * cols))
    wout_t = out_weight.T
    wup_t = up_weight.T
    wdown_t = rel_rows(down_weight.T)

    normed, qkv, mixed, stats, keep, send, xmid = front(info, x_parts, affine, wqkv_t, wout_t, rows)
    got = swap(send, "tensor", 1)
    last = swap(fold_far(info, keep, got), "tensor", 2)
    middle, n_own, stats_two = second_norm(info, xmid, keep, got, last, affine)
    n_own, n_near, n_far, n_cross = gather_parts(n_own)

    g_rel = cotangent(info, cot_parts, rows)
    weights = (wup_t, up_weight, down_weight, wdown_t)
    hidden, gpre, pn_own, pn_near, pd_keep, pd_send = feed(
        info, True, n_own, n_near, g_rel, middle, weights
    )
    hidden, gpre, pn_far, pn_cross, pd_keep, pd_send = feed(
        info, False, n_far, n_cross, g_rel, middle, weights, (hidden, gpre, pd_keep, pd_send)
    )
    got_own = swap(pn_near, "tensor", 1)
    got_far = swap(pn_cross, "tensor", 1)
    far_sum = call(
        add_kernel,
        info,
        (pn_far, got_far),
        [lanes(D, QB)] * 2,
        array(D, rows // 4),
        lanes(D, QB),
        rows // 4 // QB,
        (rows * D // 4, rows * D * 3 // 2),
    )
    last = swap(far_sum, "tensor", 2)
    grad_mid, sums_two = back_norm(
        info, pn_own, got_own, last, middle, stats_two, g_rel, affine
    )
    g_parts = gather_parts(grad_mid)

    rows_dims = ((1,), (1,))
    n_rel = jnp.concatenate([n_own, n_far, n_near, n_cross], axis=1)
    grad_down = sum_groups(dot(hidden, g_rel, rows_dims).astype(BF), group)
    grad_up = sum_groups(dot(n_rel, gpre, rows_dims).astype(BF), group)

    joined, keep, send, gown = back(info, g_parts, qkv, stats, out_weight, wqkv)
    gm_rel = jnp.concatenate([g_parts[0], g_parts[2], g_parts[1], g_parts[3]], axis=1)
    grad_rest = jnp.concatenate([dot(joined, normed, rows_dims), dot(mixed, gm_rel, rows_dims)])
    grad_rest = sum_groups(grad_rest.astype(BF), group)

    got = swap(send, "tensor", 1)
    last = swap(fold_columns_far(info, keep, got, False), "tensor", 2)
    total, rowsums, sums_one = first_sums(info, keep, got, last, x, stats, own_affine[:, :2])
    rowsums = total_over(rowsums, "tensor")
    x_grad = x_gradient(info, total, rowsums, x, stats, own_affine[:, :2], gown, home_rows)

    got = swap(pd_send, "tensor", 1)
    last = swap(fold_columns_far(info, pd_keep, got, True), "tensor", 2)
    out = out_rows(info, pd_keep, got, last, home_rows)

    sums_two = lax.dynamic_slice_in_dim(total_over(sums_two, "tensor"), me * cols, cols)
    small = total_over(jnp.concatenate([sums_one, sums_two], axis=1), "dp") * weight

    def scaled(item):
        return item.astype(F32) * weight

    grad_qkv = scaled(grad_rest[: 3 * cols]).reshape(3, cols, D).transpose(2, 0, 1)
    return (
        out.T,
        x_grad.T,
        small[:, 0],
        small[:, 1],
        grad_qkv,
        scaled(grad_rest[3 * cols :]),
        small[:, 2],
        small[:, 3],
        scaled(grad_up),
        scaled(grad_down),
    )


def solution(mesh):
    rows, vector = P("dp", "tensor"), P("tensor")
    qkv, wide, tall = P(None, None, "tensor"), P(None, "tensor"), P("tensor", None)
    return jax.shard_map(
        shards,
        mesh=mesh,
        in_specs=(rows, rows, P(), vector, vector, qkv, tall, vector, vector, wide, tall),
        out_specs=(rows, rows, vector, vector, qkv, tall, vector, vector, wide, tall),
        check_vma=False,
    )
```

```python
import functools

import jax
import jax.numpy as jnp
from jax import lax
from jax.experimental import pallas as pl
from jax.experimental.pallas import tpu as pltpu
from jax.sharding import PartitionSpec as P


D = 1120
HD = 56
EPS = 1e-05
BF = jnp.bfloat16
F32 = jnp.float32
QB = 256
SCALE = HD ** (-0.5)
MIB = 1 << 20


def swap(value, axis, mask):
    size = lax.axis_size(axis)
    return lax.ppermute(value, axis, [(i, i ^ mask) for i in range(size)])


def dot(left, right, dims=((1,), (0,))):
    return lax.dot_general(left, right, (dims, ((), ())), preferred_element_type=F32)


def gelu_tanh(values):
    return jax.nn.gelu(values, approximate=True)


def spot(rel):
    return (rel % 2) * 2 + rel // 2


def whole(shape):
    return pl.BlockSpec(shape, lambda i, *_: (0,) * len(shape), pipeline_mode=pl.Buffered(1))


def lanes(rows, width, where=None):
    return pl.BlockSpec((rows, width), (lambda i, s: (0, i)) if where is None else where)


class Line:
    def __init__(self, info):
        self.info = info
        self.last = None

    def start(self):
        if self.last is not None:
            self.info = after(self.info, self.last)
        return self.info

    def tie(self, value):
        return after(value, self.last)

    def other(self, function, value):
        self.last = function(self.tie(value))
        return self.last


def call(body, line, args, in_specs, outs, out_specs, steps, scratch=(), vmem=16, alias=None):
    result = pl.pallas_call(
        body,
        out_shape=outs,
        grid_spec=pltpu.PrefetchScalarGridSpec(
            num_scalar_prefetch=1,
            grid=(steps,),
            in_specs=in_specs,
            out_specs=out_specs,
            scratch_shapes=list(scratch),
        ),
        input_output_aliases=alias or {},
        compiler_params=pltpu.CompilerParams(
            dimension_semantics=("arbitrary",), vmem_limit_bytes=vmem * MIB
        ),
        cost_estimate=pl.CostEstimate(flops=1, bytes_accessed=1, transcendentals=0),
    )(line.start(), *args)
    line.last = result[-1] if isinstance(result, (tuple, list)) else result
    return result


def array(*shape, dtype=BF):
    return jax.ShapeDtypeStruct(shape, dtype)


def place_features(info, parts, scratch, live=None):
    count = parts[0].shape[0]
    for rel in range(4):
        value = parts[rel][...].astype(F32)
        if live is not None:
            value = jnp.where(live, value, 0.0)
        start = pl.multiple_of((info[4] ^ rel) * count, 8)
        scratch[pl.ds(start, count), :] = value


def split_features(info, wide, keep, send):
    count = keep.shape[0] // 2
    for rel in range(4):
        part = send if rel % 2 else keep
        start = pl.multiple_of((info[4] ^ rel) * count, 8)
        half = rel // 2 * count
        part[half : half + count, :] = wide[pl.ds(start, count), :].astype(BF)


def live_lanes(info, base, width):
    return base + lax.broadcasted_iota(jnp.int32, (1, width), 1) < info[3]


def first_of(rows, bounds):
    start = jnp.zeros_like(rows)
    for bound in bounds:
        start = jnp.where(rows >= bound, bound, start)
    return start


def window_blocks(bounds, step):
    return step - first_of(step * QB, bounds) // QB + 1


def allowed_keys(bounds, base, width):
    keys = base + QB - width + lax.broadcasted_iota(jnp.int32, (width, QB), 0)
    rows = base + lax.broadcasted_iota(jnp.int32, (1, QB), 1)
    return (keys >= first_of(rows, bounds)) & (keys <= rows)


def norm_rows(values):
    mean_row = jnp.sum(values, axis=0, keepdims=True) * (1.0 / D)
    centered = values - mean_row
    var_row = jnp.sum(centered * centered, axis=0, keepdims=True) * (1.0 / D)
    inv_row = lax.rsqrt(var_row + EPS)
    return (centered * inv_row, mean_row, inv_row)


def front_kernel(
    heads,
    info,
    own,
    near,
    far,
    cross,
    affine_own,
    affine_near,
    affine_far,
    affine_cross,
    wqkv,
    wout,
    normed,
    qkv,
    mixed,
    stats,
    keep,
    send,
    xmid,
    affine,
    wide,
    kbuf,
    vtbuf,
    proj,
):
    step = pl.program_id(0)
    cols = heads * HD
    base = step * QB
    bounds = [info[k] for k in range(4)]
    count = window_blocks(bounds, step)
    here = pl.ds(pl.multiple_of(base, QB), QB)
    per = keep.shape[1] // 2 // QB
    rel = (step // per) ^ info[4]
    inner = step % per

    @pl.when(step == 0)
    def _():
        place_features(info, (affine_own, affine_near, affine_far, affine_cross), affine)

    @pl.when(base >= bounds[3])
    def _():
        normed[...] = jnp.zeros_like(normed)
        qkv[...] = jnp.zeros_like(qkv)
        mixed[...] = jnp.zeros_like(mixed)
        stats[...] = jnp.zeros_like(stats)
        proj[...] = jnp.zeros_like(proj)
        wide[...] = jnp.zeros_like(wide)

    @pl.when(base < bounds[3])
    def _():
        place_features(info, (own, near, far, cross), wide, live_lanes(info, base, QB))
        hat, mean_row, inv_row = norm_rows(wide[...])
        stats[0:1, :] = mean_row
        stats[1:2, :] = inv_row
        normed[...] = (hat * affine[:, 0:1] + affine[:, 1:2]).astype(BF)
        joined = dot(wqkv[...], normed[...])
        qkv[...] = joined.astype(BF)
        for h in range(heads):
            keys = joined[cols + HD * h : cols + HD * (h + 1)]
            kbuf[h, here, :] = keys.T.astype(BF)
            vtbuf[h, :, here] = joined[2 * cols + HD * h : 2 * cols + HD * (h + 1)].astype(BF)
        for blocks in range(1, 4):

            @pl.when(count == blocks)
            def _(blocks=blocks):
                width = blocks * QB
                window = pl.ds(pl.multiple_of(base + QB - width, QB), width)
                allowed = allowed_keys(bounds, base, width)
                pieces = []
                for h in range(heads):
                    query = joined[HD * h : HD * (h + 1)].astype(BF)
                    scores = dot(kbuf[h, window, :], query) * SCALE
                    scores = jnp.where(allowed, scores, -1e30)
                    top = jnp.max(scores, axis=0, keepdims=True)
                    shifted = jnp.exp(scores - top)
                    total = jnp.sum(shifted, axis=0, keepdims=True)
                    weights = (shifted * (1.0 / total)).astype(BF)
                    pieces.append(dot(vtbuf[h, :, window], weights))
                    stats[2 + h : 3 + h, :] = top + jnp.log(total)
                mixed[...] = jnp.concatenate(pieces, axis=0).astype(BF)

        proj[...] = dot(wout[...], mixed[...]).astype(BF)

    target = pl.ds(pl.multiple_of((rel // 2) * (per * QB) + inner * QB, QB), QB)

    @pl.when(rel % 2 == 0)
    def _():
        keep[:, target] = proj[...]

    @pl.when(rel % 2 == 1)
    def _():
        send[:, target] = proj[...]

    @pl.when(rel == 0)
    def _():
        xmid[:, pl.ds(pl.multiple_of(inner * QB, QB), QB)] = wide[...].astype(BF)


def front(line, parts, affine, wqkv, wout, rows):
    joined, cols = wqkv.shape[0], wqkv.shape[0] // 3
    heads = cols // HD
    steps = rows // QB
    per = steps // 4

    def rel_lanes(i, s):
        return (0, spot((i // per) ^ s[4]) * per + i % per)

    return call(
        functools.partial(front_kernel, heads),
        line,
        (*parts, *affine, wqkv, wout),
        [lanes(cols, QB)] * 4
        + [whole((cols, 4))] * 4
        + [whole((joined, D)), whole((D, cols))],
        (
            array(D, rows),
            array(joined, rows),
            array(cols, rows),
            array(16, rows, dtype=F32),
            array(D, rows // 2),
            array(D, rows // 2),
            array(D, rows // 4),
            array(D, 4, dtype=F32),
        ),
        (
            lanes(D, QB),
            lanes(joined, QB),
            lanes(cols, QB, rel_lanes),
            lanes(16, QB),
            whole((D, rows // 2)),
            whole((D, rows // 2)),
            whole((D, rows // 4)),
            whole((D, 4)),
        ),
        steps,
        [
            pltpu.VMEM((D, QB), F32),
            pltpu.VMEM((heads, rows, HD), BF),
            pltpu.VMEM((heads, HD, rows), BF),
            pltpu.VMEM((D, QB), BF),
        ],
        vmem=62,
    )


def add_kernel(info, left, right, out):
    out[...] = (left[...].astype(F32) + right[...].astype(F32)).astype(BF)


def fold_far(line, keep, got):
    rows = keep.shape[1] // 2
    step = 256
    shift = rows // step
    spec = lanes(D, step, lambda i, s: (0, i + shift))
    return call(
        add_kernel,
        line,
        (keep, got),
        [spec, spec],
        array(D, rows),
        lanes(D, step),
        rows // step,
    )


def middle_kernel(info, xmid, keep, got, last, affine, middle, normed, stats):
    values = xmid[...].astype(F32) + keep[...].astype(F32)
    values = values + got[...].astype(F32) + last[...].astype(F32)
    middle[...] = values
    hat, mean_row, inv_row = norm_rows(values)
    normed[...] = (hat * affine[:, 2:3] + affine[:, 3:4]).astype(BF)
    stats[...] = jnp.concatenate([mean_row, inv_row] * 4, axis=0)


def second_norm(line, xmid, keep, got, last, affine):
    rows = xmid.shape[1]
    step = 128
    return call(
        middle_kernel,
        line,
        (xmid, keep, got, last, affine),
        [lanes(D, step)] * 4 + [whole((D, 4))],
        (array(D, rows, dtype=F32), array(D, rows), array(8, rows, dtype=F32)),
        (lanes(D, step), lanes(D, step), lanes(8, step)),
        rows // step,
    )


def cotangent_kernel(per, info, own, near, far, cross, out, wide):
    step = pl.program_id(0)
    place = step // per
    rel = (place % 2) * 2 + place // 2
    base = ((info[4] ^ rel) * per + step % per) * QB
    place_features(info, (own, near, far, cross), wide, live_lanes(info, base, QB))
    out[...] = wide[...].astype(BF)


def cotangent(line, parts, rows):
    steps = rows // QB
    per = steps // 4

    def natural(i, s):
        return (0, (s[4] ^ spot(i // per)) * per + i % per)

    return call(
        functools.partial(cotangent_kernel, per),
        line,
        parts,
        [lanes(parts[0].shape[0], QB, natural)] * 4,
        array(D, rows),
        lanes(D, QB),
        steps,
        [pltpu.VMEM((D, QB), F32)],
    )


def feed_kernel(
    first, per, info, n_one, n_two, g_rel, middle, wup_t, wup, wdown, wdown_t, *refs
):
    hidden, gpre, pd_keep, pd_send, pn_one, pn_two, now, act, wide = refs[-9:]
    step = pl.program_id(0)
    rel = (0 if first else 2) + step // per
    base = ((info[4] ^ rel) * per + step % per) * QB

    @pl.when(step < per)
    def _():
        now[...] = n_one[...]

    @pl.when(step >= per)
    def _():
        now[...] = n_two[...]

    @pl.when(base >= info[3])
    def _():
        for ref in (hidden, gpre, act, pd_keep, pd_send):
            ref[...] = jnp.zeros_like(ref)

    @pl.when(base < info[3])
    def _():
        pre = dot(wup_t[...], now[...])
        value, pull = jax.vjp(gelu_tanh, pre)
        hidden[...] = value.astype(BF)
        gpre[...] = pull(dot(wdown[...], g_rel[...]))[0].astype(BF)
        act[...] = dot(wup[...], gpre[...]).astype(BF)
        wide[...] = dot(wdown_t[...], hidden[...])
        if first:

            @pl.when(step < per)
            def _():
                wide[...] += middle[...]

        split_features(info, wide, pd_keep, pd_send)

    @pl.when(step < per)
    def _():
        pn_one[...] = act[...]

    @pl.when(step >= per)
    def _():
        pn_two[...] = act[...]


def feed(line, first, n_one, n_two, g_rel, middle, weights, before=()):
    rows = g_rel.shape[1]
    steps = rows // QB // 2
    per = steps // 2
    cols = D // 4

    def place(i, s):
        return (0, ((i // per) * 2 + (0 if first else 1)) * per + i % per)

    low = lanes(D, QB, lambda i, s: (0, jnp.minimum(i, per - 1)))
    high = lanes(D, QB, lambda i, s: (0, jnp.maximum(i - per, 0)))
    spec = lanes(D, QB, place)
    half = lanes(2 * cols, QB, place)
    args = (n_one, n_two, g_rel, middle, *weights, *before)
    fixed = 4 + len(weights)
    return call(
        functools.partial(feed_kernel, first, per),
        line,
        args,
        [low, high, spec, low]
        + [whole((D, D))] * 4
        + [pl.BlockSpec(memory_space=pl.ANY)] * len(before),
        (
            array(D, rows),
            array(D, rows),
            array(2 * cols, rows),
            array(2 * cols, rows),
            array(D, rows // 4),
            array(D, rows // 4),
        ),
        (spec, spec, half, half, low, high),
        steps,
        [pltpu.VMEM((D, QB), BF), pltpu.VMEM((D, QB), BF), pltpu.VMEM((D, QB), F32)],
        vmem=62,
        alias={fixed + 1 + k: k for k in range(len(before))},
    )


def back_norm_kernel(info, keep, got, last, middle, stats, g_rel, affine, grad, turned, sums):
    @pl.when(pl.program_id(0) == 0)
    def _():
        sums[...] = jnp.zeros_like(sums)

    total = keep[...].astype(F32) + got[...].astype(F32) + last[...].astype(F32)
    inv_row = stats[1:2, :]
    hat = (middle[...] - stats[0:1, :]) * inv_row
    scaled = total * affine[:, 2:3]
    product = scaled * hat
    mean_one = jnp.sum(scaled, axis=0, keepdims=True) * (1.0 / D)
    mean_two = jnp.sum(product, axis=0, keepdims=True) * (1.0 / D)
    grad[...] = (
        g_rel[...].astype(F32) + inv_row * (scaled - mean_one - hat * mean_two)
    ).astype(BF)
    sums[:, 2:3] += jnp.sum(total * hat, axis=1, keepdims=True)
    sums[:, 3:4] += jnp.sum(total, axis=1, keepdims=True)

    @pl.when(pl.program_id(0) == pl.num_programs(0) - 1)
    def _():
        turned[...] = sums[...].T[:8]


def back_norm(line, keep, got, last, middle, stats, g_rel, affine):
    rows = middle.shape[1]
    step = 128
    return call(
        back_norm_kernel,
        line,
        (keep, got, last, middle, stats, g_rel, affine),
        [lanes(D, step)] * 4 + [lanes(8, step), lanes(D, step), whole((D, 4))],
        (array(D, rows), array(8, D, dtype=F32)),
        (lanes(D, step), whole((8, D))),
        rows // step,
        [pltpu.VMEM((D, 128), F32)],
    )


def back_kernel(
    heads,
    info,
    own,
    near,
    far,
    cross,
    qkv,
    qkv_now,
    stats,
    wout,
    wqkv,
    gown,
    keep,
    send,
    joined,
    now,
    wide,
    kbuf,
    vbuf,
    ktbuf,
    dkbuf,
    dvbuf,
):
    steps = pl.num_programs(0)
    step = steps - 1 - pl.program_id(0)
    cols = heads * HD
    base = step * QB
    bounds = [info[k] for k in range(4)]
    count = window_blocks(bounds, step)
    here = pl.ds(pl.multiple_of(base, QB), QB)
    rel = (step // (steps // 4)) ^ info[4]

    @pl.when(pl.program_id(0) == 0)
    def _():
        dkbuf[...] = jnp.zeros_like(dkbuf)
        dvbuf[...] = jnp.zeros_like(dvbuf)
        for h in range(heads):
            keys = qkv[cols + HD * h : cols + HD * (h + 1), :]
            ktbuf[h] = keys
            kbuf[h] = keys.T
            vbuf[h] = qkv[2 * cols + HD * h : 2 * cols + HD * (h + 1), :].T

    for r, part in enumerate((own, near, far, cross)):

        @pl.when(rel == r)
        def _(part=part):
            now[...] = part[...]

    wide[...] = now[...].astype(F32)
    gown[...] = wide[pl.ds(pl.multiple_of(info[4] * cols, 8), cols), :].astype(BF)

    @pl.when(base >= bounds[3])
    def _():
        for ref in (joined, keep, send):
            ref[...] = jnp.zeros_like(ref)

    @pl.when(base < bounds[3])
    def _():
        gmix = dot(wout[...], now[...])
        for blocks in range(1, 4):

            @pl.when(count == blocks)
            def _(blocks=blocks):
                width = blocks * QB
                window = pl.ds(pl.multiple_of(base + QB - width, QB), width)
                allowed = allowed_keys(bounds, base, width)
                for h in range(heads):
                    query = qkv_now[HD * h : HD * (h + 1), :]
                    grads = gmix[HD * h : HD * (h + 1)].astype(BF)
                    scores = dot(kbuf[h, window, :], query) * SCALE
                    probs = jnp.exp(
                        jnp.where(allowed, scores, -1e30) - stats[2 + h : 3 + h, :]
                    )
                    grad_probs = dot(vbuf[h, window, :], grads)
                    dvbuf[h, :, window] += dot(grads, probs.astype(BF), ((1,), (1,)))
                    delta = jnp.sum(probs * grad_probs, axis=0, keepdims=True)
                    grad_scores = (probs * (grad_probs - delta) * SCALE).astype(BF)
                    dkbuf[h, :, window] += dot(query, grad_scores, ((1,), (1,)))
                    wide[HD * h : HD * (h + 1), :] = dot(ktbuf[h, :, window], grad_scores)

        for h in range(heads):
            wide[cols + HD * h : cols + HD * (h + 1), :] = dkbuf[h, :, here]
            wide[2 * cols + HD * h : 2 * cols + HD * (h + 1), :] = dvbuf[h, :, here]
        joined[...] = wide[: 3 * cols, :].astype(BF)
        wide[...] = dot(wqkv[...], joined[...])
        split_features(info, wide, keep, send)


def back(line, parts, qkv, stats, wout, wqkv):
    rows = qkv.shape[1]
    joined, cols = qkv.shape[0], qkv.shape[0] // 3
    heads = cols // HD
    steps = rows // QB
    per = steps // 4

    def turn(i, s):
        return (0, steps - 1 - i)

    def part_spec(r):
        def where(i, s):
            step = steps - 1 - i
            return (0, jnp.where((step // per) ^ s[4] == r, step % per, 0))

        return lanes(D, QB, where)

    return call(
        functools.partial(back_kernel, heads),
        line,
        (*parts, qkv, qkv, stats, wout, wqkv),
        [part_spec(r) for r in range(4)]
        + [whole((joined, rows)), lanes(joined, QB, turn), lanes(16, QB, turn)]
        + [whole((cols, D)), whole((D, joined))],
        (array(cols, rows), array(2 * cols, rows), array(2 * cols, rows), array(joined, rows)),
        (
            lanes(cols, QB, turn),
            lanes(2 * cols, QB, turn),
            lanes(2 * cols, QB, turn),
            lanes(joined, QB, turn),
        ),
        steps,
        [
            pltpu.VMEM((D, QB), BF),
            pltpu.VMEM((D, QB), F32),
            pltpu.VMEM((heads, rows, HD), BF),
            pltpu.VMEM((heads, rows, HD), BF),
            pltpu.VMEM((heads, HD, rows), BF),
            pltpu.VMEM((heads, HD, rows), F32),
            pltpu.VMEM((heads, HD, rows), F32),
        ],
        vmem=62,
    )


def column_maps(relative, row):
    def mine(i, s):
        return (row, spot(i ^ s[4]) if relative else i)

    def near(i, s):
        return (row, spot(i ^ s[4] ^ 1) if relative else i)

    return (mine, near)


def fold_columns_far(line, keep, got, relative):
    cols, rows = keep.shape[0] // 2, keep.shape[1]
    block = rows // 4
    mine, near = column_maps(relative, 1)
    return call(
        add_kernel,
        line,
        (keep, got),
        [lanes(cols, block, mine), lanes(cols, block, near)],
        array(cols, rows),
        lanes(cols, block),
        4,
    )


def out_kernel(info, keep, got, last, out):
    total = keep[...].astype(F32) + got[...].astype(F32) + last[...].astype(F32)
    live = live_lanes(info, pl.program_id(0) * out.shape[1], out.shape[1])
    out[...] = jnp.where(live, total, 0.0).astype(BF)


def out_rows(line, keep, got, last, home_rows):
    cols, rows = last.shape
    block = rows // 4
    mine, near = column_maps(True, 0)
    return call(
        out_kernel,
        line,
        (keep, got, last),
        [lanes(cols, block, mine), lanes(cols, block, near), lanes(cols, block)],
        array(cols, home_rows),
        lanes(cols, block),
        4,
    )


def first_sums_kernel(info, keep, got, last, x, stats, gain, other, total, both, sums):
    step = pl.program_id(0)
    cols, block = total.shape

    @pl.when(step == 0)
    def _():
        sums[...] = jnp.zeros_like(sums)

    live = live_lanes(info, step * block, block)
    grad = keep[...].astype(F32) + got[...].astype(F32) + last[...].astype(F32)
    grad = jnp.where(live, grad, 0.0)
    hat = (jnp.where(live, x[...].astype(F32), 0.0) - stats[0:1, :]) * stats[1:2, :]
    scaled = grad * gain[:, 0:1]
    total[...] = grad
    one = jnp.sum(scaled, axis=0, keepdims=True)
    two = jnp.sum(scaled * hat, axis=0, keepdims=True)
    both[:, pl.ds(pl.multiple_of(step * block, 128), block)] = jnp.concatenate([one, two] * 4, axis=0)
    mine = pl.ds(pl.multiple_of(info[4] * cols, 8), cols)
    sums[mine, 0:1] += jnp.sum(grad * hat, axis=1, keepdims=True)
    sums[mine, 1:2] += jnp.sum(grad, axis=1, keepdims=True)

    @pl.when(step == pl.num_programs(0) - 1)
    def _():
        start = both.shape[1] - D
        both[:, start:] = sums[...].T[:8] + other[...]


def first_sums(line, keep, got, last, x, stats, gain, other):
    cols, rows = last.shape
    block = rows // 4
    top = lanes(cols, block)
    return call(
        first_sums_kernel,
        line,
        (keep, got, last, x, stats, gain, other),
        [top, top, top, top, lanes(16, block), whole((cols, 2)), whole((8, D))],
        (array(cols, rows, dtype=F32), array(8, rows + D, dtype=F32)),
        (top, whole((8, rows + D))),
        4,
        [pltpu.VMEM((D, 128), F32)],
    )


def x_grad_kernel(info, total, rowsums, x, stats, gain, gown, out):
    live = live_lanes(info, pl.program_id(0) * out.shape[1], out.shape[1])
    inv_row = stats[1:2, :]
    hat = (jnp.where(live, x[...].astype(F32), 0.0) - stats[0:1, :]) * inv_row
    inner = total[...] * gain[:, 0:1] - rowsums[0:1, :] * (1.0 / D)
    inner = inner - hat * (rowsums[1:2, :] * (1.0 / D))
    grad = gown[...].astype(F32) + inv_row * inner
    out[...] = jnp.where(live, grad, 0.0).astype(BF)


def x_gradient(line, total, rowsums, x, stats, gain, gown, home_rows):
    cols, rows = total.shape
    block = rows // 4
    top = lanes(cols, block)
    return call(
        x_grad_kernel,
        line,
        (total, rowsums, x, stats, gain, gown),
        [top, lanes(8, block), top, lanes(16, block), whole((cols, 2)), top],
        array(cols, home_rows),
        top,
        4,
    )


def after(value, *before):
    return lax.optimization_barrier((value, *before))[0]


def gather_parts(value, before=()):
    far = swap(value, "tensor", 2)
    near = swap(value, "tensor", 1)
    return (value, near, far, swap(after(far, *before) if before else far, "tensor", 1))


def total_over(value, axis):
    mask = 1
    while mask < lax.axis_size(axis):
        value = value + swap(value, axis, mask)
        mask *= 2
    return value


def weight_kernel(jobs, orders, info, *refs):
    count = 2 * len(jobs)
    outs, total, refs = refs[-count - 1 : -1], refs[-1], refs[: -count - 1]
    for k, groups in enumerate(jobs):
        top = 0
        for pieces in groups:
            left, right = refs[:pieces], refs[pieces : 2 * pieces]
            refs = refs[2 * pieces :]
            rows = left[0].shape[0]
            value = dot(left[0][...], right[0][...], ((1,), (1,)))
            for m in range(1, pieces):
                value = value + dot(left[m][...], right[m][...], ((1,), (1,)))
            total[top : top + rows, :] = value
            top += rows
        mine, send = outs[2 * k : 2 * k + 2]
        half = mine.shape[0]
        bit = info[8 + orders[k][0] // 2]
        mine[...] = total[pl.ds(pl.multiple_of(bit * half, 8), half), :].astype(BF)
        send[...] = total[pl.ds(pl.multiple_of((1 - bit) * half, 8), half), :].astype(BF)


WSTEP = 256


def rows_of(item, place):
    return item.shape[1] if place is None else item.shape[1] // 4


def weight_gradients(line, jobs, orders, first=0, width=D):
    args, specs, shape = [], [], []
    skip = first // WSTEP
    for pairs in jobs:
        shape.append(tuple(len(left) for left, right in pairs))
        for left, right in pairs:
            for item, place in left:
                spec = (item.shape[0], rows_of(item, place))
                args.append(item)
                specs.append(
                    pl.BlockSpec(
                        spec, lambda i, s, k=place or 0: (0, k), pipeline_mode=pl.Buffered(1)
                    )
                )
            for item, place in right:
                args.append(item)
                specs.append(
                    pl.BlockSpec(
                        (WSTEP, rows_of(item, place)), lambda i, s, k=place or 0: (i + skip, k)
                    )
                )
    result = call(
        functools.partial(weight_kernel, tuple(shape), tuple(orders)),
        line,
        args,
        specs,
        (array(D // 2, width),) * (2 * len(jobs)),
        (lanes(D // 2, WSTEP),) * (2 * len(jobs)),
        -(-width // WSTEP),
        [pltpu.VMEM((D, WSTEP), F32)],
        vmem=62,
    )
    return [GroupSum(line, result[2 * k : 2 * k + 2], orders[k]) for k in range(len(jobs))]


def spread_kernel(info, *refs, orders, divided):
    step = pl.program_id(0)
    pieces = len(orders)
    parts, weight, outs = refs[: 4 * pieces], refs[4 * pieces], refs[4 * pieces + 1 :]
    left = 0
    for m, (first, second) in enumerate(orders):
        right = left + parts[4 * m].shape[1]
        place = ((step // 2) ^ info[8 + first // 2]) * 2 + ((step % 2) ^ info[8 + second // 2])
        for top, out in enumerate(outs):
            inside = (step >= 3 if top else step < 3) if divided else step >= 0
            for k in range(4):

                @pl.when((place == k) & inside)
                def _(out=out, part=parts[4 * m + k], left=left, right=right):
                    out[:, left:right] = part[...].astype(F32) * weight[0:1, 0:1]
        left = right


def spread_groups(line, sums, weight, divided=False):
    rows = sums[0].mine.shape[0]
    if divided:
        outs = (array(3 * rows, D, dtype=F32), array(rows, D, dtype=F32))
        specs = (
            pl.BlockSpec((rows, D), lambda i, s: (jnp.minimum(i, 2), 0)),
            pl.BlockSpec((rows, D), lambda i, s: (0, 0)),
        )
    else:
        outs = (array(4 * rows, D, dtype=F32),)
        specs = (pl.BlockSpec((rows, D), lambda i, s: (i, 0)),)
    parts = [item for one in sums for item in (one.mine, one.second, one.first, one.both)]
    return call(
        functools.partial(
            spread_kernel, orders=tuple(one.order for one in sums), divided=divided
        ),
        line,
        (*parts, weight),
        [whole(item.shape) for item in parts] + [whole((1, 1))],
        outs,
        specs,
        4,
    )


class GroupSum:
    def __init__(self, line, halves, order):
        self.line = line
        self.order = order
        self.mine, send = halves
        self.got = swap(send, "dp", order[0])

    def add(self, bit=None):
        def whole_or_half(value):
            if bit is None:
                return value.astype(F32)
            half = value.shape[0] // 2
            return lax.dynamic_slice_in_dim(value, bit * half, half).astype(F32)

        mine, got = self.line.tie(self.mine), self.got
        self.line.last = (whole_or_half(mine) + whole_or_half(got)).astype(BF)
        return self.line.last

    def quarter(self):
        bit = lax.axis_index("dp") // self.order[1] % 2
        send, self.mine = self.add(1 - bit), self.add(bit)
        self.got = swap(send, "dp", self.order[1])

    def meet(self):
        mask = 4
        self.mine = self.add()
        while mask < lax.axis_size("dp") // 2:
            self.got = swap(self.mine, "dp", mask)
            self.mine = self.add()
            mask *= 2
        self.got = swap(self.mine, "dp", mask)

    def close(self):
        self.mine = self.add()
        self.second = swap(self.mine, "dp", self.order[1])
        self.first = swap(self.mine, "dp", self.order[0])

    def relay(self, tie=False):
        second = self.line.tie(self.second) if tie else self.second
        self.both = swap(second, "dp", self.order[0])


def shards(
    x_home,
    cot_home,
    cell_len,
    norm1_gain,
    norm1_bias,
    qkv_weight,
    out_weight,
    norm2_gain,
    norm2_bias,
    up_weight,
    down_weight,
):
    groups = cell_len.shape[0]
    home_rows, cols = x_home.shape
    rows = -(-home_rows // 1024) * 1024
    me = lax.axis_index("tensor").astype(jnp.int32)
    group = lax.axis_index("dp")
    weight = groups / jnp.sum(cell_len).astype(F32)
    my_len = lax.dynamic_index_in_dim(cell_len, group, 0, keepdims=False)
    bounds = jnp.cumsum(my_len).astype(jnp.int32)
    group_bits = jnp.stack([group % 2, group // 2 % 2]).astype(jnp.int32)
    info = jnp.concatenate([bounds, jnp.broadcast_to(me, (4,)), group_bits])
    line = Line(info)

    x = x_home.T
    cot = cot_home.T
    own_affine = jnp.stack([norm1_gain, norm1_bias, norm2_gain, norm2_bias], axis=1)
    affine_parts = gather_parts(own_affine)
    wqkv_t = qkv_weight.transpose(1, 2, 0).reshape(3 * cols, D)
    wout_t = out_weight.T
    x_parts = gather_parts(x, (wout_t, affine_parts[3]))
    cot_far = swap(after(cot, x_parts[2]), "tensor", 2)

    normed, qkv, mixed, stats, keep, send, xmid, affine = front(
        line, x_parts, affine_parts, wqkv_t, wout_t, rows
    )
    got = swap(after(send, cot_far), "tensor", 1)
    far_sum = fold_far(line, keep, got)
    last = swap(far_sum, "tensor", 2)
    cot_parts = (cot, swap(line.tie(cot), "tensor", 1), cot_far, swap(line.tie(cot_far), "tensor", 1))
    g_rel = cotangent(line, cot_parts, rows)
    wup_t = line.other(lambda v: v.T, up_weight)
    wdown_t = line.other(lambda v: v.T, down_weight)
    middle, n_own, stats_two = second_norm(line, xmid, keep, got, last, affine)
    n_far, n_near = swap(n_own, "tensor", 2), swap(n_own, "tensor", 1)

    weights = (wup_t, up_weight, down_weight, wdown_t)
    hidden, gpre, pd_keep, pd_send, pn_own, pn_near = feed(
        line, True, n_own, n_near, g_rel, middle, weights
    )
    n_cross = swap(line.tie(n_far), "tensor", 1)
    got_own = swap(pn_near, "tensor", 1)
    hidden, gpre, pd_keep, pd_send, pn_far, pn_cross = feed(
        line, False, n_far, n_cross, g_rel, middle, weights, (hidden, gpre, pd_keep, pd_send)
    )
    got_far = swap(pn_cross, "tensor", 1)
    far_sum = call(
        add_kernel,
        line,
        (pn_far, got_far),
        [lanes(D, QB)] * 2,
        array(D, rows // 4),
        lanes(D, QB),
        rows // 4 // QB,
    )
    last = swap(far_sum, "tensor", 2)

    def entire(*values):
        return [(value, None) for value in values]

    def row_blocks(value):
        return [(value, k) for k in range(4)]

    n_parts = entire(n_own, n_far, n_near, n_cross)
    down, up = weight_gradients(
        line,
        [[(entire(hidden), entire(g_rel))], [(n_parts, row_blocks(gpre))]],
        [(1, 2), (2, 1)],
    )
    grad_mid, sums_two = back_norm(
        line, pn_own, got_own, last, middle, stats_two, g_rel, affine
    )
    g_far, g_near = swap(grad_mid, "tensor", 2), swap(grad_mid, "tensor", 1)
    pd_got = swap(pd_send, "tensor", 1)
    wqkv = line.other(lambda v: v.reshape(D, 3 * cols), qkv_weight)
    pd_sum = fold_columns_far(line, pd_keep, pd_got, True)
    pd_last = swap(after(pd_sum, g_far), "tensor", 2)
    down.quarter()
    up.quarter()
    g_cross = swap(line.tie(g_far), "tensor", 1)
    down.meet()
    up.meet()

    g_parts = (grad_mid, g_near, g_far, g_cross)
    gown, keep, send, joined = back(line, g_parts, qkv, stats, out_weight, wqkv)
    last_jobs = [
        (entire(joined), entire(normed)),
        (row_blocks(mixed), entire(grad_mid, g_far, g_near, g_cross)),
    ]
    (rest_one,) = weight_gradients(line, [last_jobs], [(1, 2)], 0, 2 * WSTEP)
    down.close()
    up.close()
    got = swap(line.tie(send), "tensor", 1)
    (rest_two,) = weight_gradients(line, [last_jobs], [(2, 1)], 2 * WSTEP, D - 2 * WSTEP)
    far_sum = fold_columns_far(line, keep, got, False)
    last = swap(far_sum, "tensor", 2)
    down.relay()
    rest_one.quarter()
    out = out_rows(line, pd_keep, pd_got, pd_last, home_rows)
    rest_two.quarter()
    up.relay()
    scale = weight.reshape(1, 1)
    (grad_down,) = spread_groups(line, [down], scale)
    rest_one.meet()
    total, both = first_sums(line, keep, got, last, x, stats, own_affine[:, :2], sums_two)
    rest_two.meet()
    both = both + swap(both, "tensor", 1)
    both = both + swap(both, "tensor", 2)
    (grad_up,) = spread_groups(line, [up], scale)
    rest_one.close()
    x_grad = x_gradient(line, total, both, x, stats, own_affine[:, :2], gown, home_rows)
    small = total_over(both[:, rows:], "dp")
    rest_two.close()
    rest_one.relay()
    rest_two.relay()
    small = lax.dynamic_slice_in_dim(small, me * cols, cols, axis=1) * weight
    grad_qkv, grad_out = spread_groups(line, [rest_one, rest_two], scale, True)

    return (
        out.T,
        x_grad.T,
        small[0],
        small[1],
        grad_qkv.reshape(3, cols, D).transpose(2, 0, 1),
        grad_out,
        small[2],
        small[3],
        grad_up,
        grad_down,
    )


def solution(mesh):
    rows, vector = P("dp", "tensor"), P("tensor")
    qkv, wide, tall = P(None, None, "tensor"), P(None, "tensor"), P("tensor", None)
    return jax.shard_map(
        shards,
        mesh=mesh,
        in_specs=(rows, rows, P(), vector, vector, qkv, tall, vector, vector, wide, tall),
        out_specs=(rows, rows, vector, vector, qkv, tall, vector, vector, wide, tall),
        check_vma=False,
    )
```

```python
import functools
import math

import jax
import jax.numpy as jnp
from jax import lax
from jax.experimental import pallas as pl
from jax.experimental.pallas import tpu as pltpu
from jax.sharding import PartitionSpec as P


D = 1120
HD = 56
EPS = 1e-05
BF = jnp.bfloat16
F32 = jnp.float32
QB = 256
TAIL = 512
SUB = 128
SCALE = HD ** (-0.5)
GELU_A = (2.0 / math.pi) ** 0.5
GELU_B = 0.044715
MIB = 1 << 20


def swap(value, axis, mask):
    size = lax.axis_size(axis)
    return lax.ppermute(value, axis, [(i, i ^ mask) for i in range(size)])


def dot(left, right, dims=((1,), (0,))):
    return lax.dot_general(left, right, (dims, ((), ())), preferred_element_type=F32)


def gelu_both(v):
    square = v * v
    gate = 0.5 * jnp.tanh(v * (GELU_A + GELU_A * GELU_B * square)) + 0.5
    slope = v * (2.0 * GELU_A + 6.0 * GELU_A * GELU_B * square)
    return (v * gate, gate + gate * (1.0 - gate) * slope)


def spot(rel):
    return (rel % 2) * 2 + rel // 2


def whole(shape):
    return pl.BlockSpec(shape, lambda i, *_: (0,) * len(shape), pipeline_mode=pl.Buffered(1))


def lanes(rows, width, where=None):
    return pl.BlockSpec((rows, width), (lambda i, s: (0, i)) if where is None else where)


class Line:
    def __init__(self, info):
        self.info = info
        self.last = None

    def start(self):
        if self.last is not None:
            self.info = after(self.info, self.last)
        return self.info

    def tie(self, value):
        return after(value, self.last)

    def other(self, function, value):
        self.last = function(self.tie(value))
        return self.last


def call(body, line, args, in_specs, outs, out_specs, steps, scratch=(), vmem=16, alias=None):
    result = pl.pallas_call(
        body,
        out_shape=outs,
        grid_spec=pltpu.PrefetchScalarGridSpec(
            num_scalar_prefetch=1,
            grid=(steps,),
            in_specs=in_specs,
            out_specs=out_specs,
            scratch_shapes=list(scratch),
        ),
        input_output_aliases=alias or {},
        compiler_params=pltpu.CompilerParams(
            dimension_semantics=("arbitrary",), vmem_limit_bytes=vmem * MIB
        ),
        cost_estimate=pl.CostEstimate(flops=1, bytes_accessed=1, transcendentals=0),
    )(line.start(), *args)
    line.last = result[-1] if isinstance(result, (tuple, list)) else result
    return result


def array(*shape, dtype=BF):
    return jax.ShapeDtypeStruct(shape, dtype)


def place_features(info, parts, scratch, live=None):
    count = parts[0].shape[0]
    for rel in range(4):
        value = parts[rel][...].astype(F32)
        if live is not None:
            value = jnp.where(live, value, 0.0)
        start = pl.multiple_of((info[4] ^ rel) * count, 8)
        scratch[pl.ds(start, count), :] = value


def split_features(info, wide, keep, send):
    count = keep.shape[0] // 2
    for rel in range(4):
        part = send if rel % 2 else keep
        start = pl.multiple_of((info[4] ^ rel) * count, 8)
        half = rel // 2 * count
        part[half : half + count, :] = wide[pl.ds(start, count), :].astype(BF)


def live_lanes(info, base, width):
    return base + lax.broadcasted_iota(jnp.int32, (1, width), 1) < info[3]


def first_of(rows, bounds):
    start = jnp.zeros_like(rows)
    for bound in bounds:
        start = jnp.where(rows >= bound, bound, start)
    return start


def each_window(bounds, base, shift, attend, skip):
    def part(index, carry):
        first = pl.multiple_of(base + index * SUB, SUB)
        here = pl.ds(pl.multiple_of(index * SUB, SUB), SUB)
        count = first // SUB - first_of(first, bounds) // SUB + 1

        @pl.when(first >= bounds[3])
        def _():
            skip(here)

        for blocks in range(1, TAIL // SUB + 2):

            @pl.when((count == blocks) & (first < bounds[3]))
            def _(blocks=blocks):
                width = blocks * SUB
                window = pl.ds(pl.multiple_of(first + shift + SUB - width, SUB), width)
                keys = first + SUB - width + lax.broadcasted_iota(jnp.int32, (width, SUB), 0)
                rows = first + lax.broadcasted_iota(jnp.int32, (1, SUB), 1)
                attend(here, window, (keys >= first_of(rows, bounds)) & (keys <= rows))

        return carry

    lax.fori_loop(0, QB // SUB, part, 0)


def norm_rows(values):
    mean_row = jnp.sum(values, axis=0, keepdims=True) * (1.0 / D)
    centered = values - mean_row
    var_row = jnp.sum(centered * centered, axis=0, keepdims=True) * (1.0 / D)
    inv_row = lax.rsqrt(var_row + EPS)
    return (centered * inv_row, mean_row, inv_row)


def front_kernel(heads, chunk, steps, info, *refs):
    own, near, far, cross, affine_own, affine_near, affine_far, affine_cross, wqkv, wout = refs[:10]
    normed, qkv, mixed, stats, keep, send, xmid, affine, wide, kbuf, vtbuf, proj = refs[-12:]
    step = pl.program_id(0)
    cols = heads * HD
    tail = TAIL if chunk else 0
    place = chunk * steps + step
    base = place * QB
    bounds = [info[k] for k in range(4)]
    here = pl.ds(pl.multiple_of(tail + step * QB, QB), QB)
    per = steps // 4
    rel = (step // per) ^ info[4]
    inner = step % per

    @pl.when(step == 0)
    def _():
        place_features(info, (affine_own, affine_near, affine_far, affine_cross), affine)
        if chunk:
            before = refs[10]
            for h in range(heads):
                keys = before[cols + HD * h : cols + HD * (h + 1), :]
                kbuf[h, :TAIL, :] = keys.T
                vtbuf[h, :, :TAIL] = before[2 * cols + HD * h : 2 * cols + HD * (h + 1), :]

    @pl.when(base >= bounds[3])
    def _():
        for ref in (normed, qkv, mixed, stats, proj, wide):
            ref[...] = jnp.zeros_like(ref)

    @pl.when(base < bounds[3])
    def _():
        place_features(info, (own, near, far, cross), wide, live_lanes(info, base, QB))
        hat, mean_row, inv_row = norm_rows(wide[...])
        stats[0:1, :] = mean_row
        stats[1:2, :] = inv_row
        normed[...] = (hat * affine[:, 0:1] + affine[:, 1:2]).astype(BF)
        joined = dot(wqkv[...], normed[...])
        qkv[...] = joined.astype(BF)
        for h in range(heads):
            keys = joined[cols + HD * h : cols + HD * (h + 1)]
            kbuf[h, here, :] = keys.T.astype(BF)
            vtbuf[h, :, here] = joined[2 * cols + HD * h : 2 * cols + HD * (h + 1)].astype(BF)

        def attend(lane, window, allowed):
            every = range(heads)
            scores = [dot(kbuf[h, window, :], qkv[HD * h : HD * (h + 1), lane]) for h in every]
            scores = [jnp.where(allowed, item * SCALE, -1e30) for item in scores]
            tops = [jnp.max(item, axis=0, keepdims=True) for item in scores]
            shifted = [jnp.exp(item - top) for item, top in zip(scores, tops)]
            totals = [jnp.sum(item, axis=0, keepdims=True) for item in shifted]
            weights = [(item * (1.0 / total)).astype(BF) for item, total in zip(shifted, totals)]
            pieces = [dot(vtbuf[h, :, window], weights[h]) for h in every]
            for h in every:
                stats[2 + h : 3 + h, lane] = tops[h] + jnp.log(totals[h])
            mixed[:, lane] = jnp.concatenate(pieces, axis=0).astype(BF)

        def skip(lane):
            mixed[:, lane] = jnp.zeros((cols, SUB), BF)

        each_window(bounds, base, tail - chunk * steps * QB, attend, skip)
        proj[...] = dot(wout[...], mixed[...]).astype(BF)

    target = pl.ds(pl.multiple_of((rel // 2) * (per * QB) + inner * QB, QB), QB)

    @pl.when(rel % 2 == 0)
    def _():
        keep[:, target] = proj[...]

    @pl.when(rel % 2 == 1)
    def _():
        send[:, target] = proj[...]

    @pl.when(rel == 0)
    def _():
        xmid[:, pl.ds(pl.multiple_of(inner * QB, QB), QB)] = wide[...].astype(BF)


def front(line, chunk, parts, affine, wqkv, wout, rows, count, before=()):
    joined, cols = wqkv.shape[0], wqkv.shape[0] // 3
    heads = cols // HD
    size = rows // count
    steps = size // QB
    last = size // TAIL - 1
    extra = [pl.BlockSpec((joined, TAIL), lambda i, s: (0, last), pipeline_mode=pl.Buffered(1))]
    extra.append(pl.BlockSpec(memory_space=pl.ANY))
    return call(
        functools.partial(front_kernel, heads, chunk, steps),
        line,
        (*parts, *affine, wqkv, wout, *before),
        [lanes(cols, QB)] * 4
        + [whole((cols, 4))] * 4
        + [whole((joined, D)), whole((D, cols))]
        + extra[: len(before)],
        (
            array(D, size),
            array(joined, size),
            array(cols, size),
            array(16, rows, dtype=F32),
            array(D, size // 2),
            array(D, size // 2),
            array(D, size // 4),
            array(D, 4, dtype=F32),
        ),
        (
            lanes(D, QB),
            lanes(joined, QB),
            lanes(cols, QB),
            lanes(16, QB, lambda i, s: (0, chunk * steps + i)),
            whole((D, size // 2)),
            whole((D, size // 2)),
            whole((D, size // 4)),
            whole((D, 4)),
        ),
        steps,
        [
            pltpu.VMEM((D, QB), F32),
            pltpu.VMEM((heads, TAIL + size, HD), BF),
            pltpu.VMEM((heads, HD, TAIL + size), BF),
            pltpu.VMEM((D, QB), BF),
        ],
        vmem=62,
        alias={12: 3} if before else None,
    )


def add_kernel(info, left, right, out):
    out[...] = (left[...].astype(F32) + right[...].astype(F32)).astype(BF)


def fold_far(line, keep, got):
    rows = keep.shape[1] // 2
    step = 256
    shift = rows // step
    spec = lanes(D, step, lambda i, s: (0, i + shift))
    return call(
        add_kernel,
        line,
        (keep, got),
        [spec, spec],
        array(D, rows),
        lanes(D, step),
        rows // step,
    )


def middle_kernel(info, xmid, keep, got, last, affine, middle, normed, stats):
    values = xmid[...].astype(F32) + keep[...].astype(F32)
    values = values + got[...].astype(F32) + last[...].astype(F32)
    middle[...] = values
    hat, mean_row, inv_row = norm_rows(values)
    normed[...] = (hat * affine[:, 2:3] + affine[:, 3:4]).astype(BF)
    stats[...] = jnp.concatenate([mean_row, inv_row] * 4, axis=0)


def second_norm(line, xmid, keep, got, last, affine):
    rows = xmid.shape[1]
    step = 128
    return call(
        middle_kernel,
        line,
        (xmid, keep, got, last, affine),
        [lanes(D, step)] * 4 + [whole((D, 4))],
        (array(D, rows, dtype=F32), array(D, rows), array(8, rows, dtype=F32)),
        (lanes(D, step), lanes(D, step), lanes(8, step)),
        rows // step,
    )


def turn_kernel(*refs):
    half = len(refs) // 2
    for value, out in zip(refs[:half], refs[half:]):
        out[...] = value[...].T


def turned(*values):
    specs, outs, out_specs = [], [], []
    for value in values:
        rows, cols = value.shape
        outs.append(array(cols, rows))
        if cols == D:
            specs.append(pl.BlockSpec((rows, WSTEP), lambda i: (0, i)))
            out_specs.append(pl.BlockSpec((WSTEP, rows), lambda i: (i, 0)))
        else:
            specs.append(pl.BlockSpec((WSTEP, cols), lambda i: (i, 0)))
            out_specs.append(pl.BlockSpec((cols, WSTEP), lambda i: (0, i)))
    return pl.pallas_call(
        turn_kernel,
        out_shape=tuple(outs),
        grid=(-(-D // WSTEP),),
        in_specs=specs,
        out_specs=tuple(out_specs),
        compiler_params=pltpu.CompilerParams(
            dimension_semantics=("arbitrary",), vmem_limit_bytes=62 * MIB
        ),
    )(*values)


def cotangent_kernel(first, per, info, own, near, far, cross, out, wide):
    step = pl.program_id(0)
    place = step // per
    rel = (place % 2) * 2 + place // 2
    base = first + ((info[4] ^ rel) * per + step % per) * QB
    place_features(info, (own, near, far, cross), wide, live_lanes(info, base, QB))
    out[...] = wide[...].astype(BF)


def cotangent(line, first, parts, size):
    steps = size // QB
    per = steps // 4

    def natural(i, s):
        return (0, (s[4] ^ spot(i // per)) * per + i % per)

    return call(
        functools.partial(cotangent_kernel, first, per),
        line,
        parts,
        [lanes(parts[0].shape[0], QB, natural)] * 4,
        array(D, size),
        lanes(D, QB),
        steps,
        [pltpu.VMEM((D, QB), F32)],
    )


def feed_kernel(blocks, info, *refs):
    count = len(blocks)
    normed, refs = refs[:count], refs[count:]
    cots, refs = refs[:count], refs[count:]
    owners = [k for k in range(count) if blocks[k][1] == 0]
    middles, refs = refs[: len(owners)], refs[len(owners) :]
    wup_t, wdown, wup, wdown_t = refs[:4]
    hidden, gpre, n_all, pd_keep, pd_send = refs[-9 - count : -4 - count]
    acts = refs[-4 - count : -4]
    now, cot, act, wide = refs[-4:]
    step = pl.program_id(0)
    size = now.shape[1]
    base = 0
    for k, (chunk, rel) in enumerate(blocks):
        base = jnp.where(step == k, (chunk * 4 + (info[4] ^ rel)) * size, base)

        @pl.when(step == k)
        def _(k=k):
            now[...] = normed[k][...]
            cot[...] = cots[k][...]

    n_all[...] = now[...]

    @pl.when(base >= info[3])
    def _():
        for ref in (hidden, gpre, act, pd_keep, pd_send):
            ref[...] = jnp.zeros_like(ref)

    @pl.when(base < info[3])
    def _():
        value, slope = gelu_both(dot(wup_t[...], now[...]))
        hidden[...] = value.astype(BF)
        gpre[...] = (dot(wdown[...], cot[...]) * slope).astype(BF)
        act[...] = dot(wup[...], gpre[...]).astype(BF)
        wide[...] = dot(wdown_t[...], hidden[...])
        for k, middle in zip(owners, middles):

            @pl.when(step == k)
            def _(middle=middle):
                wide[...] += middle[...]

        split_features(info, wide, pd_keep, pd_send)

    for k in range(count):

        @pl.when(step == k)
        def _(k=k):
            acts[k][...] = act[...]


def feed(line, blocks, normed, cots, middles, weights, rows, before=()):
    count = len(blocks)
    size = normed[0].shape[1]
    half = D // 2
    owners = [k for k in range(count) if blocks[k][1] == 0]

    def place(i, s):
        index = 0
        for k, (chunk, rel) in enumerate(blocks):
            index = jnp.where(i == k, chunk * 4 + spot(rel), index)
        return (0, index)

    def one(index):
        return pl.BlockSpec((D, size), lambda i, s: (0, index), pipeline_mode=pl.Buffered(1))

    args = (*normed, *[cots[c] for c, r in blocks], *[middles[blocks[k][0]] for k in owners])
    fixed = 1 + len(args) + 4
    return call(
        functools.partial(feed_kernel, tuple(blocks)),
        line,
        (*args, *weights, *before),
        [one(0)] * count
        + [one(spot(r)) for c, r in blocks]
        + [one(0)] * len(owners)
        + [whole((D, D))] * 4
        + [pl.BlockSpec(memory_space=pl.ANY)] * len(before),
        (array(D, rows),) * 3 + (array(half, rows),) * 2 + (array(D, size),) * count,
        (lanes(D, size, place),) * 3 + (lanes(half, size, place),) * 2 + (one(0),) * count,
        count,
        [
            pltpu.VMEM((D, size), BF),
            pltpu.VMEM((D, size), BF),
            pltpu.VMEM((D, size), BF),
            pltpu.VMEM((D, size), F32),
        ],
        vmem=62,
        alias={fixed + k: k for k in range(len(before))},
    )


def back_norm_kernel(info, keep, got, last, middle, stats, g_rel, affine, grad, turned, sums):
    @pl.when(pl.program_id(0) == 0)
    def _():
        sums[...] = jnp.zeros_like(sums)

    total = keep[...].astype(F32) + got[...].astype(F32) + last[...].astype(F32)
    inv_row = stats[1:2, :]
    hat = (middle[...] - stats[0:1, :]) * inv_row
    scaled = total * affine[:, 2:3]
    product = scaled * hat
    mean_one = jnp.sum(scaled, axis=0, keepdims=True) * (1.0 / D)
    mean_two = jnp.sum(product, axis=0, keepdims=True) * (1.0 / D)
    grad[...] = (
        g_rel[...].astype(F32) + inv_row * (scaled - mean_one - hat * mean_two)
    ).astype(BF)
    sums[:, 2:3] += jnp.sum(total * hat, axis=1, keepdims=True)
    sums[:, 3:4] += jnp.sum(total, axis=1, keepdims=True)

    @pl.when(pl.program_id(0) == pl.num_programs(0) - 1)
    def _():
        turned[...] = sums[...].T[:8]


def back_norm(line, keep, got, last, middle, stats, g_rel, affine):
    rows = middle.shape[1]
    step = 128
    return call(
        back_norm_kernel,
        line,
        (keep, got, last, middle, stats, g_rel, affine),
        [lanes(D, step)] * 4 + [lanes(8, step), lanes(D, step), whole((D, 4))],
        (array(D, rows), array(8, D, dtype=F32)),
        (lanes(D, step), whole((8, D))),
        rows // step,
        [pltpu.VMEM((D, 128), F32)],
    )


def back_kernel(heads, chunk, final, info, *refs):
    parts, qkv, stats, wout, wqkv = refs[:4], *refs[4:8]
    refs = refs[8:]
    if chunk:
        before, refs = refs[0], refs[1:]
    if not final:
        carry, refs = refs[:2], refs[2:]
    carry_out = refs[-16:-14] if chunk else ()
    gown, gm_all, keep, send, joined = refs[-14:-9]
    now, query_now, grad_now, wide, kbuf, vbuf, ktbuf, dkbuf, dvbuf = refs[-9:]
    per = pl.num_programs(0)
    step = per - 1 - pl.program_id(0)
    cols = heads * HD
    tail = TAIL if chunk else 0
    size = qkv.shape[1]
    place = chunk * per + step
    base = place * QB
    bounds = [info[k] for k in range(4)]
    here = pl.ds(pl.multiple_of(tail + step * QB, QB), QB)
    inner = parts[0].shape[1] // QB
    rel = (step // inner) ^ info[4]
    local = pl.ds(pl.multiple_of(step % inner * QB, QB), QB)

    def hold(source, start, width):
        for h in range(heads):
            keys = source[cols + HD * h : cols + HD * (h + 1), :]
            ktbuf[h, :, start : start + width] = keys
            kbuf[h, start : start + width, :] = keys.T
            vbuf[h, start : start + width, :] = source[
                2 * cols + HD * h : 2 * cols + HD * (h + 1), :
            ].T

    @pl.when(pl.program_id(0) == 0)
    def _():
        dkbuf[...] = jnp.zeros_like(dkbuf)
        dvbuf[...] = jnp.zeros_like(dvbuf)
        hold(qkv, tail, size)
        if chunk:
            hold(before, 0, TAIL)
        if not final:
            dkbuf[:, :, tail + size - TAIL : tail + size] = carry[0][...]
            dvbuf[:, :, tail + size - TAIL : tail + size] = carry[1][...]

    query_now[...] = qkv[:cols, pl.ds(pl.multiple_of(step * QB, QB), QB)]
    for r in range(4):

        @pl.when(rel == r)
        def _(r=r):
            now[...] = parts[r][:, local]

    gm_all[...] = now[...]
    wide[...] = now[...].astype(F32)
    gown[...] = wide[pl.ds(pl.multiple_of(info[4] * cols, 8), cols), :].astype(BF)

    @pl.when(base >= bounds[3])
    def _():
        for ref in (joined, keep, send):
            ref[...] = jnp.zeros_like(ref)

    @pl.when(base < bounds[3])
    def _():
        grad_now[...] = dot(wout[...], now[...]).astype(BF)

        def attend(lane, window, allowed):
            every = range(heads)
            parts = [slice(HD * h, HD * (h + 1)) for h in every]
            query = [query_now[part, lane] for part in parts]
            grads = [grad_now[part, lane] for part in parts]
            scores = [dot(kbuf[h, window, :], query[h]) * SCALE for h in every]
            grad_probs = [dot(vbuf[h, window, :], grads[h]) for h in every]
            probs = [
                jnp.exp(jnp.where(allowed, scores[h], -1e30) - stats[2 + h : 3 + h, lane])
                for h in every
            ]
            for h in every:
                dvbuf[h, :, window] += dot(grads[h], probs[h].astype(BF), ((1,), (1,)))
            deltas = [
                jnp.sum(probs[h] * grad_probs[h], axis=0, keepdims=True) for h in every
            ]
            grad_scores = [
                (probs[h] * (grad_probs[h] - deltas[h]) * SCALE).astype(BF) for h in every
            ]
            for h in every:
                dkbuf[h, :, window] += dot(query[h], grad_scores[h], ((1,), (1,)))
                wide[parts[h], lane] = dot(ktbuf[h, :, window], grad_scores[h])

        def skip(lane):
            wide[:cols, lane] = jnp.zeros((cols, SUB), F32)

        each_window(bounds, base, tail - chunk * per * QB, attend, skip)
        for h in range(heads):
            wide[cols + HD * h : cols + HD * (h + 1), :] = dkbuf[h, :, here]
            wide[2 * cols + HD * h : 2 * cols + HD * (h + 1), :] = dvbuf[h, :, here]
        joined[...] = wide[: 3 * cols, :].astype(BF)
        wide[...] = dot(wqkv[...], joined[...])
        split_features(info, wide, keep, send)

    if chunk:

        @pl.when(pl.program_id(0) == per - 1)
        def _():
            carry_out[0][...] = dkbuf[:, :, :TAIL]
            carry_out[1][...] = dvbuf[:, :, :TAIL]


def back(line, chunk, parts, qkvs, stats, wout, wqkv, made=None):
    joined, size = qkvs[0].shape
    rows = len(qkvs) * size
    cols = joined // 3
    heads = cols // HD
    steps = size // QB
    final = made is None
    carried = (heads, HD, TAIL)

    def turn(i, s):
        return (0, chunk * steps + steps - 1 - i)

    args = [*parts, qkvs[chunk], stats, wout, wqkv]
    specs = [whole((D, size // 4))] * 4 + [whole((joined, size)), lanes(16, QB, turn)]
    specs += [whole((cols, D)), whole((D, joined))]
    if chunk:
        last = size // TAIL - 1
        args.append(qkvs[chunk - 1])
        specs.append(
            pl.BlockSpec((joined, TAIL), lambda i, s: (0, last), pipeline_mode=pl.Buffered(1))
        )
    alias = None
    outs = [array(*carried, dtype=F32)] * 2 if chunk else []
    out_specs = [whole(carried)] * 2 if chunk else []
    if not final:
        args += made[:2]
        specs += [whole(carried)] * 2
        alias = {1 + len(args) + k: len(outs) + k for k in range(5)}
        args += made[2:]
        specs += [pl.BlockSpec(memory_space=pl.ANY)] * 5
    heights = (cols, D, 2 * cols, 2 * cols, joined)
    return call(
        functools.partial(back_kernel, heads, chunk, final),
        line,
        args,
        specs,
        (*outs, *[array(height, rows) for height in heights]),
        (*out_specs, *[lanes(height, QB, turn) for height in heights]),
        steps,
        [
            pltpu.VMEM((D, QB), BF),
            pltpu.VMEM((cols, QB), BF),
            pltpu.VMEM((cols, QB), BF),
            pltpu.VMEM((D, QB), F32),
            pltpu.VMEM((heads, TAIL + size, HD), BF),
            pltpu.VMEM((heads, TAIL + size, HD), BF),
            pltpu.VMEM((heads, HD, TAIL + size), BF),
            pltpu.VMEM((heads, HD, TAIL + size), F32),
            pltpu.VMEM((heads, HD, TAIL + size), F32),
        ],
        vmem=62,
        alias=alias,
    )


def row_order(info, value, mask):
    block = value.shape[1] // 4
    return [
        value[:, pl.ds(pl.multiple_of(spot(info[4] ^ mask ^ j) * block, 128), block)]
        for j in range(4)
    ]


def columns_kernel(info, keep, got, out):
    block = out.shape[1] // 4
    pairs = zip(row_order(info, keep, 0), row_order(info, got, 1))
    for j, (left, right) in enumerate(pairs):
        total = left.astype(F32) + right.astype(F32)
        out[:, j * block : (j + 1) * block] = total.astype(BF)


def fold_columns_far(line, keep, got, relative, size):
    cols, rows = keep.shape[0] // 2, keep.shape[1]
    low = lanes(cols, size, lambda i, s: (1, i))
    return call(
        columns_kernel if relative else add_kernel,
        line,
        (keep, got),
        [low, low],
        array(cols, rows),
        lanes(cols, size),
        rows // size,
    )


def out_kernel(info, keep, got, last, out):
    block = out.shape[1] // 4
    pairs = zip(row_order(info, keep, 0), row_order(info, got, 1))
    for j, (left, right) in enumerate(pairs):
        here = slice(j * block, (j + 1) * block)
        total = left.astype(F32) + right.astype(F32) + last[:, here].astype(F32)
        live = live_lanes(info, pl.program_id(0) * out.shape[1] + j * block, block)
        out[:, here] = jnp.where(live, total, 0.0).astype(BF)


def out_rows(line, keep, got, last, home_rows, size):
    cols, rows = last.shape
    top = lanes(cols, size)
    return call(
        out_kernel,
        line,
        (keep, got, last),
        [top, top, top],
        array(cols, home_rows),
        top,
        rows // size,
    )


def first_sums_kernel(info, keep, got, last, x, stats, gain, other, total, both, sums):
    step = pl.program_id(0)
    cols, block = total.shape

    @pl.when(step == 0)
    def _():
        sums[...] = jnp.zeros_like(sums)

    live = live_lanes(info, step * block, block)
    grad = keep[...].astype(F32) + got[...].astype(F32) + last[...].astype(F32)
    grad = jnp.where(live, grad, 0.0)
    hat = (jnp.where(live, x[...].astype(F32), 0.0) - stats[0:1, :]) * stats[1:2, :]
    scaled = grad * gain[:, 0:1]
    total[...] = grad
    one = jnp.sum(scaled, axis=0, keepdims=True)
    two = jnp.sum(scaled * hat, axis=0, keepdims=True)
    both[:, pl.ds(pl.multiple_of(step * block, 128), block)] = jnp.concatenate([one, two] * 4, axis=0)
    mine = pl.ds(pl.multiple_of(info[4] * cols, 8), cols)
    sums[mine, 0:1] += jnp.sum(grad * hat, axis=1, keepdims=True)
    sums[mine, 1:2] += jnp.sum(grad, axis=1, keepdims=True)

    @pl.when(step == pl.num_programs(0) - 1)
    def _():
        start = both.shape[1] - D
        both[:, start:] = sums[...].T[:8] + other[...]


def first_sums(line, keep, got, last, x, stats, gain, other):
    cols, rows = last.shape
    block = rows // 4
    top = lanes(cols, block)
    return call(
        first_sums_kernel,
        line,
        (keep, got, last, x, stats, gain, other),
        [top, top, top, top, lanes(16, block), whole((cols, 2)), whole((8, D))],
        (array(cols, rows, dtype=F32), array(8, rows + D, dtype=F32)),
        (top, whole((8, rows + D))),
        4,
        [pltpu.VMEM((D, 128), F32)],
    )


def x_grad_kernel(info, total, rowsums, x, stats, gain, gown, out):
    live = live_lanes(info, pl.program_id(0) * out.shape[1], out.shape[1])
    inv_row = stats[1:2, :]
    hat = (jnp.where(live, x[...].astype(F32), 0.0) - stats[0:1, :]) * inv_row
    inner = total[...] * gain[:, 0:1] - rowsums[0:1, :] * (1.0 / D)
    inner = inner - hat * (rowsums[1:2, :] * (1.0 / D))
    grad = gown[...].astype(F32) + inv_row * inner
    out[...] = jnp.where(live, grad, 0.0).astype(BF)


def x_gradient(line, total, rowsums, x, stats, gain, gown, home_rows):
    cols, rows = total.shape
    block = rows // 4
    top = lanes(cols, block)
    return call(
        x_grad_kernel,
        line,
        (total, rowsums, x, stats, gain, gown),
        [top, lanes(8, block), top, lanes(16, block), whole((cols, 2)), top],
        array(cols, home_rows),
        top,
        4,
    )


def after(value, *before):
    return lax.optimization_barrier((value, *before))[0]


def gather_parts(value, before=()):
    far = swap(value, "tensor", 2)
    near = swap(value, "tensor", 1)
    return (value, near, far, swap(after(far, *before) if before else far, "tensor", 1))


def total_over(value, axis):
    mask = 1
    while mask < lax.axis_size(axis):
        value = value + swap(value, axis, mask)
        mask *= 2
    return value


def weight_kernel(jobs, orders, info, *refs):
    count = 2 * len(jobs)
    outs, total, refs = refs[-count - 1 : -1], refs[-1], refs[: -count - 1]
    for k, groups in enumerate(jobs):
        top = 0
        for pieces in groups:
            left, right = refs[:pieces], refs[pieces : 2 * pieces]
            refs = refs[2 * pieces :]
            rows = left[0].shape[0]
            value = dot(left[0][...], right[0][...], ((1,), (1,)))
            for m in range(1, pieces):
                value = value + dot(left[m][...], right[m][...], ((1,), (1,)))
            total[top : top + rows, :] = value
            top += rows
        mine, send = outs[2 * k : 2 * k + 2]
        half = mine.shape[0]
        bit = info[8 + orders[k][0] // 2]
        mine[...] = total[pl.ds(pl.multiple_of(bit * half, 8), half), :].astype(BF)
        send[...] = total[pl.ds(pl.multiple_of((1 - bit) * half, 8), half), :].astype(BF)


WSTEP = 256


def weight_gradients(line, jobs, orders, first=0, width=D, before=()):
    args, specs, shape = [], [], []
    skip = first // WSTEP
    for pairs in jobs:
        shape.append(tuple(len(left) for left, right in pairs))
        for left, right in pairs:
            for item, k, parts in left:
                args.append(item)
                specs.append(
                    pl.BlockSpec(
                        (item.shape[0], item.shape[1] // parts),
                        lambda i, s, k=k: (0, k),
                        pipeline_mode=pl.Buffered(1),
                    )
                )
            for item, k, parts in right:
                args.append(item)
                specs.append(
                    pl.BlockSpec(
                        (WSTEP, item.shape[1] // parts), lambda i, s, k=k: (i + skip, k)
                    )
                )
    result = call(
        functools.partial(weight_kernel, tuple(shape), tuple(orders)),
        line,
        args,
        specs,
        (array(D // 2, width),) * (2 * len(jobs)),
        (lanes(D // 2, WSTEP),) * (2 * len(jobs)),
        -(-width // WSTEP),
        [pltpu.VMEM((D, WSTEP), F32)],
        vmem=62,
    )
    return [
        GroupSum(line, result[2 * k], after(result[2 * k + 1], *before), orders[k])
        for k in range(len(jobs))
    ]


def spread_kernel(info, *refs, orders, divided):
    step = pl.program_id(0)
    pieces = len(orders)
    parts, weight, outs = refs[: 4 * pieces], refs[4 * pieces], refs[4 * pieces + 1 :]
    left = 0
    for m, (first, second) in enumerate(orders):
        right = left + parts[4 * m].shape[1]
        place = ((step // 2) ^ info[8 + first // 2]) * 2 + ((step % 2) ^ info[8 + second // 2])
        for top, out in enumerate(outs):
            inside = (step >= 3 if top else step < 3) if divided else step >= 0
            for k in range(4):

                @pl.when((place == k) & inside)
                def _(out=out, part=parts[4 * m + k], left=left, right=right):
                    out[:, left:right] = part[...].astype(F32) * weight[0:1, 0:1]
        left = right


def spread_groups(line, sums, weight, divided=False):
    rows = sums[0].mine.shape[0]
    if divided:
        outs = (array(3 * rows, D, dtype=F32), array(rows, D, dtype=F32))
        specs = (
            pl.BlockSpec((rows, D), lambda i, s: (jnp.minimum(i, 2), 0)),
            pl.BlockSpec((rows, D), lambda i, s: (0, 0)),
        )
    else:
        outs = (array(4 * rows, D, dtype=F32),)
        specs = (pl.BlockSpec((rows, D), lambda i, s: (i, 0)),)
    parts = [item for one in sums for item in (one.mine, one.second, one.first, one.both)]
    return call(
        functools.partial(
            spread_kernel, orders=tuple(one.order for one in sums), divided=divided
        ),
        line,
        (*parts, weight),
        [whole(item.shape) for item in parts] + [whole((1, 1))],
        outs,
        specs,
        4,
    )


class GroupSum:
    def __init__(self, line, mine, send, order):
        self.line = line
        self.order = order
        self.mine = mine
        self.got = swap(send, "dp", order[0])

    def add(self, bit=None):
        def whole_or_half(value):
            if bit is None:
                return value.astype(F32)
            half = value.shape[0] // 2
            return lax.dynamic_slice_in_dim(value, bit * half, half).astype(F32)

        mine, got = self.line.tie(self.mine), self.got
        self.line.last = (whole_or_half(mine) + whole_or_half(got)).astype(BF)
        return self.line.last

    def quarter(self):
        bit = lax.axis_index("dp") // self.order[1] % 2
        send, self.mine = self.add(1 - bit), self.add(bit)
        self.got = swap(send, "dp", self.order[1])

    def meet(self):
        mask = 4
        self.mine = self.add()
        while mask < lax.axis_size("dp") // 2:
            self.got = swap(self.mine, "dp", mask)
            self.mine = self.add()
            mask *= 2
        self.got = swap(self.mine, "dp", mask)

    def close(self):
        self.mine = self.add()
        self.second = swap(self.mine, "dp", self.order[1])
        self.first = swap(self.mine, "dp", self.order[0])

    def relay(self, tie=False):
        second = self.line.tie(self.second) if tie else self.second
        self.both = swap(second, "dp", self.order[0])


def shards(
    x_home,
    cot_home,
    cell_len,
    norm1_gain,
    norm1_bias,
    qkv_weight,
    out_weight,
    norm2_gain,
    norm2_bias,
    up_weight,
    down_weight,
):
    groups = cell_len.shape[0]
    home_rows, cols = x_home.shape
    rows = -(-home_rows // 1024) * 1024
    me = lax.axis_index("tensor").astype(jnp.int32)
    group = lax.axis_index("dp")
    weight = groups / jnp.sum(cell_len).astype(F32)
    my_len = lax.dynamic_index_in_dim(cell_len, group, 0, keepdims=False)
    bounds = jnp.cumsum(my_len).astype(jnp.int32)
    group_bits = jnp.stack([group % 2, group // 2 % 2]).astype(jnp.int32)
    info = jnp.concatenate([bounds, jnp.broadcast_to(me, (4,)), group_bits])
    line = Line(info)

    chunks = 2
    size = rows // chunks
    block = size // 4
    x = x_home.T
    x_cuts = [x[:, :size], x[:, size:]]
    cot = cot_home.T
    cot_cuts = [cot[:, :size], cot[:, size:]]
    own_affine = jnp.stack([norm1_gain, norm1_bias, norm2_gain, norm2_bias], axis=1)
    wqkv_t = qkv_weight.transpose(1, 2, 0).reshape(3 * cols, D)
    wout_t, wup_t, wdown_t, wqkv = turned(out_weight, up_weight, down_weight, wqkv_t)
    affine_parts = gather_parts(own_affine, (wout_t, x_cuts[1], *cot_cuts))
    x_zero = gather_parts(x_cuts[0], (affine_parts[3],))
    x_next = after(x_cuts[1], affine_parts[1])
    x_next_far, x_next_near = swap(x_next, "tensor", 2), swap(x_next, "tensor", 1)
    cot_far = [swap(after(cot_cuts[0], x_zero[2]), "tensor", 2)]

    def cot_parts(c):
        value, far = cot_cuts[c], cot_far[c]
        return (value, swap(line.tie(value), "tensor", 1), far, swap(line.tie(far), "tensor", 1))

    normed, qkv, mixed, stats, keep, send, xmid, affine = front(
        line, 0, x_zero, affine_parts, wqkv_t, wout_t, rows, chunks
    )
    normed, qkv, mixed, xmid = [normed], [qkv], [mixed], [xmid]
    folds = []
    got = swap(after(send, cot_far[0], x_next_far, x_next_near), "tensor", 1)
    x_next_cross = swap(line.tie(x_next_far), "tensor", 1)
    far_sum = fold_far(line, keep, got)
    folds.append((keep, got, swap(far_sum, "tensor", 2)))
    cot_far.append(swap(after(cot_cuts[1], far_sum), "tensor", 2))
    cots = [cot_parts(0)]
    results = front(
        line,
        1,
        (x_next, x_next_near, x_next_far, x_next_cross),
        affine_parts,
        wqkv_t,
        wout_t,
        rows,
        chunks,
        (qkv[0], stats),
    )
    normed.append(results[0])
    qkv.append(results[1])
    mixed.append(results[2])
    stats, keep, send = results[3:6]
    xmid.append(results[6])
    middle, stats_two, n_parts = [], [], []

    def norm_chunk(c):
        values, n_own, stat = second_norm(line, xmid[c], *folds[c], affine)
        middle.append(values)
        stats_two.append(stat)
        n_parts.append([n_own, swap(n_own, "tensor", 1), swap(n_own, "tensor", 2), None])

    got = swap(after(send, cot_far[1], folds[0][2]), "tensor", 1)
    norm_chunk(0)
    far_sum = fold_far(line, keep, got)
    folds.append((keep, got, swap(far_sum, "tensor", 2)))
    g_rel = [cotangent(line, 0, cots[0], size)]
    cots.append(cot_parts(1))
    g_rel.append(cotangent(line, size, cots[1], size))
    norm_chunk(1)

    weights = (wup_t, down_weight, up_weight, wdown_t)

    def feed_blocks(blocks, before=()):
        picked = [n_parts[c][r] for c, r in blocks]
        made = feed(line, blocks, picked, g_rel, middle, weights, rows, before)
        return made[:5], made[5:]

    state, (pn_own, pn_near) = feed_blocks([(0, 0), (0, 1)])
    n_parts[0][3] = swap(line.tie(n_parts[0][2]), "tensor", 1)
    own_sums = [(pn_own, swap(pn_near, "tensor", 1))]
    state, (pn_far, pn_cross, pn_own, pn_near) = feed_blocks(
        [(0, 2), (0, 3), (1, 0), (1, 1)], state
    )
    n_parts[1][3] = swap(line.tie(n_parts[1][2]), "tensor", 1)
    own_sums.append((pn_own, swap(after(pn_near, n_parts[1][2]), "tensor", 1)))

    def send_far(pn_far, pn_cross, *before):
        far_sum = call(
            add_kernel,
            line,
            (pn_far, swap(after(pn_cross, *before), "tensor", 1)),
            [lanes(D, block)] * 2,
            array(D, block),
            lanes(D, block),
            1,
        )
        return swap(far_sum, "tensor", 2)

    last = [send_far(pn_far, pn_cross, n_parts[1][2])]
    state, (pn_far, pn_cross) = feed_blocks([(1, 2), (1, 3)], state)
    hidden, gpre, n_all, pd_keep, pd_send = state
    last.append(send_far(pn_far, pn_cross, last[0]))
    g_parts = []

    def back_chunk(c):
        grad_mid, sums = back_norm(
            line, *own_sums[c], last[c], middle[c], stats_two[c], g_rel[c], affine
        )
        near, far = swap(grad_mid, "tensor", 1), swap(grad_mid, "tensor", 2)
        g_parts.append([grad_mid, near, far, None])
        return sums

    sums_two = back_chunk(0)
    pairs = [[(item, c, chunks) for c in range(chunks)] for item in (hidden, gpre, n_all)]
    g_pieces = [(item, 0, 1) for item in g_rel]
    down, up = weight_gradients(
        line, [[(pairs[0], g_pieces)], [([(n_all, 0, 1)], [(gpre, 0, 1)])]], [(1, 2), (2, 1)], before=(last[1],)
    )
    sums_two = sums_two + back_chunk(1)
    pd_got = swap(pd_send, "tensor", 1)
    pd_sum = fold_columns_far(line, pd_keep, pd_got, True, size)
    g_parts[1][3] = swap(line.tie(g_parts[1][2]), "tensor", 1)
    g_parts[0][3] = swap(line.tie(g_parts[0][2]), "tensor", 1)
    down.quarter()
    up.quarter()

    made = back(line, 1, g_parts[1], qkv, stats, out_weight, wqkv)
    down.meet()
    up.meet()
    pd_last = swap(line.tie(pd_sum), "tensor", 2)
    gown, gm_all, keep, send, joined = back(
        line, 0, g_parts[0], qkv, stats, out_weight, wqkv, made
    )
    last_jobs = [
        ([(joined, c, chunks) for c in range(chunks)], [(item, 0, 1) for item in normed]),
        ([(item, 0, 1) for item in mixed], [(gm_all, c, chunks) for c in range(chunks)]),
    ]
    (rest_one,) = weight_gradients(
        line, [last_jobs], [(1, 2)], 0, 2 * WSTEP, before=(down.got,)
    )
    down.close()
    got = swap(line.tie(send), "tensor", 1)
    (rest_two,) = weight_gradients(line, [last_jobs], [(2, 1)], 2 * WSTEP, D - 2 * WSTEP)
    far_sum = fold_columns_far(line, keep, got, False, size)
    last = swap(far_sum, "tensor", 2)
    out = out_rows(line, pd_keep, pd_got, pd_last, home_rows, size)
    rest_one.quarter()
    up.close()
    rest_two.quarter()
    total, both = first_sums(line, keep, got, last, x, stats, own_affine[:, :2], sums_two)
    rest_one.meet()
    down.relay()
    rest_two.meet()
    scale = weight.reshape(1, 1)
    (grad_down,) = spread_groups(line, [down], scale)
    both = both + swap(both, "tensor", 1)
    up.relay()
    both = both + swap(both, "tensor", 2)
    rest_one.close()
    x_grad = x_gradient(line, total, both, x, stats, own_affine[:, :2], gown, home_rows)
    rest_two.close()
    (grad_up,) = spread_groups(line, [up], scale)
    rest_one.relay()
    rest_two.relay()
    small = after(both[:, rows:], rest_one.second, rest_two.second)
    mask = groups // 2
    pair = (small, swap(small, "dp", mask))
    grad_qkv, grad_out = spread_groups(line, [rest_one, rest_two], scale, True)
    while pair:
        small = line.other(lambda v: v[0] + v[1], pair)
        mask //= 2
        pair = (small, swap(small, "dp", mask)) if mask else None
    small = lax.dynamic_slice_in_dim(small, me * cols, cols, axis=1) * weight

    return (
        out.T,
        x_grad.T,
        small[0],
        small[1],
        grad_qkv.reshape(3, cols, D).transpose(2, 0, 1),
        grad_out,
        small[2],
        small[3],
        grad_up,
        grad_down,
    )


def solution(mesh):
    rows, vector = P("dp", "tensor"), P("tensor")
    qkv, wide, tall = P(None, None, "tensor"), P(None, "tensor"), P("tensor", None)
    return jax.shard_map(
        shards,
        mesh=mesh,
        in_specs=(rows, rows, P(), vector, vector, qkv, tall, vector, vector, wide, tall),
        out_specs=(rows, rows, vector, vector, qkv, tall, vector, vector, wide, tall),
        check_vma=False,
    )
```

```python
import functools
import math

import jax
import jax.numpy as jnp
from jax import lax
from jax.experimental import pallas as pl
from jax.experimental.pallas import tpu as pltpu
from jax.sharding import PartitionSpec as P


D = 1120
HD = 56
EPS = 1e-05
BF = jnp.bfloat16
F32 = jnp.float32
QB = 256
TAIL = 512
SUB = 128
SCALE = HD ** (-0.5)
GELU_A = (2.0 / math.pi) ** 0.5
GELU_B = 0.044715
MIB = 1 << 20


def swap(value, axis, mask):
    size = lax.axis_size(axis)
    return lax.ppermute(value, axis, [(i, i ^ mask) for i in range(size)])


def dot(left, right, dims=((1,), (0,))):
    return lax.dot_general(left, right, (dims, ((), ())), preferred_element_type=F32)


def gelu_both(v):
    square = v * v
    gate = 0.5 * jnp.tanh(v * (GELU_A + GELU_A * GELU_B * square)) + 0.5
    slope = v * (2.0 * GELU_A + 6.0 * GELU_A * GELU_B * square)
    return (v * gate, gate + gate * (1.0 - gate) * slope)


def spot(rel):
    return (rel % 2) * 2 + rel // 2


def whole(shape):
    return pl.BlockSpec(shape, lambda i, *_: (0,) * len(shape), pipeline_mode=pl.Buffered(1))


def lanes(rows, width, where=None):
    return pl.BlockSpec((rows, width), (lambda i, s: (0, i)) if where is None else where)


class Line:
    def __init__(self, info):
        self.info = info
        self.last = None

    def start(self):
        if self.last is not None:
            self.info = after(self.info, self.last)
        return self.info

    def tie(self, value):
        return after(value, self.last)

    def other(self, function, value):
        self.last = function(self.tie(value))
        return self.last


def call(body, line, args, in_specs, outs, out_specs, steps, scratch=(), vmem=16, alias=None):
    result = pl.pallas_call(
        body,
        out_shape=outs,
        grid_spec=pltpu.PrefetchScalarGridSpec(
            num_scalar_prefetch=1,
            grid=(steps,),
            in_specs=in_specs,
            out_specs=out_specs,
            scratch_shapes=list(scratch),
        ),
        input_output_aliases=alias or {},
        compiler_params=pltpu.CompilerParams(
            dimension_semantics=("arbitrary",), vmem_limit_bytes=vmem * MIB
        ),
        cost_estimate=pl.CostEstimate(flops=1, bytes_accessed=1, transcendentals=0),
    )(line.start(), *args)
    line.last = result[-1] if isinstance(result, (tuple, list)) else result
    return result


def array(*shape, dtype=BF):
    return jax.ShapeDtypeStruct(shape, dtype)


def place_features(info, parts, scratch, live=None):
    count = parts[0].shape[0]
    for rel in range(4):
        value = parts[rel][...].astype(F32)
        if live is not None:
            value = jnp.where(live, value, 0.0)
        start = pl.multiple_of((info[4] ^ rel) * count, 8)
        scratch[pl.ds(start, count), :] = value


def split_features(info, wide, keep, send):
    count = keep.shape[0] // 2
    for rel in range(4):
        part = send if rel % 2 else keep
        start = pl.multiple_of((info[4] ^ rel) * count, 8)
        half = rel // 2 * count
        part[half : half + count, :] = wide[pl.ds(start, count), :].astype(BF)


def live_lanes(info, base, width):
    return base + lax.broadcasted_iota(jnp.int32, (1, width), 1) < info[3]


def first_of(rows, bounds):
    start = jnp.zeros_like(rows)
    for bound in bounds:
        start = jnp.where(rows >= bound, bound, start)
    return start


def each_window(bounds, base, shift, attend, skip):
    def part(index, carry):
        first = pl.multiple_of(base + index * SUB, SUB)
        here = pl.ds(pl.multiple_of(index * SUB, SUB), SUB)
        count = first // SUB - first_of(first, bounds) // SUB + 1

        @pl.when(first >= bounds[3])
        def _():
            skip(here)

        for blocks in range(1, TAIL // SUB + 2):

            @pl.when((count == blocks) & (first < bounds[3]))
            def _(blocks=blocks):
                width = blocks * SUB
                window = pl.ds(pl.multiple_of(first + shift + SUB - width, SUB), width)
                keys = first + SUB - width + lax.broadcasted_iota(jnp.int32, (width, SUB), 0)
                rows = first + lax.broadcasted_iota(jnp.int32, (1, SUB), 1)
                attend(here, window, (keys >= first_of(rows, bounds)) & (keys <= rows))

        return carry

    lax.fori_loop(0, QB // SUB, part, 0)


def norm_rows(values):
    mean_row = jnp.sum(values, axis=0, keepdims=True) * (1.0 / D)
    centered = values - mean_row
    var_row = jnp.sum(centered * centered, axis=0, keepdims=True) * (1.0 / D)
    inv_row = lax.rsqrt(var_row + EPS)
    return (centered * inv_row, mean_row, inv_row)


def front_kernel(heads, chunk, steps, info, *refs):
    own, near, far, cross, affine_own, affine_near, affine_far, affine_cross, wqkv, wout = refs[:10]
    normed, qkv, mixed, stats, keep, send, xmid, affine, wide, kbuf, vtbuf, proj = refs[-12:]
    step = pl.program_id(0)
    cols = heads * HD
    tail = TAIL if chunk else 0
    place = chunk * steps + step
    base = place * QB
    bounds = [info[k] for k in range(4)]
    here = pl.ds(pl.multiple_of(tail + step * QB, QB), QB)
    per = steps // 4
    rel = (step // per) ^ info[4]
    inner = step % per

    @pl.when(step == 0)
    def _():
        place_features(info, (affine_own, affine_near, affine_far, affine_cross), affine)
        if chunk:
            before = refs[10]
            for h in range(heads):
                keys = before[cols + HD * h : cols + HD * (h + 1), :]
                kbuf[h, :TAIL, :] = keys.T
                vtbuf[h, :, :TAIL] = before[2 * cols + HD * h : 2 * cols + HD * (h + 1), :]

    @pl.when(base >= bounds[3])
    def _():
        for ref in (normed, qkv, mixed, stats, proj, wide):
            ref[...] = jnp.zeros_like(ref)

    @pl.when(base < bounds[3])
    def _():
        place_features(info, (own, near, far, cross), wide, live_lanes(info, base, QB))
        hat, mean_row, inv_row = norm_rows(wide[...])
        stats[0:1, :] = mean_row
        stats[1:2, :] = inv_row
        normed[...] = (hat * affine[:, 0:1] + affine[:, 1:2]).astype(BF)
        joined = dot(wqkv[...], normed[...])
        qkv[...] = joined.astype(BF)
        for h in range(heads):
            keys = joined[cols + HD * h : cols + HD * (h + 1)]
            kbuf[h, here, :] = keys.T.astype(BF)
            vtbuf[h, :, here] = joined[2 * cols + HD * h : 2 * cols + HD * (h + 1)].astype(BF)

        def attend(lane, window, allowed):
            every = range(heads)
            scores = [dot(kbuf[h, window, :], qkv[HD * h : HD * (h + 1), lane]) for h in every]
            scores = [jnp.where(allowed, item * SCALE, -1e30) for item in scores]
            tops = [jnp.max(item, axis=0, keepdims=True) for item in scores]
            shifted = [jnp.exp(item - top) for item, top in zip(scores, tops)]
            totals = [jnp.sum(item, axis=0, keepdims=True) for item in shifted]
            weights = [(item * (1.0 / total)).astype(BF) for item, total in zip(shifted, totals)]
            pieces = [dot(vtbuf[h, :, window], weights[h]) for h in every]
            for h in every:
                stats[2 + h : 3 + h, lane] = tops[h] + jnp.log(totals[h])
            mixed[:, lane] = jnp.concatenate(pieces, axis=0).astype(BF)

        def skip(lane):
            mixed[:, lane] = jnp.zeros((cols, SUB), BF)

        each_window(bounds, base, tail - chunk * steps * QB, attend, skip)
        proj[...] = dot(wout[...], mixed[...]).astype(BF)

    target = pl.ds(pl.multiple_of((rel // 2) * (per * QB) + inner * QB, QB), QB)

    @pl.when(rel % 2 == 0)
    def _():
        keep[:, target] = proj[...]

    @pl.when(rel % 2 == 1)
    def _():
        send[:, target] = proj[...]

    @pl.when(rel == 0)
    def _():
        xmid[:, pl.ds(pl.multiple_of(inner * QB, QB), QB)] = wide[...].astype(BF)


def front(line, chunk, parts, affine, wqkv, wout, rows, count, before=()):
    joined, cols = wqkv.shape[0], wqkv.shape[0] // 3
    heads = cols // HD
    size = rows // count
    steps = size // QB
    last = size // TAIL - 1
    extra = [pl.BlockSpec((joined, TAIL), lambda i, s: (0, last), pipeline_mode=pl.Buffered(1))]
    extra.append(pl.BlockSpec(memory_space=pl.ANY))
    return call(
        functools.partial(front_kernel, heads, chunk, steps),
        line,
        (*parts, *affine, wqkv, wout, *before),
        [lanes(cols, QB)] * 4
        + [whole((cols, 4))] * 4
        + [whole((joined, D)), whole((D, cols))]
        + extra[: len(before)],
        (
            array(D, size),
            array(joined, size),
            array(cols, size),
            array(16, rows, dtype=F32),
            array(D, size // 2),
            array(D, size // 2),
            array(D, size // 4),
            array(D, 4, dtype=F32),
        ),
        (
            lanes(D, QB),
            lanes(joined, QB),
            lanes(cols, QB),
            lanes(16, QB, lambda i, s: (0, chunk * steps + i)),
            whole((D, size // 2)),
            whole((D, size // 2)),
            whole((D, size // 4)),
            whole((D, 4)),
        ),
        steps,
        [
            pltpu.VMEM((D, QB), F32),
            pltpu.VMEM((heads, TAIL + size, HD), BF),
            pltpu.VMEM((heads, HD, TAIL + size), BF),
            pltpu.VMEM((D, QB), BF),
        ],
        vmem=62,
        alias={12: 3} if before else None,
    )


def add_kernel(info, left, right, out):
    out[...] = (left[...].astype(F32) + right[...].astype(F32)).astype(BF)


def fold_far(line, keep, got):
    rows = keep.shape[1] // 2
    step = 256
    shift = rows // step
    spec = lanes(D, step, lambda i, s: (0, i + shift))
    return call(
        add_kernel,
        line,
        (keep, got),
        [spec, spec],
        array(D, rows),
        lanes(D, step),
        rows // step,
    )


def middle_kernel(info, xmid, keep, got, last, affine, middle, normed, stats):
    values = xmid[...].astype(F32) + keep[...].astype(F32)
    values = values + got[...].astype(F32) + last[...].astype(F32)
    middle[...] = values
    hat, mean_row, inv_row = norm_rows(values)
    normed[...] = (hat * affine[:, 2:3] + affine[:, 3:4]).astype(BF)
    stats[...] = jnp.concatenate([mean_row, inv_row] * 4, axis=0)


def second_norm(line, xmid, keep, got, last, affine):
    rows = xmid.shape[1]
    step = 128
    return call(
        middle_kernel,
        line,
        (xmid, keep, got, last, affine),
        [lanes(D, step)] * 4 + [whole((D, 4))],
        (array(D, rows, dtype=F32), array(D, rows), array(8, rows, dtype=F32)),
        (lanes(D, step), lanes(D, step), lanes(8, step)),
        rows // step,
    )


def turn_kernel(*refs):
    half = len(refs) // 2
    for value, out in zip(refs[:half], refs[half:]):
        out[...] = value[...].T


def turned(*values):
    specs, outs, out_specs = [], [], []
    for value in values:
        rows, cols = value.shape
        outs.append(array(cols, rows))
        if cols == D:
            specs.append(pl.BlockSpec((rows, WSTEP), lambda i: (0, i)))
            out_specs.append(pl.BlockSpec((WSTEP, rows), lambda i: (i, 0)))
        else:
            specs.append(pl.BlockSpec((WSTEP, cols), lambda i: (i, 0)))
            out_specs.append(pl.BlockSpec((cols, WSTEP), lambda i: (0, i)))
    return pl.pallas_call(
        turn_kernel,
        out_shape=tuple(outs),
        grid=(-(-D // WSTEP),),
        in_specs=specs,
        out_specs=tuple(out_specs),
        compiler_params=pltpu.CompilerParams(
            dimension_semantics=("arbitrary",), vmem_limit_bytes=62 * MIB
        ),
    )(*values)


def cotangent_kernel(first, per, info, own, near, far, cross, out, wide):
    step = pl.program_id(0)
    place = step // per
    rel = (place % 2) * 2 + place // 2
    base = first + ((info[4] ^ rel) * per + step % per) * QB
    place_features(info, (own, near, far, cross), wide, live_lanes(info, base, QB))
    out[...] = wide[...].astype(BF)


def cotangent(line, first, parts, size):
    steps = size // QB
    per = steps // 4

    def natural(i, s):
        return (0, (s[4] ^ spot(i // per)) * per + i % per)

    return call(
        functools.partial(cotangent_kernel, first, per),
        line,
        parts,
        [lanes(parts[0].shape[0], QB, natural)] * 4,
        array(D, size),
        lanes(D, QB),
        steps,
        [pltpu.VMEM((D, QB), F32)],
    )


def feed_kernel(blocks, info, *refs):
    count = len(blocks)
    normed, refs = refs[:count], refs[count:]
    cots, refs = refs[:count], refs[count:]
    owners = [k for k in range(count) if blocks[k][1] == 0]
    middles, refs = refs[: len(owners)], refs[len(owners) :]
    wup_t, wdown, wup, wdown_t = refs[:4]
    hidden, gpre, n_all, pd_keep, pd_send = refs[-9 - count : -4 - count]
    acts = refs[-4 - count : -4]
    now, cot, act, wide = refs[-4:]
    step = pl.program_id(0)
    size = now.shape[1]
    base = 0
    for k, (chunk, rel) in enumerate(blocks):
        base = jnp.where(step == k, (chunk * 4 + (info[4] ^ rel)) * size, base)

        @pl.when(step == k)
        def _(k=k):
            now[...] = normed[k][...]
            cot[...] = cots[k][...]

    n_all[...] = now[...]

    @pl.when(base >= info[3])
    def _():
        for ref in (hidden, gpre, act, pd_keep, pd_send):
            ref[...] = jnp.zeros_like(ref)

    @pl.when(base < info[3])
    def _():
        value, slope = gelu_both(dot(wup_t[...], now[...]))
        hidden[...] = value.astype(BF)
        gpre[...] = (dot(wdown[...], cot[...]) * slope).astype(BF)
        act[...] = dot(wup[...], gpre[...]).astype(BF)
        wide[...] = dot(wdown_t[...], hidden[...])
        for k, middle in zip(owners, middles):

            @pl.when(step == k)
            def _(middle=middle):
                wide[...] += middle[...]

        split_features(info, wide, pd_keep, pd_send)

    for k in range(count):

        @pl.when(step == k)
        def _(k=k):
            acts[k][...] = act[...]


def feed(line, blocks, normed, cots, middles, weights, rows, before=()):
    count = len(blocks)
    size = normed[0].shape[1]
    half = D // 2
    owners = [k for k in range(count) if blocks[k][1] == 0]

    def place(i, s):
        index = 0
        for k, (chunk, rel) in enumerate(blocks):
            index = jnp.where(i == k, chunk * 4 + spot(rel), index)
        return (0, index)

    def one(index):
        return pl.BlockSpec((D, size), lambda i, s: (0, index), pipeline_mode=pl.Buffered(1))

    args = (*normed, *[cots[c] for c, r in blocks], *[middles[blocks[k][0]] for k in owners])
    fixed = 1 + len(args) + 4
    return call(
        functools.partial(feed_kernel, tuple(blocks)),
        line,
        (*args, *weights, *before),
        [one(0)] * count
        + [one(spot(r)) for c, r in blocks]
        + [one(0)] * len(owners)
        + [whole((D, D))] * 4
        + [pl.BlockSpec(memory_space=pl.ANY)] * len(before),
        (array(D, rows),) * 3 + (array(half, rows),) * 2 + (array(D, size),) * count,
        (lanes(D, size, place),) * 3 + (lanes(half, size, place),) * 2 + (one(0),) * count,
        count,
        [
            pltpu.VMEM((D, size), BF),
            pltpu.VMEM((D, size), BF),
            pltpu.VMEM((D, size), BF),
            pltpu.VMEM((D, size), F32),
        ],
        vmem=62,
        alias={fixed + k: k for k in range(len(before))},
    )


def back_norm_kernel(info, keep, got, last, middle, stats, g_rel, affine, grad, turned, sums):
    @pl.when(pl.program_id(0) == 0)
    def _():
        sums[...] = jnp.zeros_like(sums)

    total = keep[...].astype(F32) + got[...].astype(F32) + last[...].astype(F32)
    inv_row = stats[1:2, :]
    hat = (middle[...] - stats[0:1, :]) * inv_row
    scaled = total * affine[:, 2:3]
    product = scaled * hat
    mean_one = jnp.sum(scaled, axis=0, keepdims=True) * (1.0 / D)
    mean_two = jnp.sum(product, axis=0, keepdims=True) * (1.0 / D)
    grad[...] = (
        g_rel[...].astype(F32) + inv_row * (scaled - mean_one - hat * mean_two)
    ).astype(BF)
    sums[:, 2:3] += jnp.sum(total * hat, axis=1, keepdims=True)
    sums[:, 3:4] += jnp.sum(total, axis=1, keepdims=True)

    @pl.when(pl.program_id(0) == pl.num_programs(0) - 1)
    def _():
        turned[...] = sums[...].T[:8]


def back_norm(line, keep, got, last, middle, stats, g_rel, affine):
    rows = middle.shape[1]
    step = 128
    return call(
        back_norm_kernel,
        line,
        (keep, got, last, middle, stats, g_rel, affine),
        [lanes(D, step)] * 4 + [lanes(8, step), lanes(D, step), whole((D, 4))],
        (array(D, rows), array(8, D, dtype=F32)),
        (lanes(D, step), whole((8, D))),
        rows // step,
        [pltpu.VMEM((D, 128), F32)],
    )


def back_kernel(heads, chunk, final, info, *refs):
    parts, qkv, stats, wout, wqkv = refs[:4], *refs[4:8]
    refs = refs[8:]
    if chunk:
        before, refs = refs[0], refs[1:]
    if not final:
        carry, refs = refs[:2], refs[2:]
    carry_out = refs[-16:-14] if chunk else ()
    gown, gm_all, keep, send, joined = refs[-14:-9]
    now, query_now, grad_now, wide, kbuf, vbuf, ktbuf, dkbuf, dvbuf = refs[-9:]
    per = pl.num_programs(0)
    step = per - 1 - pl.program_id(0)
    cols = heads * HD
    tail = TAIL if chunk else 0
    size = qkv.shape[1]
    place = chunk * per + step
    base = place * QB
    bounds = [info[k] for k in range(4)]
    here = pl.ds(pl.multiple_of(tail + step * QB, QB), QB)
    inner = parts[0].shape[1] // QB
    rel = (step // inner) ^ info[4]
    local = pl.ds(pl.multiple_of(step % inner * QB, QB), QB)

    def hold(source, start, width):
        for h in range(heads):
            keys = source[cols + HD * h : cols + HD * (h + 1), :]
            ktbuf[h, :, start : start + width] = keys
            kbuf[h, start : start + width, :] = keys.T
            vbuf[h, start : start + width, :] = source[
                2 * cols + HD * h : 2 * cols + HD * (h + 1), :
            ].T

    @pl.when(pl.program_id(0) == 0)
    def _():
        dkbuf[...] = jnp.zeros_like(dkbuf)
        dvbuf[...] = jnp.zeros_like(dvbuf)
        hold(qkv, tail, size)
        if chunk:
            hold(before, 0, TAIL)
        if not final:
            dkbuf[:, :, tail + size - TAIL : tail + size] = carry[0][...]
            dvbuf[:, :, tail + size - TAIL : tail + size] = carry[1][...]

    query_now[...] = qkv[:cols, pl.ds(pl.multiple_of(step * QB, QB), QB)]
    for r in range(4):

        @pl.when(rel == r)
        def _(r=r):
            now[...] = parts[r][:, local]

    gm_all[...] = now[...]
    wide[...] = now[...].astype(F32)
    gown[...] = wide[pl.ds(pl.multiple_of(info[4] * cols, 8), cols), :].astype(BF)

    @pl.when(base >= bounds[3])
    def _():
        for ref in (joined, keep, send):
            ref[...] = jnp.zeros_like(ref)

    @pl.when(base < bounds[3])
    def _():
        grad_now[...] = dot(wout[...], now[...]).astype(BF)

        def attend(lane, window, allowed):
            every = range(heads)
            parts = [slice(HD * h, HD * (h + 1)) for h in every]
            query = [query_now[part, lane] for part in parts]
            grads = [grad_now[part, lane] for part in parts]
            scores = [dot(kbuf[h, window, :], query[h]) * SCALE for h in every]
            grad_probs = [dot(vbuf[h, window, :], grads[h]) for h in every]
            probs = [
                jnp.exp(jnp.where(allowed, scores[h], -1e30) - stats[2 + h : 3 + h, lane])
                for h in every
            ]
            for h in every:
                dvbuf[h, :, window] += dot(grads[h], probs[h].astype(BF), ((1,), (1,)))
            deltas = [
                jnp.sum(probs[h] * grad_probs[h], axis=0, keepdims=True) for h in every
            ]
            grad_scores = [
                (probs[h] * (grad_probs[h] - deltas[h]) * SCALE).astype(BF) for h in every
            ]
            for h in every:
                dkbuf[h, :, window] += dot(query[h], grad_scores[h], ((1,), (1,)))
                wide[parts[h], lane] = dot(ktbuf[h, :, window], grad_scores[h])

        def skip(lane):
            wide[:cols, lane] = jnp.zeros((cols, SUB), F32)

        each_window(bounds, base, tail - chunk * per * QB, attend, skip)
        for h in range(heads):
            wide[cols + HD * h : cols + HD * (h + 1), :] = dkbuf[h, :, here]
            wide[2 * cols + HD * h : 2 * cols + HD * (h + 1), :] = dvbuf[h, :, here]
        joined[...] = wide[: 3 * cols, :].astype(BF)
        wide[...] = dot(wqkv[...], joined[...])
        split_features(info, wide, keep, send)

    if chunk:

        @pl.when(pl.program_id(0) == per - 1)
        def _():
            carry_out[0][...] = dkbuf[:, :, :TAIL]
            carry_out[1][...] = dvbuf[:, :, :TAIL]


def back(line, chunk, parts, qkvs, stats, wout, wqkv, made=None):
    joined, size = qkvs[0].shape
    rows = len(qkvs) * size
    cols = joined // 3
    heads = cols // HD
    steps = size // QB
    final = made is None
    carried = (heads, HD, TAIL)

    def turn(i, s):
        return (0, chunk * steps + steps - 1 - i)

    args = [*parts, qkvs[chunk], stats, wout, wqkv]
    specs = [whole((D, size // 4))] * 4 + [whole((joined, size)), lanes(16, QB, turn)]
    specs += [whole((cols, D)), whole((D, joined))]
    if chunk:
        last = size // TAIL - 1
        args.append(qkvs[chunk - 1])
        specs.append(
            pl.BlockSpec((joined, TAIL), lambda i, s: (0, last), pipeline_mode=pl.Buffered(1))
        )
    alias = None
    outs = [array(*carried, dtype=F32)] * 2 if chunk else []
    out_specs = [whole(carried)] * 2 if chunk else []
    if not final:
        args += made[:2]
        specs += [whole(carried)] * 2
        alias = {1 + len(args) + k: len(outs) + k for k in range(5)}
        args += made[2:]
        specs += [pl.BlockSpec(memory_space=pl.ANY)] * 5
    heights = (cols, D, 2 * cols, 2 * cols, joined)
    return call(
        functools.partial(back_kernel, heads, chunk, final),
        line,
        args,
        specs,
        (*outs, *[array(height, rows) for height in heights]),
        (*out_specs, *[lanes(height, QB, turn) for height in heights]),
        steps,
        [
            pltpu.VMEM((D, QB), BF),
            pltpu.VMEM((cols, QB), BF),
            pltpu.VMEM((cols, QB), BF),
            pltpu.VMEM((D, QB), F32),
            pltpu.VMEM((heads, TAIL + size, HD), BF),
            pltpu.VMEM((heads, TAIL + size, HD), BF),
            pltpu.VMEM((heads, HD, TAIL + size), BF),
            pltpu.VMEM((heads, HD, TAIL + size), F32),
            pltpu.VMEM((heads, HD, TAIL + size), F32),
        ],
        vmem=62,
        alias=alias,
    )


def row_order(info, value, mask):
    block = value.shape[1] // 4
    return [
        value[:, pl.ds(pl.multiple_of(spot(info[4] ^ mask ^ j) * block, 128), block)]
        for j in range(4)
    ]


def columns_kernel(info, keep, got, out):
    block = out.shape[1] // 4
    pairs = zip(row_order(info, keep, 0), row_order(info, got, 1))
    for j, (left, right) in enumerate(pairs):
        total = left.astype(F32) + right.astype(F32)
        out[:, j * block : (j + 1) * block] = total.astype(BF)


def fold_columns_far(line, keep, got, relative, size):
    cols, rows = keep.shape[0] // 2, keep.shape[1]
    low = lanes(cols, size, lambda i, s: (1, i))
    return call(
        columns_kernel if relative else add_kernel,
        line,
        (keep, got),
        [low, low],
        array(cols, rows),
        lanes(cols, size),
        rows // size,
    )


def out_kernel(info, keep, got, last, out):
    block = out.shape[1] // 4
    pairs = zip(row_order(info, keep, 0), row_order(info, got, 1))
    for j, (left, right) in enumerate(pairs):
        here = slice(j * block, (j + 1) * block)
        total = left.astype(F32) + right.astype(F32) + last[:, here].astype(F32)
        live = live_lanes(info, pl.program_id(0) * out.shape[1] + j * block, block)
        out[:, here] = jnp.where(live, total, 0.0).astype(BF)


def out_rows(line, keep, got, last, home_rows, size):
    cols, rows = last.shape
    top = lanes(cols, size)
    return call(
        out_kernel,
        line,
        (keep, got, last),
        [top, top, top],
        array(cols, home_rows),
        top,
        rows // size,
    )


def first_sums_kernel(info, keep, got, last, x, stats, gain, other, total, both, sums):
    step = pl.program_id(0)
    cols, block = total.shape

    @pl.when(step == 0)
    def _():
        sums[...] = jnp.zeros_like(sums)

    live = live_lanes(info, step * block, block)
    grad = keep[...].astype(F32) + got[...].astype(F32) + last[...].astype(F32)
    grad = jnp.where(live, grad, 0.0)
    hat = (jnp.where(live, x[...].astype(F32), 0.0) - stats[0:1, :]) * stats[1:2, :]
    scaled = grad * gain[:, 0:1]
    total[...] = grad
    one = jnp.sum(scaled, axis=0, keepdims=True)
    two = jnp.sum(scaled * hat, axis=0, keepdims=True)
    both[:, pl.ds(pl.multiple_of(step * block, 128), block)] = jnp.concatenate([one, two] * 4, axis=0)
    mine = pl.ds(pl.multiple_of(info[4] * cols, 8), cols)
    sums[mine, 0:1] += jnp.sum(grad * hat, axis=1, keepdims=True)
    sums[mine, 1:2] += jnp.sum(grad, axis=1, keepdims=True)

    @pl.when(step == pl.num_programs(0) - 1)
    def _():
        start = both.shape[1] - D
        both[:, start:] = sums[...].T[:8] + other[...]


def first_sums(line, keep, got, last, x, stats, gain, other):
    cols, rows = last.shape
    block = rows // 4
    top = lanes(cols, block)
    return call(
        first_sums_kernel,
        line,
        (keep, got, last, x, stats, gain, other),
        [top, top, top, top, lanes(16, block), whole((cols, 2)), whole((8, D))],
        (array(cols, rows, dtype=F32), array(8, rows + D, dtype=F32)),
        (top, whole((8, rows + D))),
        4,
        [pltpu.VMEM((D, 128), F32)],
    )


def x_grad_kernel(info, total, rowsums, x, stats, gain, gown, out):
    live = live_lanes(info, pl.program_id(0) * out.shape[1], out.shape[1])
    inv_row = stats[1:2, :]
    hat = (jnp.where(live, x[...].astype(F32), 0.0) - stats[0:1, :]) * inv_row
    inner = total[...] * gain[:, 0:1] - rowsums[0:1, :] * (1.0 / D)
    inner = inner - hat * (rowsums[1:2, :] * (1.0 / D))
    grad = gown[...].astype(F32) + inv_row * inner
    out[...] = jnp.where(live, grad, 0.0).astype(BF)


def x_gradient(line, total, rowsums, x, stats, gain, gown, home_rows):
    cols, rows = total.shape
    block = rows // 4
    top = lanes(cols, block)
    return call(
        x_grad_kernel,
        line,
        (total, rowsums, x, stats, gain, gown),
        [top, lanes(8, block), top, lanes(16, block), whole((cols, 2)), top],
        array(cols, home_rows),
        top,
        4,
    )


def after(value, *before):
    return lax.optimization_barrier((value, *before))[0]


def gather_parts(value, before=()):
    far = swap(value, "tensor", 2)
    near = swap(value, "tensor", 1)
    return (value, near, far, swap(after(far, *before) if before else far, "tensor", 1))


def total_over(value, axis):
    mask = 1
    while mask < lax.axis_size(axis):
        value = value + swap(value, axis, mask)
        mask *= 2
    return value


def weight_kernel(jobs, orders, info, *refs):
    count = 2 * len(jobs)
    outs, total, refs = refs[-count - 1 : -1], refs[-1], refs[: -count - 1]
    for k, groups in enumerate(jobs):
        top = 0
        for pieces in groups:
            left, right = refs[:pieces], refs[pieces : 2 * pieces]
            refs = refs[2 * pieces :]
            rows = left[0].shape[0]
            value = dot(left[0][...], right[0][...], ((1,), (1,)))
            for m in range(1, pieces):
                value = value + dot(left[m][...], right[m][...], ((1,), (1,)))
            total[top : top + rows, :] = value
            top += rows
        mine, send = outs[2 * k : 2 * k + 2]
        half = mine.shape[0]
        bit = info[8 + orders[k][0] // 2]
        mine[...] = total[pl.ds(pl.multiple_of(bit * half, 8), half), :].astype(BF)
        send[...] = total[pl.ds(pl.multiple_of((1 - bit) * half, 8), half), :].astype(BF)


WSTEP = 256


def weight_gradients(line, jobs, orders, first=0, width=D, before=()):
    args, specs, shape = [], [], []
    skip = first // WSTEP
    for pairs in jobs:
        shape.append(tuple(len(left) for left, right in pairs))
        for left, right in pairs:
            for item, k, parts in left:
                args.append(item)
                specs.append(
                    pl.BlockSpec(
                        (item.shape[0], item.shape[1] // parts),
                        lambda i, s, k=k: (0, k),
                        pipeline_mode=pl.Buffered(1),
                    )
                )
            for item, k, parts in right:
                args.append(item)
                specs.append(
                    pl.BlockSpec(
                        (WSTEP, item.shape[1] // parts), lambda i, s, k=k: (i + skip, k)
                    )
                )
    result = call(
        functools.partial(weight_kernel, tuple(shape), tuple(orders)),
        line,
        args,
        specs,
        (array(D // 2, width),) * (2 * len(jobs)),
        (lanes(D // 2, WSTEP),) * (2 * len(jobs)),
        -(-width // WSTEP),
        [pltpu.VMEM((D, WSTEP), F32)],
        vmem=62,
    )
    return [
        GroupSum(line, result[2 * k], after(result[2 * k + 1], *before), orders[k])
        for k in range(len(jobs))
    ]


def spread_kernel(info, *refs, orders, divided):
    step = pl.program_id(0)
    pieces = len(orders)
    parts, weight, outs = refs[: 4 * pieces], refs[4 * pieces], refs[4 * pieces + 1 :]
    left = 0
    for m, (first, second) in enumerate(orders):
        right = left + parts[4 * m].shape[1]
        place = ((step // 2) ^ info[8 + first // 2]) * 2 + ((step % 2) ^ info[8 + second // 2])
        for top, out in enumerate(outs):
            inside = (step >= 3 if top else step < 3) if divided else step >= 0
            for k in range(4):

                @pl.when((place == k) & inside)
                def _(out=out, part=parts[4 * m + k], left=left, right=right):
                    out[:, left:right] = part[...].astype(F32) * weight[0:1, 0:1]
        left = right


def spread_groups(line, sums, weight, divided=False):
    rows = sums[0].mine.shape[0]
    if divided:
        outs = (array(3 * rows, D, dtype=F32), array(rows, D, dtype=F32))
        specs = (
            pl.BlockSpec((rows, D), lambda i, s: (jnp.minimum(i, 2), 0)),
            pl.BlockSpec((rows, D), lambda i, s: (0, 0)),
        )
    else:
        outs = (array(4 * rows, D, dtype=F32),)
        specs = (pl.BlockSpec((rows, D), lambda i, s: (i, 0)),)
    parts = [item for one in sums for item in (one.mine, one.second, one.first, one.both)]
    return call(
        functools.partial(
            spread_kernel, orders=tuple(one.order for one in sums), divided=divided
        ),
        line,
        (*parts, weight),
        [whole(item.shape) for item in parts] + [whole((1, 1))],
        outs,
        specs,
        4,
    )


class GroupSum:
    def __init__(self, line, mine, send, order):
        self.line = line
        self.order = order
        self.mine = mine
        self.got = swap(send, "dp", order[0])

    def add(self, bit=None):
        def whole_or_half(value):
            if bit is None:
                return value.astype(F32)
            half = value.shape[0] // 2
            return lax.dynamic_slice_in_dim(value, bit * half, half).astype(F32)

        mine, got = self.line.tie(self.mine), self.got
        self.line.last = (whole_or_half(mine) + whole_or_half(got)).astype(BF)
        return self.line.last

    def quarter(self):
        bit = lax.axis_index("dp") // self.order[1] % 2
        send, self.mine = self.add(1 - bit), self.add(bit)
        self.got = swap(send, "dp", self.order[1])

    def meet(self):
        mask = 4
        self.mine = self.add()
        while mask < lax.axis_size("dp") // 2:
            self.got = swap(self.mine, "dp", mask)
            self.mine = self.add()
            mask *= 2
        self.got = swap(self.mine, "dp", mask)

    def close(self):
        self.mine = self.add()
        self.second = swap(self.mine, "dp", self.order[1])
        self.first = swap(self.mine, "dp", self.order[0])

    def relay(self, tie=False):
        second = self.line.tie(self.second) if tie else self.second
        self.both = swap(second, "dp", self.order[0])


def shards(
    x_home,
    cot_home,
    cell_len,
    norm1_gain,
    norm1_bias,
    qkv_weight,
    out_weight,
    norm2_gain,
    norm2_bias,
    up_weight,
    down_weight,
):
    groups = cell_len.shape[0]
    home_rows, cols = x_home.shape
    rows = -(-home_rows // 1024) * 1024
    me = lax.axis_index("tensor").astype(jnp.int32)
    group = lax.axis_index("dp")
    weight = groups / jnp.sum(cell_len).astype(F32)
    my_len = lax.dynamic_index_in_dim(cell_len, group, 0, keepdims=False)
    bounds = jnp.cumsum(my_len).astype(jnp.int32)
    group_bits = jnp.stack([group % 2, group // 2 % 2]).astype(jnp.int32)
    info = jnp.concatenate([bounds, jnp.broadcast_to(me, (4,)), group_bits])
    line = Line(info)

    chunks = 2
    size = rows // chunks
    block = size // 4
    x = x_home.T
    x_cuts = [x[:, :size], x[:, size:]]
    cot = cot_home.T
    cot_cuts = [cot[:, :size], cot[:, size:]]
    own_affine = jnp.stack([norm1_gain, norm1_bias, norm2_gain, norm2_bias], axis=1)
    wqkv_t = qkv_weight.transpose(1, 2, 0).reshape(3 * cols, D)
    wout_t, wup_t, wdown_t, wqkv = turned(out_weight, up_weight, down_weight, wqkv_t)
    affine_parts = gather_parts(own_affine, (wout_t, x_cuts[1], *cot_cuts))
    x_zero = gather_parts(x_cuts[0], (affine_parts[3],))
    x_next = after(x_cuts[1], affine_parts[1])
    x_next_far, x_next_near = swap(x_next, "tensor", 2), swap(x_next, "tensor", 1)
    cot_far = [swap(after(cot_cuts[0], x_zero[2]), "tensor", 2)]

    def cot_parts(c):
        value, far = cot_cuts[c], cot_far[c]
        return (value, swap(line.tie(value), "tensor", 1), far, swap(line.tie(far), "tensor", 1))

    normed, qkv, mixed, stats, keep, send, xmid, affine = front(
        line, 0, x_zero, affine_parts, wqkv_t, wout_t, rows, chunks
    )
    normed, qkv, mixed, xmid = [normed], [qkv], [mixed], [xmid]
    folds = []
    got = swap(after(send, cot_far[0], x_next_far, x_next_near), "tensor", 1)
    x_next_cross = swap(line.tie(x_next_far), "tensor", 1)
    far_sum = fold_far(line, keep, got)
    folds.append((keep, got, swap(far_sum, "tensor", 2)))
    cot_far.append(swap(after(cot_cuts[1], far_sum), "tensor", 2))
    cots = [cot_parts(0)]
    results = front(
        line,
        1,
        (x_next, x_next_near, x_next_far, x_next_cross),
        affine_parts,
        wqkv_t,
        wout_t,
        rows,
        chunks,
        (qkv[0], stats),
    )
    normed.append(results[0])
    qkv.append(results[1])
    mixed.append(results[2])
    stats, keep, send = results[3:6]
    xmid.append(results[6])
    middle, stats_two, n_parts = [], [], []

    def norm_chunk(c):
        values, n_own, stat = second_norm(line, xmid[c], *folds[c], affine)
        middle.append(values)
        stats_two.append(stat)
        n_parts.append([n_own, swap(n_own, "tensor", 1), swap(n_own, "tensor", 2), None])

    got = swap(after(send, cot_far[1], folds[0][2]), "tensor", 1)
    norm_chunk(0)
    far_sum = fold_far(line, keep, got)
    folds.append((keep, got, swap(far_sum, "tensor", 2)))
    g_rel = [cotangent(line, 0, cots[0], size)]
    cots.append(cot_parts(1))
    g_rel.append(cotangent(line, size, cots[1], size))
    norm_chunk(1)

    weights = (wup_t, down_weight, up_weight, wdown_t)

    def feed_blocks(blocks, before=()):
        picked = [n_parts[c][r] for c, r in blocks]
        made = feed(line, blocks, picked, g_rel, middle, weights, rows, before)
        return made[:5], made[5:]

    state, (pn_own, pn_near) = feed_blocks([(0, 0), (0, 1)])
    n_parts[0][3] = swap(line.tie(n_parts[0][2]), "tensor", 1)
    own_sums = [(pn_own, swap(pn_near, "tensor", 1))]
    state, (pn_far, pn_cross, pn_own, pn_near) = feed_blocks(
        [(0, 2), (0, 3), (1, 0), (1, 1)], state
    )
    n_parts[1][3] = swap(line.tie(n_parts[1][2]), "tensor", 1)
    own_sums.append((pn_own, swap(after(pn_near, n_parts[1][2]), "tensor", 1)))

    def send_far(pn_far, pn_cross, *before):
        far_sum = call(
            add_kernel,
            line,
            (pn_far, swap(after(pn_cross, *before), "tensor", 1)),
            [lanes(D, block)] * 2,
            array(D, block),
            lanes(D, block),
            1,
        )
        return swap(far_sum, "tensor", 2)

    last = [send_far(pn_far, pn_cross, n_parts[1][2])]
    state, (pn_far, pn_cross) = feed_blocks([(1, 2), (1, 3)], state)
    hidden, gpre, n_all, pd_keep, pd_send = state
    last.append(send_far(pn_far, pn_cross, last[0]))
    g_parts = []

    def back_chunk(c):
        grad_mid, sums = back_norm(
            line, *own_sums[c], last[c], middle[c], stats_two[c], g_rel[c], affine
        )
        near, far = swap(grad_mid, "tensor", 1), swap(grad_mid, "tensor", 2)
        g_parts.append([grad_mid, near, far, None])
        return sums

    sums_two = back_chunk(0)
    pairs = [[(item, c, chunks) for c in range(chunks)] for item in (hidden, gpre, n_all)]
    g_pieces = [(item, 0, 1) for item in g_rel]
    down, up = weight_gradients(
        line, [[(pairs[0], g_pieces)], [([(n_all, 0, 1)], [(gpre, 0, 1)])]], [(1, 2), (2, 1)], before=(last[1],)
    )
    sums_two = sums_two + back_chunk(1)
    pd_got = swap(pd_send, "tensor", 1)
    pd_sum = fold_columns_far(line, pd_keep, pd_got, True, size)
    g_parts[1][3] = swap(line.tie(g_parts[1][2]), "tensor", 1)
    g_parts[0][3] = swap(line.tie(g_parts[0][2]), "tensor", 1)
    down.quarter()
    up.quarter()

    made = back(line, 1, g_parts[1], qkv, stats, out_weight, wqkv)
    down.meet()
    up.meet()
    pd_last = swap(line.tie(pd_sum), "tensor", 2)
    gown, gm_all, keep, send, joined = back(
        line, 0, g_parts[0], qkv, stats, out_weight, wqkv, made
    )
    last_jobs = [
        ([(joined, c, chunks) for c in range(chunks)], [(item, 0, 1) for item in normed]),
        ([(item, 0, 1) for item in mixed], [(gm_all, c, chunks) for c in range(chunks)]),
    ]
    scale = weight.reshape(1, 1)
    (rest_one,) = weight_gradients(
        line, [last_jobs], [(1, 2)], 0, 3 * WSTEP, before=(down.got,)
    )
    down.close()
    got = swap(line.tie(send), "tensor", 1)
    (rest_two,) = weight_gradients(
        line, [last_jobs], [(2, 1)], 3 * WSTEP, D - 3 * WSTEP, before=()
    )
    far_sum = fold_columns_far(line, keep, got, False, size)
    last = swap(far_sum, "tensor", 2)
    out = out_rows(line, pd_keep, pd_got, pd_last, home_rows, size)
    rest_one.quarter()
    up.close()
    rest_two.quarter()
    total, both = first_sums(line, keep, got, last, x, stats, own_affine[:, :2], sums_two)
    rest_one.meet()
    down.relay()
    rest_two.meet()
    (grad_down,) = spread_groups(line, [down], scale)
    both = both + swap(both, "tensor", 1)
    both = both + swap(both, "tensor", 2)
    x_grad = x_gradient(line, total, both, x, stats, own_affine[:, :2], gown, home_rows)
    rest_one.close()
    rest_one.relay()
    rest_two.close()
    up.relay()
    (grad_up,) = spread_groups(line, [up], scale)
    rest_two.relay()
    small = after(both[:, rows:], rest_one.second, rest_two.second)
    mask = groups // 2
    pair = (small, swap(small, "dp", mask))
    grad_qkv, grad_out = spread_groups(line, [rest_one, rest_two], scale, True)
    while pair:
        small = line.other(lambda v: v[0] + v[1], pair)
        mask //= 2
        pair = (small, swap(small, "dp", mask)) if mask else None
    small = lax.dynamic_slice_in_dim(small, me * cols, cols, axis=1) * weight

    return (
        out.T,
        x_grad.T,
        small[0],
        small[1],
        grad_qkv.reshape(3, cols, D).transpose(2, 0, 1),
        grad_out,
        small[2],
        small[3],
        grad_up,
        grad_down,
    )


def solution(mesh):
    rows, vector = P("dp", "tensor"), P("tensor")
    qkv, wide, tall = P(None, None, "tensor"), P(None, "tensor"), P("tensor", None)
    return jax.shard_map(
        shards,
        mesh=mesh,
        in_specs=(rows, rows, P(), vector, vector, qkv, tall, vector, vector, wide, tall),
        out_specs=(rows, rows, vector, vector, qkv, tall, vector, vector, wide, tall),
        check_vma=False,
    )
```

```python
import functools
import math

import jax
import jax.numpy as jnp
from jax import lax
from jax.experimental import pallas as pl
from jax.experimental.pallas import tpu as pltpu
from jax.sharding import PartitionSpec as P


D = 1120
HD = 56
EPS = 1e-05
BF = jnp.bfloat16
F32 = jnp.float32
QB = 256
TAIL = 512
SUB = 128
SCALE = HD ** (-0.5)
SCALE_TWO = SCALE * math.log2(math.e)
GELU_A = (2.0 / math.pi) ** 0.5
GELU_B = 0.044715
MIB = 1 << 20


def swap(value, axis, mask):
    size = lax.axis_size(axis)
    return lax.ppermute(value, axis, [(i, i ^ mask) for i in range(size)])


def dot(left, right, dims=((1,), (0,))):
    return lax.dot_general(left, right, (dims, ((), ())), preferred_element_type=F32)


def gelu_both(v):
    square = v * v
    gate = 0.5 * jnp.tanh(v * (GELU_A + GELU_A * GELU_B * square)) + 0.5
    slope = v * (2.0 * GELU_A + 6.0 * GELU_A * GELU_B * square)
    return (v * gate, gate + gate * (1.0 - gate) * slope)


def spot(rel):
    return (rel % 2) * 2 + rel // 2


def whole(shape):
    return pl.BlockSpec(shape, lambda i, *_: (0,) * len(shape), pipeline_mode=pl.Buffered(1))


def lanes(rows, width, where=None):
    return pl.BlockSpec((rows, width), (lambda i, s: (0, i)) if where is None else where)


class Line:
    def __init__(self, info):
        self.info = info
        self.last = None

    def start(self):
        if self.last is not None:
            self.info = after(self.info, self.last)
        return self.info

    def tie(self, value):
        return after(value, self.last)

    def other(self, function, value):
        self.last = function(self.tie(value))
        return self.last


def call(body, line, args, in_specs, outs, out_specs, steps, scratch=(), vmem=16, alias=None):
    result = pl.pallas_call(
        body,
        out_shape=outs,
        grid_spec=pltpu.PrefetchScalarGridSpec(
            num_scalar_prefetch=1,
            grid=(steps,),
            in_specs=in_specs,
            out_specs=out_specs,
            scratch_shapes=list(scratch),
        ),
        input_output_aliases=alias or {},
        compiler_params=pltpu.CompilerParams(
            dimension_semantics=("arbitrary",), vmem_limit_bytes=vmem * MIB
        ),
        cost_estimate=pl.CostEstimate(flops=1, bytes_accessed=1, transcendentals=0),
    )(line.start(), *args)
    line.last = result[-1] if isinstance(result, (tuple, list)) else result
    return result


def array(*shape, dtype=BF):
    return jax.ShapeDtypeStruct(shape, dtype)


def place_features(info, parts, scratch, live=None):
    count = parts[0].shape[0]
    for rel in range(4):
        value = parts[rel][...].astype(F32)
        if live is not None:
            value = jnp.where(live, value, 0.0)
        start = pl.multiple_of((info[4] ^ rel) * count, 8)
        scratch[pl.ds(start, count), :] = value


def split_features(info, wide, keep, send):
    count = keep.shape[0] // 2
    for rel in range(4):
        part = send if rel % 2 else keep
        start = pl.multiple_of((info[4] ^ rel) * count, 8)
        half = rel // 2 * count
        part[half : half + count, :] = wide[pl.ds(start, count), :].astype(BF)


def live_lanes(info, base, width):
    return base + lax.broadcasted_iota(jnp.int32, (1, width), 1) < info[3]


def first_of(rows, bounds):
    start = jnp.zeros_like(rows)
    for bound in bounds:
        start = jnp.where(rows >= bound, bound, start)
    return start


def each_window(bounds, base, shift, attend, skip):
    def part(index, carry):
        first = pl.multiple_of(base + index * SUB, SUB)
        here = pl.ds(pl.multiple_of(index * SUB, SUB), SUB)
        count = first // SUB - first_of(first, bounds) // SUB + 1

        @pl.when(first >= bounds[3])
        def _():
            skip(here)

        for blocks in range(1, TAIL // SUB + 2):

            @pl.when((count == blocks) & (first < bounds[3]))
            def _(blocks=blocks):
                width = blocks * SUB
                window = pl.ds(pl.multiple_of(first + shift + SUB - width, SUB), width)
                keys = first + SUB - width + lax.broadcasted_iota(jnp.int32, (width, SUB), 0)
                rows = first + lax.broadcasted_iota(jnp.int32, (1, SUB), 1)
                attend(here, window, (keys >= first_of(rows, bounds)) & (keys <= rows))

        return carry

    lax.fori_loop(0, QB // SUB, part, 0)


def norm_rows(values):
    mean_row = jnp.sum(values, axis=0, keepdims=True) * (1.0 / D)
    centered = values - mean_row
    var_row = jnp.sum(centered * centered, axis=0, keepdims=True) * (1.0 / D)
    inv_row = lax.rsqrt(var_row + EPS)
    return (centered * inv_row, mean_row, inv_row)


def front_kernel(heads, chunk, steps, info, *refs):
    own, near, far, cross, affine_own, affine_near, affine_far, affine_cross, wqkv, wout = refs[:10]
    normed, qkv, mixed, stats, keep, send, xmid, affine, wide, kbuf, vtbuf, proj = refs[-12:]
    step = pl.program_id(0)
    cols = heads * HD
    tail = TAIL if chunk else 0
    place = chunk * steps + step
    base = place * QB
    bounds = [info[k] for k in range(4)]
    here = pl.ds(pl.multiple_of(tail + step * QB, QB), QB)
    per = steps // 4
    rel = (step // per) ^ info[4]
    inner = step % per

    @pl.when(step == 0)
    def _():
        place_features(info, (affine_own, affine_near, affine_far, affine_cross), affine)
        if chunk:
            before = refs[10]
            for h in range(heads):
                keys = before[cols + HD * h : cols + HD * (h + 1), :]
                kbuf[h, :TAIL, :] = keys.T
                vtbuf[h, :, :TAIL] = before[2 * cols + HD * h : 2 * cols + HD * (h + 1), :]

    @pl.when(base >= bounds[3])
    def _():
        for ref in (normed, qkv, mixed, stats, proj, wide):
            ref[...] = jnp.zeros_like(ref)

    @pl.when(base < bounds[3])
    def _():
        place_features(info, (own, near, far, cross), wide, live_lanes(info, base, QB))
        hat, mean_row, inv_row = norm_rows(wide[...])
        stats[0:1, :] = mean_row
        stats[1:2, :] = inv_row
        normed[...] = (hat * affine[:, 0:1] + affine[:, 1:2]).astype(BF)
        joined = dot(wqkv[...], normed[...])
        qkv[...] = joined.astype(BF)
        for h in range(heads):
            keys = joined[cols + HD * h : cols + HD * (h + 1)]
            kbuf[h, here, :] = keys.T.astype(BF)
            vtbuf[h, :, here] = joined[2 * cols + HD * h : 2 * cols + HD * (h + 1)].astype(BF)

        def attend(lane, window, allowed):
            every = range(heads)
            scores = [dot(kbuf[h, window, :], qkv[HD * h : HD * (h + 1), lane]) for h in every]
            scores = [jnp.where(allowed, item * SCALE_TWO, -1e30) for item in scores]
            tops = [jnp.max(item, axis=0, keepdims=True) for item in scores]
            shifted = [jnp.exp2(item - top) for item, top in zip(scores, tops)]
            totals = [jnp.sum(item, axis=0, keepdims=True) for item in shifted]
            weights = [(item * (1.0 / total)).astype(BF) for item, total in zip(shifted, totals)]
            pieces = [dot(vtbuf[h, :, window], weights[h]) for h in every]
            for h in every:
                stats[2 + h : 3 + h, lane] = tops[h] + jnp.log2(totals[h])
            mixed[:, lane] = jnp.concatenate(pieces, axis=0).astype(BF)

        def skip(lane):
            mixed[:, lane] = jnp.zeros((cols, SUB), BF)

        each_window(bounds, base, tail - chunk * steps * QB, attend, skip)
        proj[...] = dot(wout[...], mixed[...]).astype(BF)

    target = pl.ds(pl.multiple_of((rel // 2) * (per * QB) + inner * QB, QB), QB)

    @pl.when(rel % 2 == 0)
    def _():
        keep[:, target] = proj[...]

    @pl.when(rel % 2 == 1)
    def _():
        send[:, target] = proj[...]

    @pl.when(rel == 0)
    def _():
        xmid[:, pl.ds(pl.multiple_of(inner * QB, QB), QB)] = wide[...].astype(BF)


def front(line, chunk, parts, affine, wqkv, wout, rows, count, before=()):
    joined, cols = wqkv.shape[0], wqkv.shape[0] // 3
    heads = cols // HD
    size = rows // count
    steps = size // QB
    last = size // TAIL - 1
    extra = [pl.BlockSpec((joined, TAIL), lambda i, s: (0, last), pipeline_mode=pl.Buffered(1))]
    extra.append(pl.BlockSpec(memory_space=pl.ANY))
    return call(
        functools.partial(front_kernel, heads, chunk, steps),
        line,
        (*parts, *affine, wqkv, wout, *before),
        [lanes(cols, QB)] * 4
        + [whole((cols, 4))] * 4
        + [whole((joined, D)), whole((D, cols))]
        + extra[: len(before)],
        (
            array(D, size),
            array(joined, size),
            array(cols, size),
            array(16, rows, dtype=F32),
            array(D, size // 2),
            array(D, size // 2),
            array(D, size // 4),
            array(D, 4, dtype=F32),
        ),
        (
            lanes(D, QB),
            lanes(joined, QB),
            lanes(cols, QB),
            lanes(16, QB, lambda i, s: (0, chunk * steps + i)),
            whole((D, size // 2)),
            whole((D, size // 2)),
            whole((D, size // 4)),
            whole((D, 4)),
        ),
        steps,
        [
            pltpu.VMEM((D, QB), F32),
            pltpu.VMEM((heads, TAIL + size, HD), BF),
            pltpu.VMEM((heads, HD, TAIL + size), BF),
            pltpu.VMEM((D, QB), BF),
        ],
        vmem=62,
        alias={12: 3} if before else None,
    )


def add_kernel(info, left, right, out):
    out[...] = (left[...].astype(F32) + right[...].astype(F32)).astype(BF)


def fold_far(line, keep, got):
    rows = keep.shape[1] // 2
    step = 256
    shift = rows // step
    spec = lanes(D, step, lambda i, s: (0, i + shift))
    return call(
        add_kernel,
        line,
        (keep, got),
        [spec, spec],
        array(D, rows),
        lanes(D, step),
        rows // step,
    )


def middle_kernel(info, xmid, keep, got, last, affine, middle, normed, stats):
    values = xmid[...].astype(F32) + keep[...].astype(F32)
    values = values + got[...].astype(F32) + last[...].astype(F32)
    middle[...] = values
    hat, mean_row, inv_row = norm_rows(values)
    normed[...] = (hat * affine[:, 2:3] + affine[:, 3:4]).astype(BF)
    stats[...] = jnp.concatenate([mean_row, inv_row] * 4, axis=0)


def second_norm(line, xmid, keep, got, last, affine):
    rows = xmid.shape[1]
    step = 128
    return call(
        middle_kernel,
        line,
        (xmid, keep, got, last, affine),
        [lanes(D, step)] * 4 + [whole((D, 4))],
        (array(D, rows, dtype=F32), array(D, rows), array(8, rows, dtype=F32)),
        (lanes(D, step), lanes(D, step), lanes(8, step)),
        rows // step,
    )


def turn_kernel(*refs):
    half = len(refs) // 2
    for value, out in zip(refs[:half], refs[half:]):
        out[...] = value[...].T


def turned(*values):
    specs, outs, out_specs = [], [], []
    for value in values:
        rows, cols = value.shape
        outs.append(array(cols, rows))
        if cols == D:
            specs.append(pl.BlockSpec((rows, WSTEP), lambda i: (0, i)))
            out_specs.append(pl.BlockSpec((WSTEP, rows), lambda i: (i, 0)))
        else:
            specs.append(pl.BlockSpec((WSTEP, cols), lambda i: (i, 0)))
            out_specs.append(pl.BlockSpec((cols, WSTEP), lambda i: (0, i)))
    return pl.pallas_call(
        turn_kernel,
        out_shape=tuple(outs),
        grid=(-(-D // WSTEP),),
        in_specs=specs,
        out_specs=tuple(out_specs),
        compiler_params=pltpu.CompilerParams(
            dimension_semantics=("arbitrary",), vmem_limit_bytes=62 * MIB
        ),
    )(*values)


def cotangent_kernel(first, per, info, own, near, far, cross, out, wide):
    step = pl.program_id(0)
    place = step // per
    rel = (place % 2) * 2 + place // 2
    base = first + ((info[4] ^ rel) * per + step % per) * QB
    place_features(info, (own, near, far, cross), wide, live_lanes(info, base, QB))
    out[...] = wide[...].astype(BF)


def cotangent(line, first, parts, size):
    steps = size // QB
    per = steps // 4

    def natural(i, s):
        return (0, (s[4] ^ spot(i // per)) * per + i % per)

    return call(
        functools.partial(cotangent_kernel, first, per),
        line,
        parts,
        [lanes(parts[0].shape[0], QB, natural)] * 4,
        array(D, size),
        lanes(D, QB),
        steps,
        [pltpu.VMEM((D, QB), F32)],
    )


def feed_kernel(blocks, info, *refs):
    count = len(blocks)
    normed, refs = refs[:count], refs[count:]
    cots, refs = refs[:count], refs[count:]
    owners = [k for k in range(count) if blocks[k][1] == 0]
    middles, refs = refs[: len(owners)], refs[len(owners) :]
    wup_t, wdown, wup, wdown_t = refs[:4]
    hidden, gpre, n_all, pd_keep, pd_send = refs[-9 - count : -4 - count]
    acts = refs[-4 - count : -4]
    now, cot, act, wide = refs[-4:]
    step = pl.program_id(0)
    size = now.shape[1]
    base = 0
    for k, (chunk, rel) in enumerate(blocks):
        base = jnp.where(step == k, (chunk * 4 + (info[4] ^ rel)) * size, base)

        @pl.when(step == k)
        def _(k=k):
            now[...] = normed[k][...]
            cot[...] = cots[k][...]

    n_all[...] = now[...]

    @pl.when(base >= info[3])
    def _():
        for ref in (hidden, gpre, act, pd_keep, pd_send):
            ref[...] = jnp.zeros_like(ref)

    @pl.when(base < info[3])
    def _():
        value, slope = gelu_both(dot(wup_t[...], now[...]))
        hidden[...] = value.astype(BF)
        gpre[...] = (dot(wdown[...], cot[...]) * slope).astype(BF)
        act[...] = dot(wup[...], gpre[...]).astype(BF)
        wide[...] = dot(wdown_t[...], hidden[...])
        for k, middle in zip(owners, middles):

            @pl.when(step == k)
            def _(middle=middle):
                wide[...] += middle[...]

        split_features(info, wide, pd_keep, pd_send)

    for k in range(count):

        @pl.when(step == k)
        def _(k=k):
            acts[k][...] = act[...]


def feed(line, blocks, normed, cots, middles, weights, rows, before=()):
    count = len(blocks)
    size = normed[0].shape[1]
    half = D // 2
    owners = [k for k in range(count) if blocks[k][1] == 0]

    def place(i, s):
        index = 0
        for k, (chunk, rel) in enumerate(blocks):
            index = jnp.where(i == k, chunk * 4 + spot(rel), index)
        return (0, index)

    def one(index):
        return pl.BlockSpec((D, size), lambda i, s: (0, index), pipeline_mode=pl.Buffered(1))

    args = (*normed, *[cots[c] for c, r in blocks], *[middles[blocks[k][0]] for k in owners])
    fixed = 1 + len(args) + 4
    return call(
        functools.partial(feed_kernel, tuple(blocks)),
        line,
        (*args, *weights, *before),
        [one(0)] * count
        + [one(spot(r)) for c, r in blocks]
        + [one(0)] * len(owners)
        + [whole((D, D))] * 4
        + [pl.BlockSpec(memory_space=pl.ANY)] * len(before),
        (array(D, rows),) * 3 + (array(half, rows),) * 2 + (array(D, size),) * count,
        (lanes(D, size, place),) * 3 + (lanes(half, size, place),) * 2 + (one(0),) * count,
        count,
        [
            pltpu.VMEM((D, size), BF),
            pltpu.VMEM((D, size), BF),
            pltpu.VMEM((D, size), BF),
            pltpu.VMEM((D, size), F32),
        ],
        vmem=62,
        alias={fixed + k: k for k in range(len(before))},
    )


def back_norm_kernel(info, keep, got, last, middle, stats, g_rel, affine, grad, turned, sums):
    @pl.when(pl.program_id(0) == 0)
    def _():
        sums[...] = jnp.zeros_like(sums)

    total = keep[...].astype(F32) + got[...].astype(F32) + last[...].astype(F32)
    inv_row = stats[1:2, :]
    hat = (middle[...] - stats[0:1, :]) * inv_row
    scaled = total * affine[:, 2:3]
    product = scaled * hat
    mean_one = jnp.sum(scaled, axis=0, keepdims=True) * (1.0 / D)
    mean_two = jnp.sum(product, axis=0, keepdims=True) * (1.0 / D)
    grad[...] = (
        g_rel[...].astype(F32) + inv_row * (scaled - mean_one - hat * mean_two)
    ).astype(BF)
    sums[:, 2:3] += jnp.sum(total * hat, axis=1, keepdims=True)
    sums[:, 3:4] += jnp.sum(total, axis=1, keepdims=True)

    @pl.when(pl.program_id(0) == pl.num_programs(0) - 1)
    def _():
        turned[...] = sums[...].T[:8]


def back_norm(line, keep, got, last, middle, stats, g_rel, affine):
    rows = middle.shape[1]
    step = 128
    return call(
        back_norm_kernel,
        line,
        (keep, got, last, middle, stats, g_rel, affine),
        [lanes(D, step)] * 4 + [lanes(8, step), lanes(D, step), whole((D, 4))],
        (array(D, rows), array(8, D, dtype=F32)),
        (lanes(D, step), whole((8, D))),
        rows // step,
        [pltpu.VMEM((D, 128), F32)],
    )


def back_kernel(heads, chunk, final, info, *refs):
    parts, qkv, stats, wout, wqkv = refs[:4], *refs[4:8]
    refs = refs[8:]
    if chunk:
        before, refs = refs[0], refs[1:]
    if not final:
        carry, refs = refs[:2], refs[2:]
    carry_out = refs[-16:-14] if chunk else ()
    gown, gm_all, keep, send, joined = refs[-14:-9]
    now, query_now, grad_now, wide, kbuf, vbuf, ktbuf, dkbuf, dvbuf = refs[-9:]
    per = pl.num_programs(0)
    step = per - 1 - pl.program_id(0)
    cols = heads * HD
    tail = TAIL if chunk else 0
    size = qkv.shape[1]
    place = chunk * per + step
    base = place * QB
    bounds = [info[k] for k in range(4)]
    here = pl.ds(pl.multiple_of(tail + step * QB, QB), QB)
    inner = parts[0].shape[1] // QB
    rel = (step // inner) ^ info[4]
    local = pl.ds(pl.multiple_of(step % inner * QB, QB), QB)

    def hold(source, start, width):
        for h in range(heads):
            keys = source[cols + HD * h : cols + HD * (h + 1), :]
            ktbuf[h, :, start : start + width] = keys
            kbuf[h, start : start + width, :] = keys.T
            vbuf[h, start : start + width, :] = source[
                2 * cols + HD * h : 2 * cols + HD * (h + 1), :
            ].T

    @pl.when(pl.program_id(0) == 0)
    def _():
        dkbuf[...] = jnp.zeros_like(dkbuf)
        dvbuf[...] = jnp.zeros_like(dvbuf)
        hold(qkv, tail, size)
        if chunk:
            hold(before, 0, TAIL)
        if not final:
            dkbuf[:, :, tail + size - TAIL : tail + size] = carry[0][...]
            dvbuf[:, :, tail + size - TAIL : tail + size] = carry[1][...]

    query_now[...] = qkv[:cols, pl.ds(pl.multiple_of(step * QB, QB), QB)]
    for r in range(4):

        @pl.when(rel == r)
        def _(r=r):
            now[...] = parts[r][:, local]

    gm_all[...] = now[...]
    wide[...] = now[...].astype(F32)
    gown[...] = wide[pl.ds(pl.multiple_of(info[4] * cols, 8), cols), :].astype(BF)

    @pl.when(base >= bounds[3])
    def _():
        for ref in (joined, keep, send):
            ref[...] = jnp.zeros_like(ref)

    @pl.when(base < bounds[3])
    def _():
        grad_now[...] = dot(wout[...], now[...]).astype(BF)

        def attend(lane, window, allowed):
            every = range(heads)
            parts = [slice(HD * h, HD * (h + 1)) for h in every]
            query = [query_now[part, lane] for part in parts]
            grads = [grad_now[part, lane] for part in parts]
            scores = [dot(kbuf[h, window, :], query[h]) * SCALE_TWO for h in every]
            grad_probs = [dot(vbuf[h, window, :], grads[h]) for h in every]
            probs = [
                jnp.exp2(jnp.where(allowed, scores[h], -1e30) - stats[2 + h : 3 + h, lane])
                for h in every
            ]
            for h in every:
                dvbuf[h, :, window] += dot(grads[h], probs[h].astype(BF), ((1,), (1,)))
            deltas = [
                jnp.sum(probs[h] * grad_probs[h], axis=0, keepdims=True) for h in every
            ]
            grad_scores = [
                (probs[h] * (grad_probs[h] - deltas[h]) * SCALE).astype(BF) for h in every
            ]
            for h in every:
                dkbuf[h, :, window] += dot(query[h], grad_scores[h], ((1,), (1,)))
                wide[parts[h], lane] = dot(ktbuf[h, :, window], grad_scores[h])

        def skip(lane):
            wide[:cols, lane] = jnp.zeros((cols, SUB), F32)

        each_window(bounds, base, tail - chunk * per * QB, attend, skip)
        for h in range(heads):
            wide[cols + HD * h : cols + HD * (h + 1), :] = dkbuf[h, :, here]
            wide[2 * cols + HD * h : 2 * cols + HD * (h + 1), :] = dvbuf[h, :, here]
        joined[...] = wide[: 3 * cols, :].astype(BF)
        wide[...] = dot(wqkv[...], joined[...])
        split_features(info, wide, keep, send)

    if chunk:

        @pl.when(pl.program_id(0) == per - 1)
        def _():
            carry_out[0][...] = dkbuf[:, :, :TAIL]
            carry_out[1][...] = dvbuf[:, :, :TAIL]


def back(line, chunk, parts, qkvs, stats, wout, wqkv, made=None):
    joined, size = qkvs[0].shape
    rows = len(qkvs) * size
    cols = joined // 3
    heads = cols // HD
    steps = size // QB
    final = made is None
    carried = (heads, HD, TAIL)

    def turn(i, s):
        return (0, chunk * steps + steps - 1 - i)

    args = [*parts, qkvs[chunk], stats, wout, wqkv]
    specs = [whole((D, size // 4))] * 4 + [whole((joined, size)), lanes(16, QB, turn)]
    specs += [whole((cols, D)), whole((D, joined))]
    if chunk:
        last = size // TAIL - 1
        args.append(qkvs[chunk - 1])
        specs.append(
            pl.BlockSpec((joined, TAIL), lambda i, s: (0, last), pipeline_mode=pl.Buffered(1))
        )
    alias = None
    outs = [array(*carried, dtype=F32)] * 2 if chunk else []
    out_specs = [whole(carried)] * 2 if chunk else []
    if not final:
        args += made[:2]
        specs += [whole(carried)] * 2
        alias = {1 + len(args) + k: len(outs) + k for k in range(5)}
        args += made[2:]
        specs += [pl.BlockSpec(memory_space=pl.ANY)] * 5
    heights = (cols, D, 2 * cols, 2 * cols, joined)
    return call(
        functools.partial(back_kernel, heads, chunk, final),
        line,
        args,
        specs,
        (*outs, *[array(height, rows) for height in heights]),
        (*out_specs, *[lanes(height, QB, turn) for height in heights]),
        steps,
        [
            pltpu.VMEM((D, QB), BF),
            pltpu.VMEM((cols, QB), BF),
            pltpu.VMEM((cols, QB), BF),
            pltpu.VMEM((D, QB), F32),
            pltpu.VMEM((heads, TAIL + size, HD), BF),
            pltpu.VMEM((heads, TAIL + size, HD), BF),
            pltpu.VMEM((heads, HD, TAIL + size), BF),
            pltpu.VMEM((heads, HD, TAIL + size), F32),
            pltpu.VMEM((heads, HD, TAIL + size), F32),
        ],
        vmem=62,
        alias=alias,
    )


def row_order(info, value, mask):
    block = value.shape[1] // 4
    return [
        value[:, pl.ds(pl.multiple_of(spot(info[4] ^ mask ^ j) * block, 128), block)]
        for j in range(4)
    ]


def columns_kernel(info, keep, got, out):
    block = out.shape[1] // 4
    pairs = zip(row_order(info, keep, 0), row_order(info, got, 1))
    for j, (left, right) in enumerate(pairs):
        total = left.astype(F32) + right.astype(F32)
        out[:, j * block : (j + 1) * block] = total.astype(BF)


def fold_columns_far(line, keep, got, relative, size):
    cols, rows = keep.shape[0] // 2, keep.shape[1]
    low = lanes(cols, size, lambda i, s: (1, i))
    return call(
        columns_kernel if relative else add_kernel,
        line,
        (keep, got),
        [low, low],
        array(cols, rows),
        lanes(cols, size),
        rows // size,
    )


def out_kernel(info, keep, got, last, out):
    block = out.shape[1] // 4
    pairs = zip(row_order(info, keep, 0), row_order(info, got, 1))
    for j, (left, right) in enumerate(pairs):
        here = slice(j * block, (j + 1) * block)
        total = left.astype(F32) + right.astype(F32) + last[:, here].astype(F32)
        live = live_lanes(info, pl.program_id(0) * out.shape[1] + j * block, block)
        out[:, here] = jnp.where(live, total, 0.0).astype(BF)


def out_rows(line, keep, got, last, home_rows, size):
    cols, rows = last.shape
    top = lanes(cols, size)
    return call(
        out_kernel,
        line,
        (keep, got, last),
        [top, top, top],
        array(cols, home_rows),
        top,
        rows // size,
    )


def first_sums_kernel(info, keep, got, last, x, stats, gain, other, total, both, sums):
    step = pl.program_id(0)
    cols, block = total.shape

    @pl.when(step == 0)
    def _():
        sums[...] = jnp.zeros_like(sums)

    live = live_lanes(info, step * block, block)
    grad = keep[...].astype(F32) + got[...].astype(F32) + last[...].astype(F32)
    grad = jnp.where(live, grad, 0.0)
    hat = (jnp.where(live, x[...].astype(F32), 0.0) - stats[0:1, :]) * stats[1:2, :]
    scaled = grad * gain[:, 0:1]
    total[...] = grad
    one = jnp.sum(scaled, axis=0, keepdims=True)
    two = jnp.sum(scaled * hat, axis=0, keepdims=True)
    both[:, pl.ds(pl.multiple_of(step * block, 128), block)] = jnp.concatenate([one, two] * 4, axis=0)
    mine = pl.ds(pl.multiple_of(info[4] * cols, 8), cols)
    sums[mine, 0:1] += jnp.sum(grad * hat, axis=1, keepdims=True)
    sums[mine, 1:2] += jnp.sum(grad, axis=1, keepdims=True)

    @pl.when(step == pl.num_programs(0) - 1)
    def _():
        start = both.shape[1] - D
        both[:, start:] = sums[...].T[:8] + other[...]


def first_sums(line, keep, got, last, x, stats, gain, other):
    cols, rows = last.shape
    block = rows // 4
    top = lanes(cols, block)
    return call(
        first_sums_kernel,
        line,
        (keep, got, last, x, stats, gain, other),
        [top, top, top, top, lanes(16, block), whole((cols, 2)), whole((8, D))],
        (array(cols, rows, dtype=F32), array(8, rows + D, dtype=F32)),
        (top, whole((8, rows + D))),
        4,
        [pltpu.VMEM((D, 128), F32)],
    )


def x_grad_kernel(info, total, rowsums, x, stats, gain, gown, out):
    live = live_lanes(info, pl.program_id(0) * out.shape[1], out.shape[1])
    inv_row = stats[1:2, :]
    hat = (jnp.where(live, x[...].astype(F32), 0.0) - stats[0:1, :]) * inv_row
    inner = total[...] * gain[:, 0:1] - rowsums[0:1, :] * (1.0 / D)
    inner = inner - hat * (rowsums[1:2, :] * (1.0 / D))
    grad = gown[...].astype(F32) + inv_row * inner
    out[...] = jnp.where(live, grad, 0.0).astype(BF)


def x_gradient(line, total, rowsums, x, stats, gain, gown, home_rows):
    cols, rows = total.shape
    block = rows // 4
    top = lanes(cols, block)
    return call(
        x_grad_kernel,
        line,
        (total, rowsums, x, stats, gain, gown),
        [top, lanes(8, block), top, lanes(16, block), whole((cols, 2)), top],
        array(cols, home_rows),
        top,
        4,
    )


def after(value, *before):
    return lax.optimization_barrier((value, *before))[0]


def gather_parts(value, before=()):
    far = swap(value, "tensor", 2)
    near = swap(value, "tensor", 1)
    return (value, near, far, swap(after(far, *before) if before else far, "tensor", 1))


def total_over(value, axis):
    mask = 1
    while mask < lax.axis_size(axis):
        value = value + swap(value, axis, mask)
        mask *= 2
    return value


def weight_kernel(jobs, orders, info, *refs):
    count = 2 * len(jobs)
    outs, total, refs = refs[-count - 1 : -1], refs[-1], refs[: -count - 1]
    for k, groups in enumerate(jobs):
        top = 0
        for pieces in groups:
            left, right = refs[:pieces], refs[pieces : 2 * pieces]
            refs = refs[2 * pieces :]
            rows = left[0].shape[0]
            value = dot(left[0][...], right[0][...], ((1,), (1,)))
            for m in range(1, pieces):
                value = value + dot(left[m][...], right[m][...], ((1,), (1,)))
            total[top : top + rows, :] = value
            top += rows
        mine, send = outs[2 * k : 2 * k + 2]
        half = mine.shape[0]
        bit = info[8 + orders[k][0] // 2]
        mine[...] = total[pl.ds(pl.multiple_of(bit * half, 8), half), :].astype(BF)
        send[...] = total[pl.ds(pl.multiple_of((1 - bit) * half, 8), half), :].astype(BF)


WSTEP = 256


def weight_gradients(line, jobs, orders, first=0, width=D, before=()):
    args, specs, shape = [], [], []
    skip = first // WSTEP
    for pairs in jobs:
        shape.append(tuple(len(left) for left, right in pairs))
        for left, right in pairs:
            for item, k, parts in left:
                args.append(item)
                specs.append(
                    pl.BlockSpec(
                        (item.shape[0], item.shape[1] // parts),
                        lambda i, s, k=k: (0, k),
                        pipeline_mode=pl.Buffered(1),
                    )
                )
            for item, k, parts in right:
                args.append(item)
                specs.append(
                    pl.BlockSpec(
                        (WSTEP, item.shape[1] // parts), lambda i, s, k=k: (i + skip, k)
                    )
                )
    result = call(
        functools.partial(weight_kernel, tuple(shape), tuple(orders)),
        line,
        args,
        specs,
        (array(D // 2, width),) * (2 * len(jobs)),
        (lanes(D // 2, WSTEP),) * (2 * len(jobs)),
        -(-width // WSTEP),
        [pltpu.VMEM((D, WSTEP), F32)],
        vmem=62,
    )
    return [
        GroupSum(line, result[2 * k], after(result[2 * k + 1], *before), orders[k])
        for k in range(len(jobs))
    ]


def spread_kernel(info, *refs, orders, divided):
    step = pl.program_id(0)
    pieces = len(orders)
    parts, weight, outs = refs[: 4 * pieces], refs[4 * pieces], refs[4 * pieces + 1 :]
    left = 0
    for m, (first, second) in enumerate(orders):
        right = left + parts[4 * m].shape[1]
        place = ((step // 2) ^ info[8 + first // 2]) * 2 + ((step % 2) ^ info[8 + second // 2])
        for top, out in enumerate(outs):
            inside = (step >= 3 if top else step < 3) if divided else step >= 0
            for k in range(4):

                @pl.when((place == k) & inside)
                def _(out=out, part=parts[4 * m + k], left=left, right=right):
                    out[:, left:right] = part[...].astype(F32) * weight[0:1, 0:1]
        left = right


def spread_groups(line, sums, weight, divided=False):
    rows = sums[0].mine.shape[0]
    if divided:
        outs = (array(3 * rows, D, dtype=F32), array(rows, D, dtype=F32))
        specs = (
            pl.BlockSpec((rows, D), lambda i, s: (jnp.minimum(i, 2), 0)),
            pl.BlockSpec((rows, D), lambda i, s: (0, 0)),
        )
    else:
        outs = (array(4 * rows, D, dtype=F32),)
        specs = (pl.BlockSpec((rows, D), lambda i, s: (i, 0)),)
    parts = [item for one in sums for item in (one.mine, one.second, one.first, one.both)]
    return call(
        functools.partial(
            spread_kernel, orders=tuple(one.order for one in sums), divided=divided
        ),
        line,
        (*parts, weight),
        [whole(item.shape) for item in parts] + [whole((1, 1))],
        outs,
        specs,
        4,
    )


class GroupSum:
    def __init__(self, line, mine, send, order):
        self.line = line
        self.order = order
        self.mine = mine
        self.got = swap(send, "dp", order[0])

    def add(self, bit=None):
        def whole_or_half(value):
            if bit is None:
                return value.astype(F32)
            half = value.shape[0] // 2
            return lax.dynamic_slice_in_dim(value, bit * half, half).astype(F32)

        mine, got = self.line.tie(self.mine), self.got
        self.line.last = (whole_or_half(mine) + whole_or_half(got)).astype(BF)
        return self.line.last

    def quarter(self):
        bit = lax.axis_index("dp") // self.order[1] % 2
        send, self.mine = self.add(1 - bit), self.add(bit)
        self.got = swap(send, "dp", self.order[1])

    def meet(self):
        mask = 4
        self.mine = self.add()
        while mask < lax.axis_size("dp") // 2:
            self.got = swap(self.mine, "dp", mask)
            self.mine = self.add()
            mask *= 2
        self.got = swap(self.mine, "dp", mask)

    def close(self):
        self.mine = self.add()
        self.second = swap(self.mine, "dp", self.order[1])
        self.first = swap(self.mine, "dp", self.order[0])

    def relay(self, tie=False):
        second = self.line.tie(self.second) if tie else self.second
        self.both = swap(second, "dp", self.order[0])


def shards(
    x_home,
    cot_home,
    cell_len,
    norm1_gain,
    norm1_bias,
    qkv_weight,
    out_weight,
    norm2_gain,
    norm2_bias,
    up_weight,
    down_weight,
):
    groups = cell_len.shape[0]
    home_rows, cols = x_home.shape
    rows = -(-home_rows // 1024) * 1024
    me = lax.axis_index("tensor").astype(jnp.int32)
    group = lax.axis_index("dp")
    weight = groups / jnp.sum(cell_len).astype(F32)
    my_len = lax.dynamic_index_in_dim(cell_len, group, 0, keepdims=False)
    bounds = jnp.cumsum(my_len).astype(jnp.int32)
    group_bits = jnp.stack([group % 2, group // 2 % 2]).astype(jnp.int32)
    info = jnp.concatenate([bounds, jnp.broadcast_to(me, (4,)), group_bits])
    line = Line(info)

    chunks = 2
    size = rows // chunks
    block = size // 4
    x = x_home.T
    x_cuts = [x[:, :size], x[:, size:]]
    cot = cot_home.T
    cot_cuts = [cot[:, :size], cot[:, size:]]
    own_affine = jnp.stack([norm1_gain, norm1_bias, norm2_gain, norm2_bias], axis=1)
    wqkv_t = qkv_weight.transpose(1, 2, 0).reshape(3 * cols, D)
    wout_t, wup_t, wdown_t, wqkv = turned(out_weight, up_weight, down_weight, wqkv_t)
    affine_parts = gather_parts(own_affine, (wout_t, x_cuts[1], *cot_cuts))
    x_zero = gather_parts(x_cuts[0], (affine_parts[3],))
    x_next = after(x_cuts[1], affine_parts[1])
    x_next_far, x_next_near = swap(x_next, "tensor", 2), swap(x_next, "tensor", 1)
    cot_far = [swap(after(cot_cuts[0], x_zero[2]), "tensor", 2)]

    def cot_parts(c):
        value, far = cot_cuts[c], cot_far[c]
        return (value, swap(line.tie(value), "tensor", 1), far, swap(line.tie(far), "tensor", 1))

    normed, qkv, mixed, stats, keep, send, xmid, affine = front(
        line, 0, x_zero, affine_parts, wqkv_t, wout_t, rows, chunks
    )
    normed, qkv, mixed, xmid = [normed], [qkv], [mixed], [xmid]
    folds = []
    got = swap(after(send, cot_far[0], x_next_far, x_next_near), "tensor", 1)
    x_next_cross = swap(line.tie(x_next_far), "tensor", 1)
    far_sum = fold_far(line, keep, got)
    folds.append((keep, got, swap(far_sum, "tensor", 2)))
    cot_far.append(swap(after(cot_cuts[1], far_sum), "tensor", 2))
    cots = [cot_parts(0)]
    results = front(
        line,
        1,
        (x_next, x_next_near, x_next_far, x_next_cross),
        affine_parts,
        wqkv_t,
        wout_t,
        rows,
        chunks,
        (qkv[0], stats),
    )
    normed.append(results[0])
    qkv.append(results[1])
    mixed.append(results[2])
    stats, keep, send = results[3:6]
    xmid.append(results[6])
    middle, stats_two, n_parts = [], [], []

    def norm_chunk(c):
        values, n_own, stat = second_norm(line, xmid[c], *folds[c], affine)
        middle.append(values)
        stats_two.append(stat)
        n_parts.append([n_own, swap(n_own, "tensor", 1), swap(n_own, "tensor", 2), None])

    got = swap(after(send, cot_far[1], folds[0][2]), "tensor", 1)
    norm_chunk(0)
    far_sum = fold_far(line, keep, got)
    folds.append((keep, got, swap(far_sum, "tensor", 2)))
    g_rel = [cotangent(line, 0, cots[0], size)]
    cots.append(cot_parts(1))
    g_rel.append(cotangent(line, size, cots[1], size))
    norm_chunk(1)

    weights = (wup_t, down_weight, up_weight, wdown_t)

    def feed_blocks(blocks, before=()):
        picked = [n_parts[c][r] for c, r in blocks]
        made = feed(line, blocks, picked, g_rel, middle, weights, rows, before)
        return made[:5], made[5:]

    state, (pn_own, pn_near) = feed_blocks([(0, 0), (0, 1)])
    n_parts[0][3] = swap(line.tie(n_parts[0][2]), "tensor", 1)
    own_sums = [(pn_own, swap(pn_near, "tensor", 1))]
    state, (pn_far, pn_cross, pn_own, pn_near) = feed_blocks(
        [(0, 2), (0, 3), (1, 0), (1, 1)], state
    )
    n_parts[1][3] = swap(line.tie(n_parts[1][2]), "tensor", 1)
    own_sums.append((pn_own, swap(after(pn_near, n_parts[1][2]), "tensor", 1)))

    def send_far(pn_far, pn_cross, *before):
        far_sum = call(
            add_kernel,
            line,
            (pn_far, swap(after(pn_cross, *before), "tensor", 1)),
            [lanes(D, block)] * 2,
            array(D, block),
            lanes(D, block),
            1,
        )
        return swap(far_sum, "tensor", 2)

    last = [send_far(pn_far, pn_cross, n_parts[1][2])]
    state, (pn_far, pn_cross) = feed_blocks([(1, 2), (1, 3)], state)
    hidden, gpre, n_all, pd_keep, pd_send = state
    last.append(send_far(pn_far, pn_cross, last[0]))
    g_parts = []

    def back_chunk(c):
        grad_mid, sums = back_norm(
            line, *own_sums[c], last[c], middle[c], stats_two[c], g_rel[c], affine
        )
        near, far = swap(grad_mid, "tensor", 1), swap(grad_mid, "tensor", 2)
        g_parts.append([grad_mid, near, far, None])
        return sums

    sums_two = back_chunk(0)
    pairs = [[(item, c, chunks) for c in range(chunks)] for item in (hidden, gpre, n_all)]
    g_pieces = [(item, 0, 1) for item in g_rel]
    down, up = weight_gradients(
        line, [[(pairs[0], g_pieces)], [([(n_all, 0, 1)], [(gpre, 0, 1)])]], [(1, 2), (2, 1)], before=(last[1],)
    )
    sums_two = sums_two + back_chunk(1)
    pd_got = swap(pd_send, "tensor", 1)
    pd_sum = fold_columns_far(line, pd_keep, pd_got, True, size)
    g_parts[1][3] = swap(line.tie(g_parts[1][2]), "tensor", 1)
    g_parts[0][3] = swap(line.tie(g_parts[0][2]), "tensor", 1)
    down.quarter()
    up.quarter()

    made = back(line, 1, g_parts[1], qkv, stats, out_weight, wqkv)
    down.meet()
    up.meet()
    pd_last = swap(line.tie(pd_sum), "tensor", 2)
    gown, gm_all, keep, send, joined = back(
        line, 0, g_parts[0], qkv, stats, out_weight, wqkv, made
    )
    last_jobs = [
        ([(joined, c, chunks) for c in range(chunks)], [(item, 0, 1) for item in normed]),
        ([(item, 0, 1) for item in mixed], [(gm_all, c, chunks) for c in range(chunks)]),
    ]
    scale = weight.reshape(1, 1)
    (rest_one,) = weight_gradients(
        line, [last_jobs], [(1, 2)], 0, 3 * WSTEP, before=(down.got,)
    )
    down.close()
    got = swap(line.tie(send), "tensor", 1)
    (rest_two,) = weight_gradients(
        line, [last_jobs], [(2, 1)], 3 * WSTEP, D - 3 * WSTEP, before=()
    )
    far_sum = fold_columns_far(line, keep, got, False, size)
    last = swap(far_sum, "tensor", 2)
    out = out_rows(line, pd_keep, pd_got, pd_last, home_rows, size)
    rest_one.quarter()
    up.close()
    rest_two.quarter()
    total, both = first_sums(line, keep, got, last, x, stats, own_affine[:, :2], sums_two)
    rest_one.meet()
    down.relay()
    rest_two.meet()
    (grad_down,) = spread_groups(line, [down], scale)
    both = both + swap(both, "tensor", 1)
    both = both + swap(both, "tensor", 2)
    x_grad = x_gradient(line, total, both, x, stats, own_affine[:, :2], gown, home_rows)
    rest_one.close()
    rest_one.relay()
    rest_two.close()
    up.relay()
    (grad_up,) = spread_groups(line, [up], scale)
    rest_two.relay()
    small = after(both[:, rows:], rest_one.second, rest_two.second)
    mask = groups // 2
    pair = (small, swap(small, "dp", mask))
    grad_qkv, grad_out = spread_groups(line, [rest_one, rest_two], scale, True)
    while pair:
        small = line.other(lambda v: v[0] + v[1], pair)
        mask //= 2
        pair = (small, swap(small, "dp", mask)) if mask else None
    small = lax.dynamic_slice_in_dim(small, me * cols, cols, axis=1) * weight

    return (
        out.T,
        x_grad.T,
        small[0],
        small[1],
        grad_qkv.reshape(3, cols, D).transpose(2, 0, 1),
        grad_out,
        small[2],
        small[3],
        grad_up,
        grad_down,
    )


def solution(mesh):
    rows, vector = P("dp", "tensor"), P("tensor")
    qkv, wide, tall = P(None, None, "tensor"), P(None, "tensor"), P("tensor", None)
    return jax.shard_map(
        shards,
        mesh=mesh,
        in_specs=(rows, rows, P(), vector, vector, qkv, tall, vector, vector, wide, tall),
        out_specs=(rows, rows, vector, vector, qkv, tall, vector, vector, wide, tall),
        check_vma=False,
    )
```
